128 devices in a mesh: tm: 32 (over y, z, core), series: 4 (over x).
Axes of the slice: x: 4, y: 4, z: 4, core: 2. Of those that a mesh axis runs over, the one named last changes fastest.
Arguments:
- signal: float32 [64, 1048576], P('series', 'tm')
- valid_start: int32 [64], replicated, may hold values from 0 to 262143
- valid_end: int32 [64], replicated, may hold values from 786433 to 1048576
Outputs:
- smooth: float32 [64, 1048576], P('series', 'tm')
- slope: float32 [64, 1048576], P('series', 'tm')
- covariance: float32 [64, 64], P('series')
The draws below stay inside these ranges and needn't reach their ends.
Inputs may be any that keep to these rules, and one draw needn't show every extreme that they name: `valid_end`: end of the valid samples of each series.
All inputs are finite; a program needn't handle non-finite values.
Results may differ from the reference program's by a relative error of at most 0.00015.
Values sent between devices are 32-bit elements; how exact they have to be, the bound alone decides.
No kernel may reach another device: no remote copies, remote signals or barrier semaphores. Data moves between devices by JAX's collectives and lax.ppermute only.
A program may use at most 64 MiB of HBM per device.

```python
import math
import jax
import jax.numpy as jnp
from jax import lax

HALF = 16
S = 64
NT = 1048576


def draw_signal(key, part):
    keys = jax.random.split(jax.random.fold_in(key, 17), 6)
    times = jnp.arange(NT).astype(jnp.float32) / NT
    rising = 0.5 + times
    mixing = jax.random.uniform(keys[0], (S, 1), jnp.float32, -1.0, 1.0)
    phase = jax.random.uniform(keys[4], (S, 1), jnp.float32, 0.0, 2.0 * math.pi)
    freq = jax.random.uniform(keys[5], (S, 1), jnp.float32, 3.0, 9.0)
    trend = jnp.sin(2.0 * math.pi * freq * times[None, :] + phase)
    common = jax.random.normal(keys[1], (NT,), jnp.float32)
    own = jax.random.normal(keys[2], (S, NT), jnp.float32)
    noise = 0.8 * rising[None, :] * (mixing * common[None, :] + own)
    return trend + noise


def set_ends(array, key, smallest, largest):
    dims = array.shape
    place = [jax.random.randint(jax.random.fold_in(key, axis), (), 0, dims[axis]) for axis in range(len(dims))]
    array = array.at[tuple(place)].set(smallest)
    longest = dims.index(max(dims))
    place[longest] = (place[longest] + 1) % dims[longest]
    return array.at[tuple(place)].set(largest)


def setup_inputs(seed: int = 0) -> dict:
    seeds = jax.random.split(jax.random.key(seed), 4)
    return {
        "signal": draw_signal(jax.random.fold_in(seeds[3], 71), 0),
        "valid_start": set_ends(jax.random.randint(seeds[1], (S,), 0, NT // 4), jax.random.fold_in(seeds[1], 1), 0, (NT // 4) - 1).astype(jnp.int32),
        "valid_end": set_ends(jax.random.randint(seeds[2], (S,), NT - NT // 4 + 1, NT + 1), jax.random.fold_in(seeds[2], 1), NT - NT // 4 + 1, NT).astype(jnp.int32),
    }


def reference(signal, valid_start, valid_end):
    taps = 2 * HALF + 1
    offsets = jnp.arange(-HALF, HALF + 1).astype(jnp.float32)
    second = jnp.sum(offsets * offsets)
    centre_sq = second / taps
    curved = offsets * offsets - centre_sq
    fourth = jnp.sum(curved * curved)
    padded = jnp.pad(signal, ((0, 0), (HALF, HALF)))
    level = jnp.zeros_like(signal)
    tilt = jnp.zeros_like(signal)
    bend = jnp.zeros_like(signal)
    for m in range(taps):
        window = padded[:, m:m + NT]
        level = level + window * (1.0 / taps)
        tilt = tilt + window * (offsets[m] / second)
        bend = bend + window * (curved[m] / fourth)
    first = valid_start.astype(jnp.int32)[:, None]
    last = valid_end.astype(jnp.int32)[:, None]
    moment = jnp.arange(NT, dtype=jnp.int32)[None, :]
    centre = jnp.clip(moment, first + HALF, last - HALF - 1).astype(jnp.int32)
    along = (moment - centre).astype(jnp.float32)
    lv = jnp.take_along_axis(level, centre, axis=1)
    tl = jnp.take_along_axis(tilt, centre, axis=1)
    bd = jnp.take_along_axis(bend, centre, axis=1)
    inside = (moment >= first) & (moment < last)
    smooth = jnp.where(inside, lv + tl * along + bd * (along * along - centre_sq), 0.0)
    slope = jnp.where(inside, HALF * (tl + 2.0 * along * bd), 0.0)
    resid = jnp.where(inside, signal - smooth, 0.0)
    gram = lax.dot_general(resid, resid, (((1,), (1,)), ((), ())), precision=lax.Precision.HIGHEST, preferred_element_type=jnp.float32)
    correlation = (jnp.minimum(last, valid_end[None, :]) - jnp.maximum(first, valid_start[None, :])).astype(jnp.float32)
    return smooth, slope, gram / correlation
```

```python
import functools

import jax
import jax.numpy as jnp
import numpy as np
from jax import lax
from jax.experimental import pallas as pl
from jax.experimental.pallas import tpu as pltpu
from jax.sharding import Mesh
from jax.sharding import PartitionSpec as P

HALF = 16
TAPS = 2 * HALF + 1
ROWS = 16
GROUPS = 4
LANES = 128
SPAN = 2048
BLOCKS = SPAN // LANES
TIME = ("y", "z", "core")
CHUNKS = ((2, 1), (6, 2), (14, 1))

SECOND = float(sum(j * j for j in range(-HALF, HALF + 1)))
CENTRE_SQ = SECOND / TAPS
FOURTH = float(sum((j * j - CENTRE_SQ) ** 2 for j in range(-HALF, HALF + 1)))
SMOOTH_SCALE = 2048.0 / 2387.0
SLOPE_SCALE = HALF * 16.0 / SECOND


def filter_matrix():
    place = np.concatenate([np.arange(128), np.arange(128, 192), np.arange(-64, 0)])
    j = place[:, None] - np.arange(LANES)[None, :]
    near = np.abs(j) <= HALF
    smooth = np.where(near, (163 - j * j) / 2048.0, 0.0)
    slope = np.where(near, j / 16.0, 0.0)
    return np.concatenate([smooth, slope], axis=1).astype(np.float32)


def thirds(x):
    a = x.astype(jnp.bfloat16)
    rest = x - a.astype(jnp.float32)
    b = rest.astype(jnp.bfloat16)
    c = (rest - b.astype(jnp.float32)).astype(jnp.bfloat16)
    return a, b, c


def fit_kernel(base, per, total, halo, chain, where_ref, first_ref, last_ref, *refs):
    refs = list(refs)
    x_ref, left_ref, right_ref, taps_ref = refs[:4]
    refs = refs[4:]
    if halo == "use":
        halo_left_ref, halo_right_ref = refs[:2]
        refs = refs[2:]
    if halo == "make":
        front_ref, back_ref = refs[:2]
        refs = refs[2:]
    if chain:
        refs = refs[2:]
    smooth_ref, slope_ref = refs[:2]
    outs = refs[2:6]
    refs = refs[6:]
    if halo == "make":
        refs[0][...] = front_ref[...]
        refs[1][...] = back_ref[...]
        refs = refs[2:]
    resid_ref, wide_ref, stack_ref, sems = refs

    step = pl.program_id(0)
    k = step // per
    i = step % per
    mine = where_ref[0]
    unit = (base + ((mine + k) % GROUPS) * per + i) % total
    begin = where_ref[1] * (total * SPAN) + unit * SPAN
    here = resid_ref.at[k, :, pl.ds(pl.multiple_of(i * SPAN, SPAN), SPAN)]

    left = left_ref[...]
    right = right_ref[...]
    if halo == "use":
        left = jnp.where(unit == 0, halo_left_ref[...], left)
        right = jnp.where(unit == total - 1, halo_right_ref[...], right)
    wide_ref[:, :LANES] = left
    wide_ref[:, LANES + SPAN :] = right
    wide_ref[:, LANES : LANES + SPAN] = x_ref[...]

    lane = lax.broadcasted_iota(jnp.int32, (ROWS, LANES), 1)
    low = lane < 64
    height = ROWS * BLOCKS
    parts = [thirds(wide_ref[:, b * LANES : (b + 1) * LANES]) for b in range(BLOCKS + 2)]
    for n in range(3):
        for b in range(BLOCKS):
            rows = slice(n * height + b * ROWS, n * height + (b + 1) * ROWS)
            stack_ref[rows, :LANES] = parts[b + 1][n]
            stack_ref[rows, LANES:] = jnp.where(low, parts[b + 2][n], parts[b][n])
    fit = jnp.dot(stack_ref[...], taps_ref[...], preferred_element_type=jnp.float32)
    fit = fit[:height] + (fit[height : 2 * height] + fit[2 * height :])
    for b in range(BLOCKS):
        at = slice(b * LANES, (b + 1) * LANES)
        part = fit[b * ROWS : (b + 1) * ROWS]
        smooth = part[:, :LANES] * SMOOTH_SCALE
        smooth_ref[:, at] = smooth
        slope_ref[:, at] = part[:, LANES:] * SLOPE_SCALE
        here[:, at] = x_ref[:, at] - smooth

    clean = True
    holds = False
    for r in range(ROWS):
        a = first_ref[mine * ROWS + r] - begin
        z = last_ref[mine * ROWS + r] - begin
        clean = clean & (a + HALF <= 0) & (z - HALF >= SPAN)
        holds = holds | ((a > -HALF) & (a < SPAN)) | ((z > 0) & (z < SPAN + HALF))

    @pl.when(jnp.logical_not(clean))
    def _():
        row = lax.broadcasted_iota(jnp.int32, (ROWS, LANES), 0)
        first = jnp.zeros((ROWS, LANES), jnp.int32)
        last = jnp.zeros((ROWS, LANES), jnp.int32)
        for r in range(ROWS):
            first = jnp.where(row == r, first_ref[mine * ROWS + r] - begin, first)
            last = jnp.where(row == r, last_ref[mine * ROWS + r] - begin, last)
        low_centre = first + HALF
        high_centre = last - HALF - 1

        @pl.when(holds)
        def _():
            def gather(b, sums):
                x = wide_ref[:, pl.ds(pl.multiple_of(b * LANES, LANES), LANES)]
                moment = lane + (b - 1) * LANES
                new = []
                for centre, (s0, s1, s2) in zip((low_centre, high_centre), (sums[:3], sums[3:])):
                    j = moment - centre
                    w = jnp.where((j >= -HALF) & (j <= HALF), x, 0.0)
                    f = jnp.clip(j, -HALF, HALF).astype(jnp.float32)
                    new += [s0 + w, s1 + w * f, s2 + w * (f * f - CENTRE_SQ)]
                return tuple(new)

            zero = jnp.zeros((ROWS, LANES), jnp.float32)
            sums = lax.fori_loop(0, BLOCKS + 2, gather, (zero,) * 6)
            sums = [
                jnp.broadcast_to(jnp.sum(s, axis=1, keepdims=True), (ROWS, LANES)) * (1.0 / scale)
                for s, scale in zip(sums, (float(TAPS), SECOND, FOURTH) * 2)
            ]

            def mend(b, carry):
                at = pl.ds(pl.multiple_of(b * LANES, LANES), LANES)
                moment = lane + b * LANES
                smooth = smooth_ref[:, at]
                slope = slope_ref[:, at]
                for centre, (level, tilt, bend), side in (
                    (low_centre, sums[:3], -1),
                    (high_centre, sums[3:], 1),
                ):
                    j = moment - centre
                    held = (j * side >= 1) & (j * side <= HALF)
                    f = jnp.clip(j, -HALF, HALF).astype(jnp.float32)
                    smooth = jnp.where(held, level + tilt * f + bend * (f * f - CENTRE_SQ), smooth)
                    slope = jnp.where(held, HALF * (tilt + 2.0 * f * bend), slope)
                smooth_ref[:, at] = smooth
                slope_ref[:, at] = slope
                return carry

            lax.fori_loop(0, BLOCKS, mend, 0)

        def mask(b, carry):
            at = pl.ds(pl.multiple_of(b * LANES, LANES), LANES)
            moment = lane + b * LANES
            inside = (moment >= first) & (moment < last)
            smooth = jnp.where(inside, smooth_ref[:, at], 0.0)
            smooth_ref[:, at] = smooth
            slope_ref[:, at] = jnp.where(inside, slope_ref[:, at], 0.0)
            place = pl.ds(pl.multiple_of(i * SPAN + b * LANES, LANES), LANES)
            resid_ref[k, :, place] = jnp.where(inside, x_ref[:, at] - smooth, 0.0)
            return carry

        lax.fori_loop(0, BLOCKS, mask, 0)

    @pl.when(step == GROUPS * per - 1)
    def _():
        copies = [
            pltpu.make_async_copy(resid_ref.at[n], outs[n], sems.at[n]) for n in range(GROUPS)
        ]
        for copy in copies:
            copy.start()
        for copy in copies:
            copy.wait()


def fit_chunk(chunk, where, first, last, signal, taps, halo, halos, held):
    base, per = chunk
    rows, width = signal.shape
    total = width // SPAN
    blocks = width // LANES
    chain = held is not None

    def unit(p, where):
        return (base + ((where[0] + p // per) % GROUPS) * per + p % per) % total

    def whole(shape):
        return pl.BlockSpec(shape, lambda p, *s: (0,) * len(shape))

    any_spec = pl.BlockSpec(memory_space=pl.ANY)
    main = pl.BlockSpec((rows, SPAN), lambda p, w, a, z: (0, unit(p, w)))
    in_specs = [
        main,
        pl.BlockSpec((rows, LANES), lambda p, w, a, z: (0, (unit(p, w) * BLOCKS + blocks - 1) % blocks)),
        pl.BlockSpec((rows, LANES), lambda p, w, a, z: (0, (unit(p, w) * BLOCKS + BLOCKS) % blocks)),
        whole(taps.shape),
    ]
    args = [signal, signal, signal, taps]
    if halo == "use":
        in_specs += [whole((rows, LANES))] * 2
        args += list(halos)
    if halo == "make":
        in_specs += [
            pl.BlockSpec((rows, LANES), lambda p, *s: (0, 0)),
            pl.BlockSpec((rows, LANES), lambda p, *s: (0, blocks - 1)),
        ]
        args += [signal, signal]
    aliases = {}
    if chain:
        aliases = {3 + len(args): 0, 4 + len(args): 1}
        in_specs += [any_spec] * 2
        args += list(held)
    wide = jax.ShapeDtypeStruct((rows, width), jnp.float32)
    piece = jax.ShapeDtypeStruct((rows, per * SPAN), jnp.float32)
    edge = jax.ShapeDtypeStruct((rows, LANES), jnp.float32)
    out_shape = [wide, wide] + [piece] * GROUPS
    out_specs = [main, main] + [any_spec] * GROUPS
    if halo == "make":
        out_shape += [edge] * 2
        out_specs += [whole((rows, LANES))] * 2
    return pl.pallas_call(
        functools.partial(fit_kernel, base, per, total, halo, chain),
        grid_spec=pltpu.PrefetchScalarGridSpec(
            num_scalar_prefetch=3,
            grid=(GROUPS * per,),
            in_specs=in_specs,
            out_specs=out_specs,
            scratch_shapes=[
                pltpu.VMEM((GROUPS, rows, per * SPAN), jnp.float32),
                pltpu.VMEM((rows, SPAN + 2 * LANES), jnp.float32),
                pltpu.VMEM((3 * ROWS * BLOCKS, 2 * LANES), jnp.bfloat16),
                pltpu.SemaphoreType.DMA((GROUPS,)),
            ],
        ),
        out_shape=out_shape,
        input_output_aliases=aliases,
        compiler_params=pltpu.CompilerParams(dimension_semantics=("arbitrary",)),
        cost_estimate=pl.CostEstimate(
            flops=GROUPS * per * 3 * ROWS * BLOCKS * 256 * 256 * 2,
            bytes_accessed=GROUPS * per * rows * SPAN * 4 * 4,
            transcendentals=0,
        ),
        name=f"fit_{base}",
    )(where, first, last, *args)


def gram_kernel(add, where_ref, *refs):
    parts, refs = refs[:GROUPS], refs[GROUPS:]
    if add:
        so_far_ref, refs = refs[0], refs[1:]
    out_ref, stack_ref = refs
    mine = where_ref[0]
    for k in range(GROUPS):
        at = pl.multiple_of(((mine + GROUPS - k) % GROUPS) * ROWS, ROWS)
        x = parts[k][...]
        a = x.astype(jnp.bfloat16)
        b = (x - a.astype(jnp.float32)).astype(jnp.bfloat16)
        stack_ref[pl.ds(at, ROWS)] = a
        stack_ref[pl.ds(64 + at, ROWS)] = a
        stack_ref[pl.ds(128 + at, ROWS)] = b
        stack_ref[pl.ds(192 + at, ROWS)] = b
    both = lax.dot_general(
        stack_ref[64:192],
        stack_ref[...],
        (((1,), (1,)), ((), ())),
        preferred_element_type=jnp.float32,
    )
    gram = both[:64, :128] + (both[64:, :128] + both[:64, 128:] + both[64:, 128:])
    low = lax.broadcasted_iota(jnp.int32, (8, LANES), 1) < 64
    for g in range(GROUPS):
        rows = jnp.where(low, gram[16 * g : 16 * g + 8], gram[16 * g + 8 : 16 * g + 16])
        if add:
            rows = rows + so_far_ref[g]
        out_ref[g] = rows


def gram_of(where, parts, so_far):
    width = parts[0].shape[1]
    add = so_far is not None
    vmem = pl.BlockSpec(memory_space=pltpu.VMEM)
    args = list(parts) + ([so_far] if add else [])
    return pl.pallas_call(
        functools.partial(gram_kernel, add),
        in_specs=[pl.BlockSpec(memory_space=pltpu.SMEM)] + [vmem] * len(args),
        out_specs=vmem,
        out_shape=jax.ShapeDtypeStruct((GROUPS, 8, LANES), jnp.float32),
        scratch_shapes=[pltpu.VMEM((256, width), jnp.bfloat16)],
        cost_estimate=pl.CostEstimate(
            flops=128 * 256 * width * 2, bytes_accessed=64 * width * 4, transcendentals=0
        ),
        name=f"gram_{width}",
    )(where, *args)


def packed(rows):
    return jnp.concatenate([rows[:8], rows[8:]], axis=1)


def shards(taps, signal, valid_start, valid_end):
    rows, _ = signal.shape
    mine = lax.axis_index("series")
    where = jnp.stack([mine, lax.axis_index(TIME)]).astype(jnp.int32)
    steps = lax.axis_size(TIME)
    taps = jnp.asarray(taps, jnp.bfloat16)

    gram, held, halos = None, None, None
    for n, chunk in enumerate(CHUNKS):
        halo = ("no", "make", "use")[n]
        out = fit_chunk(chunk, where, valid_start, valid_end, signal, taps, halo, halos, held)
        held = out[:2]
        parts = [out[2]]
        for k in range(1, GROUPS):
            pairs = [(s, (s + k) % GROUPS) for s in range(GROUPS)]
            parts.append(lax.ppermute(out[2 + k], "series", pairs))
        if halo == "make":
            front, back = out[6:]
            halos = (
                lax.ppermute(back, TIME, [(t, t + 1) for t in range(steps - 1)]),
                lax.ppermute(front, TIME, [(t + 1, t) for t in range(steps - 1)]),
            )
        gram = gram_of(where, parts, gram)
    gram = gram + lax.ppermute(gram, "core", [(0, 1), (1, 0)])
    others = lax.axis_size(("y", "z"))
    copies = jnp.broadcast_to(gram, (others, *gram.shape)).reshape(others * GROUPS, 8, LANES)
    gram = jnp.sum(lax.all_to_all(copies, ("y", "z", "series"), 0, 0, tiled=True), axis=0)

    first = lax.dynamic_slice_in_dim(valid_start, mine * rows, rows)[:, None]
    last = lax.dynamic_slice_in_dim(valid_end, mine * rows, rows)[:, None]
    shared = jnp.minimum(last, valid_end[None, :]) - jnp.maximum(first, valid_start[None, :])
    cov = gram / packed(shared.astype(jnp.float32))
    return (*held, jnp.concatenate([cov[:, :64], cov[:, 64:]], axis=0))


def solution(mesh):
    split = Mesh(mesh.devices.reshape(4, 4, 2, GROUPS), (*TIME, "series"))
    taps = filter_matrix()
    return jax.shard_map(
        functools.partial(shards, taps),
        mesh=split,
        in_specs=(P("series", TIME), P(), P()),
        out_specs=(P("series", TIME), P("series", TIME), P("series", None)),
        check_vma=False,
    )
```

```python
import functools

import jax
import jax.numpy as jnp
import numpy as np
from jax import lax
from jax.experimental import pallas as pl
from jax.experimental.pallas import tpu as pltpu
from jax.sharding import Mesh
from jax.sharding import PartitionSpec as P


HALF = 16
TAPS = 2 * HALF + 1
ROWS = 16
GROUPS = 4
LANES = 128
SPAN = 2048
BLOCKS = SPAN // LANES
TIME = ("y", "z", "core")
MIB = 1 << 20

SECOND = float(sum(j * j for j in range(-HALF, HALF + 1)))
CENTRE_SQ = SECOND / TAPS
FOURTH = float(sum((j * j - CENTRE_SQ) ** 2 for j in range(-HALF, HALF + 1)))
SMOOTH_SCALE = 2048.0 / 2387.0
SLOPE_SCALE = HALF * 16.0 / SECOND


def filter_matrix():
    place = np.concatenate([np.arange(128), np.arange(128, 192), np.arange(-64, 0)])
    j = place[:, None] - np.arange(LANES)[None, :]
    near = np.abs(j) <= HALF
    smooth = np.where(near, (163 - j * j) / 2048.0, 0.0)
    slope = np.where(near, j / 16.0, 0.0)
    return np.concatenate([smooth, slope], axis=1).astype(np.float32)


def thirds(x):
    a = x.astype(jnp.bfloat16)
    rest = x - a.astype(jnp.float32)
    b = rest.astype(jnp.bfloat16)
    c = (rest - b.astype(jnp.float32)).astype(jnp.bfloat16)
    return a, b, c


def aligned(start, size):
    return pl.ds(pl.multiple_of(start, LANES), size)


def fit_kernel(base, count, ends, chain, *refs):
    refs = list(refs)
    first_ref, last_ref, signal_ref, taps_hbm = refs[:4]
    refs = refs[4:]
    if ends:
        halo_refs, refs = refs[:2], refs[2:]
    if chain:
        refs = refs[2:]
    smooth_hbm, slope_hbm = refs[:2]
    outs, refs = refs[2:6], refs[6:]
    if not ends:
        edge_refs, refs = refs[:2], refs[2:]
    x_ref, fit_ref, resid_ref, taps_ref, in_sems, out_sems, piece_sems, side_sems = refs

    width = signal_ref.shape[1]
    total = width // SPAN
    per = count // GROUPS
    half = count // 2
    mine = lax.axis_index("series")
    begin = lax.axis_index(TIME) * width

    def place(n):
        return LANES + n * SPAN + (2 * LANES * (n // half) if ends else 0)

    def fetch(n):
        return pltpu.make_async_copy(
            signal_ref.at[:, aligned((base + n) % total * SPAN, SPAN)],
            x_ref.at[:, aligned(place(n), SPAN)],
            in_sems.at[n],
        )

    middle = place(half)
    tail = place(count - 1) + SPAN
    sides = [
        (signal_ref.at[:, pl.ds(base * SPAN - LANES, LANES)], x_ref.at[:, pl.ds(0, LANES)]),
        (
            signal_ref.at[:, pl.ds((base + count) % total * SPAN, LANES)],
            x_ref.at[:, pl.ds(tail, LANES)],
        ),
        (taps_hbm, taps_ref),
    ]
    if ends:
        sides += [
            (halo_refs[0], x_ref.at[:, pl.ds(middle - LANES, LANES)]),
            (halo_refs[1], x_ref.at[:, pl.ds(middle - 2 * LANES, LANES)]),
        ]
    else:
        sides += [
            (signal_ref.at[:, pl.ds(0, LANES)], edge_refs[0]),
            (signal_ref.at[:, pl.ds(width - LANES, LANES)], edge_refs[1]),
        ]
    sides = [pltpu.make_async_copy(a, b, side_sems.at[n]) for n, (a, b) in enumerate(sides)]
    for copy in sides[:3]:
        copy.start()
    for n in range(count):
        fetch(n).start()
    for copy in sides[3:]:
        copy.start()

    def give(n, kind):
        return pltpu.make_async_copy(
            fit_ref.at[kind, :, aligned(n * SPAN, SPAN)],
            (smooth_hbm, slope_hbm)[kind].at[:, aligned((base + n) % total * SPAN, SPAN)],
            out_sems.at[kind, n],
        )

    def piece(k):
        return pltpu.make_async_copy(resid_ref.at[k], outs[k], piece_sems.at[k])

    lane = lax.broadcasted_iota(jnp.int32, (ROWS, LANES), 1)
    low = lane < 64
    height = ROWS * BLOCKS

    for copy in sides:
        copy.wait()
    fetch(0).wait()

    def body(n, carry):
        at = place(n)
        k = (n // per + GROUPS - mine) % GROUPS
        mark = begin + (base + n) % total * SPAN
        out_at = n * SPAN
        piece_at = n % per * SPAN

        @pl.when(n + 1 < count)
        def _():
            fetch(n + 1).wait()

        x = x_ref[:, aligned(at - LANES, SPAN + 2 * LANES)]
        parts = thirds(x)

        def cut(m, b):
            return parts[m][:, b * LANES : (b + 1) * LANES]

        rows = [
            jnp.concatenate(
                [cut(m, b + 1), jnp.where(low, cut(m, b + 2), cut(m, b))], axis=1
            )
            for m in range(3)
            for b in range(BLOCKS)
        ]
        fit = jnp.dot(
            jnp.concatenate(rows, axis=0), taps_ref[...], preferred_element_type=jnp.float32
        )
        fit = fit[:height] + (fit[height : 2 * height] + fit[2 * height :])
        for b in range(BLOCKS):
            part = fit[b * ROWS : (b + 1) * ROWS]
            smooth = part[:, :LANES] * SMOOTH_SCALE
            fit_ref[0, :, aligned(out_at + b * LANES, LANES)] = smooth
            fit_ref[1, :, aligned(out_at + b * LANES, LANES)] = part[:, LANES:] * SLOPE_SCALE
            resid_ref[k, :, aligned(piece_at + b * LANES, LANES)] = (
                x[:, (b + 1) * LANES : (b + 2) * LANES] - smooth
            )

        latest = first_ref[mine * ROWS]
        soonest = last_ref[mine * ROWS]
        holds = False
        for r in range(ROWS):
            a = first_ref[mine * ROWS + r]
            z = last_ref[mine * ROWS + r]
            latest = jnp.maximum(latest, a)
            soonest = jnp.minimum(soonest, z)
            holds = (
                holds
                | ((a > mark - HALF) & (a < mark + SPAN))
                | ((z > mark) & (z < mark + SPAN + HALF))
            )

        @pl.when((latest + HALF > mark) | (soonest - HALF < mark + SPAN))
        def _():
            row = lax.broadcasted_iota(jnp.int32, (ROWS, LANES), 0)
            first = jnp.zeros((ROWS, LANES), jnp.int32)
            last = jnp.zeros((ROWS, LANES), jnp.int32)
            for r in range(ROWS):
                first = jnp.where(row == r, first_ref[mine * ROWS + r] - mark, first)
                last = jnp.where(row == r, last_ref[mine * ROWS + r] - mark, last)
            low_centre = first + HALF
            high_centre = last - HALF - 1

            @pl.when(holds)
            def _():
                def gather(b, sums):
                    v = x_ref[:, aligned(at + (b - 1) * LANES, LANES)]
                    moment = lane + (b - 1) * LANES
                    new = []
                    for centre, (s0, s1, s2) in zip(
                        (low_centre, high_centre), (sums[:3], sums[3:])
                    ):
                        j = moment - centre
                        w = jnp.where((j >= -HALF) & (j <= HALF), v, 0.0)
                        f = jnp.clip(j, -HALF, HALF).astype(jnp.float32)
                        new += [s0 + w, s1 + w * f, s2 + w * (f * f - CENTRE_SQ)]
                    return tuple(new)

                zero = jnp.zeros((ROWS, LANES), jnp.float32)
                sums = lax.fori_loop(0, BLOCKS + 2, gather, (zero,) * 6)
                sums = [
                    jnp.broadcast_to(jnp.sum(s, axis=1, keepdims=True), (ROWS, LANES))
                    * (1.0 / scale)
                    for s, scale in zip(sums, (float(TAPS), SECOND, FOURTH) * 2)
                ]

                def mend(b, carry):
                    to = aligned(out_at + b * LANES, LANES)
                    moment = lane + b * LANES
                    smooth = fit_ref[0, :, to]
                    slope = fit_ref[1, :, to]
                    for centre, (level, tilt, bend), side in (
                        (low_centre, sums[:3], -1),
                        (high_centre, sums[3:], 1),
                    ):
                        j = moment - centre
                        held = (j * side >= 1) & (j * side <= HALF)
                        f = jnp.clip(j, -HALF, HALF).astype(jnp.float32)
                        bent = level + tilt * f + bend * (f * f - CENTRE_SQ)
                        smooth = jnp.where(held, bent, smooth)
                        slope = jnp.where(held, HALF * (tilt + 2.0 * f * bend), slope)
                    fit_ref[0, :, to] = smooth
                    fit_ref[1, :, to] = slope
                    return carry

                lax.fori_loop(0, BLOCKS, mend, 0)

            def mask(b, carry):
                to = aligned(out_at + b * LANES, LANES)
                moment = lane + b * LANES
                inside = (moment >= first) & (moment < last)
                smooth = jnp.where(inside, fit_ref[0, :, to], 0.0)
                fit_ref[0, :, to] = smooth
                fit_ref[1, :, to] = jnp.where(inside, fit_ref[1, :, to], 0.0)
                resid_ref[k, :, aligned(piece_at + b * LANES, LANES)] = jnp.where(
                    inside, x_ref[:, aligned(at + b * LANES, LANES)] - smooth, 0.0
                )
                return carry

            lax.fori_loop(0, BLOCKS, mask, 0)

        give(n, 0).start()
        give(n, 1).start()
        for kk in range(GROUPS):

            @pl.when((k == kk) & (n % per == per - 1))
            def _():
                piece(kk).start()

        return carry

    lax.fori_loop(0, count, body, 0)
    for kk in range(GROUPS):
        piece(kk).wait()

    def drain(n, carry):
        give(n, 0).wait()
        give(n, 1).wait()
        return carry

    lax.fori_loop(0, count, drain, 0)


def fit_steps(base, count, first, last, signal, taps, halos, held):
    rows, width = signal.shape
    ends = halos is not None
    chain = held is not None
    smem = pl.BlockSpec(memory_space=pltpu.SMEM)
    loose = pl.BlockSpec(memory_space=pl.ANY)
    args = [first, last, signal, taps] + list(halos or ()) + list(held or ())
    aliases = {len(args) - 2: 0, len(args) - 1: 1} if chain else {}
    wide = jax.ShapeDtypeStruct((rows, width), jnp.float32)
    part = jax.ShapeDtypeStruct((rows, count // GROUPS * SPAN), jnp.float32)
    edge = jax.ShapeDtypeStruct((rows, LANES), jnp.float32)
    out_shape = [wide, wide] + [part] * GROUPS + ([] if ends else [edge] * 2)
    return pl.pallas_call(
        functools.partial(fit_kernel, base, count, ends, chain),
        in_specs=[smem, smem] + [loose] * (len(args) - 2),
        out_specs=[loose] * 6 + ([] if ends else [pl.BlockSpec(memory_space=pltpu.VMEM)] * 2),
        out_shape=out_shape,
        scratch_shapes=[
            pltpu.VMEM((rows, count * SPAN + (4 if ends else 2) * LANES), jnp.float32),
            pltpu.VMEM((2, rows, count * SPAN), jnp.float32),
            pltpu.VMEM((GROUPS, rows, count // GROUPS * SPAN), jnp.float32),
            pltpu.VMEM(taps.shape, taps.dtype),
            pltpu.SemaphoreType.DMA((count,)),
            pltpu.SemaphoreType.DMA((2, count)),
            pltpu.SemaphoreType.DMA((GROUPS,)),
            pltpu.SemaphoreType.DMA((5,)),
        ],
        input_output_aliases=aliases,
        compiler_params=pltpu.CompilerParams(vmem_limit_bytes=12 * MIB),
        cost_estimate=pl.CostEstimate(
            flops=count * 3 * rows * BLOCKS * 256 * 256 * 2,
            bytes_accessed=count * rows * SPAN * 4 * 4,
            transcendentals=0,
        ),
    )(*args)


def gram_kernel(spread, *refs):
    parts, refs = refs[:GROUPS], refs[GROUPS:]
    if spread:
        so_far_ref, refs = refs[0], refs[1:]
    out_ref, stack_ref = refs
    mine = lax.axis_index("series")
    for k in range(GROUPS):
        at = pl.multiple_of((mine + GROUPS - k) % GROUPS * ROWS, ROWS)
        x = parts[k][...]
        a = x.astype(jnp.bfloat16)
        b = (x - a.astype(jnp.float32)).astype(jnp.bfloat16)
        stack_ref[pl.ds(at, ROWS)] = a
        stack_ref[pl.ds(64 + at, ROWS)] = a
        stack_ref[pl.ds(128 + at, ROWS)] = b
        stack_ref[pl.ds(192 + at, ROWS)] = b
    both = lax.dot_general(
        stack_ref[64:192],
        stack_ref[...],
        (((1,), (1,)), ((), ())),
        preferred_element_type=jnp.float32,
    )
    gram = both[:64, :128] + (both[64:, :128] + both[:64, 128:] + both[64:, 128:])
    low = lax.broadcasted_iota(jnp.int32, (8, LANES), 1) < 64
    for g in range(GROUPS):
        rows = jnp.where(low, gram[16 * g : 16 * g + 8], gram[16 * g + 8 : 16 * g + 16])
        if spread:
            rows = rows + so_far_ref[g]
            for n in range(spread):
                out_ref[n, g] = rows
        else:
            out_ref[g] = rows


def gram_of(parts, so_far, spread):
    width = parts[0].shape[1]
    vmem = pl.BlockSpec(memory_space=pltpu.VMEM)
    args = list(parts) + ([so_far] if spread else [])
    lead = (spread,) if spread else ()
    return pl.pallas_call(
        functools.partial(gram_kernel, spread),
        in_specs=[vmem] * len(args),
        out_specs=vmem,
        out_shape=jax.ShapeDtypeStruct((*lead, GROUPS, 8, LANES), jnp.float32),
        scratch_shapes=[pltpu.VMEM((256, width), jnp.bfloat16)],
        compiler_params=pltpu.CompilerParams(vmem_limit_bytes=12 * MIB),
        cost_estimate=pl.CostEstimate(
            flops=128 * 256 * width * 2, bytes_accessed=64 * width * 4, transcendentals=0
        ),
        name="gram_last" if spread else "gram_first",
    )(*args)


def packed(rows):
    return jnp.concatenate([rows[:8], rows[8:]], axis=1)


def exchanged(pieces):
    parts = [pieces[0]]
    for k in (2, 1, 3):
        pairs = [(s, (s + k) % GROUPS) for s in range(GROUPS)]
        parts.append(lax.ppermute(pieces[k], "series", pairs))
    return [parts[0], parts[2], parts[1], parts[3]]


def shards(taps, signal, valid_start, valid_end):
    rows, width = signal.shape
    steps = width // SPAN
    devices = lax.axis_size(TIME)
    taps = jnp.asarray(taps, jnp.bfloat16)
    mine = lax.axis_index("series")

    first = lax.dynamic_slice_in_dim(valid_start, mine * rows, rows)[:, None]
    last = lax.dynamic_slice_in_dim(valid_end, mine * rows, rows)[:, None]
    shared = jnp.minimum(last, valid_end[None, :]) - jnp.maximum(first, valid_start[None, :])
    shared = packed(shared.astype(jnp.float32))

    quarter = steps // 4
    out = fit_steps(quarter, steps // 2, valid_start, valid_end, signal, taps, None, None)
    held, front, back = out[:2], out[6], out[7]
    parts = exchanged(out[2:6])
    left = lax.ppermute(back, TIME, [(t, t + 1) for t in range(devices - 1)])
    right = lax.ppermute(front, TIME, [(t + 1, t) for t in range(devices - 1)])
    out = fit_steps(
        3 * quarter, steps // 2, valid_start, valid_end, signal, taps, (left, right), held
    )
    held = out[:2]
    gram = gram_of(parts, None, 0)
    parts = exchanged(out[2:6])
    copies = gram_of(parts, gram, devices).reshape(devices * GROUPS, 8, LANES)
    copies = lax.all_to_all(copies, (*TIME, "series"), 0, 0, tiled=True)
    cov = jnp.sum(copies, axis=0) / shared
    return (*held, jnp.concatenate([cov[:, :64], cov[:, 64:]], axis=0))


def solution(mesh):
    split = Mesh(mesh.devices.reshape(4, 4, 2, GROUPS), (*TIME, "series"))
    return jax.shard_map(
        functools.partial(shards, filter_matrix()),
        mesh=split,
        in_specs=(P("series", TIME), P(), P()),
        out_specs=(P("series", TIME), P("series", TIME), P("series", None)),
        check_vma=False,
    )
```

```python
import functools

import jax
import jax.numpy as jnp
import numpy as np
from jax import lax
from jax.experimental import pallas as pl
from jax.experimental.pallas import tpu as pltpu
from jax.sharding import Mesh
from jax.sharding import PartitionSpec as P


HALF = 16
TAPS = 2 * HALF + 1
ROWS = 16
GROUPS = 4
LANES = 128
SPAN = 2048
BLOCKS = SPAN // LANES
TIME = ("y", "z", "core")
MIB = 1 << 20

SECOND = float(sum(j * j for j in range(-HALF, HALF + 1)))
CENTRE_SQ = SECOND / TAPS
FOURTH = float(sum((j * j - CENTRE_SQ) ** 2 for j in range(-HALF, HALF + 1)))
SMOOTH_SCALE = 2048.0 / 2387.0
SLOPE_SCALE = HALF * 16.0 / SECOND


def filter_matrix():
    place = np.concatenate([np.arange(128), np.arange(128, 192), np.arange(-64, 0)])
    j = place[:, None] - np.arange(LANES)[None, :]
    near = np.abs(j) <= HALF
    smooth = np.where(near, (163 - j * j) / 2048.0, 0.0)
    slope = np.where(near, j / 16.0, 0.0)
    return np.concatenate([smooth, slope], axis=1).astype(np.float32)


def thirds(x):
    a = x.astype(jnp.bfloat16)
    rest = x - a.astype(jnp.float32)
    b = rest.astype(jnp.bfloat16)
    c = (rest - b.astype(jnp.float32)).astype(jnp.bfloat16)
    return a, b, c


def aligned(start, size):
    return pl.ds(pl.multiple_of(start, LANES), size)


def fit_kernel(base, count, ends, chain, *refs):
    refs = list(refs)
    first_hbm, last_hbm, signal_ref, taps_hbm = refs[:4]
    refs = refs[4:]
    if ends:
        halo_refs, refs = refs[:2], refs[2:]
    if chain:
        refs = refs[2:]
    smooth_hbm, slope_hbm = refs[:2]
    outs, refs = refs[2:6], refs[6:]
    if not ends:
        edge_refs, refs = refs[:2], refs[2:]
    x_ref, fit_ref, resid_ref, taps_ref, first_ref, last_ref = refs[:6]
    in_sems, out_sems, piece_sems, side_sems = refs[6:]

    width = signal_ref.shape[1]
    total = width // SPAN
    per = count // GROUPS
    half = count // 2
    mine = lax.axis_index("series")
    begin = lax.axis_index(TIME) * width

    def place(n):
        return LANES + n * SPAN + (2 * LANES * (n // half) if ends else 0)

    def fetch(n):
        return pltpu.make_async_copy(
            signal_ref.at[:, aligned((base + n) % total * SPAN, SPAN)],
            x_ref.at[:, aligned(place(n), SPAN)],
            in_sems.at[n],
        )

    middle = place(half)
    tail = place(count - 1) + SPAN
    sides = [
        (signal_ref.at[:, pl.ds(base * SPAN - LANES, LANES)], x_ref.at[:, pl.ds(0, LANES)]),
        (
            signal_ref.at[:, pl.ds((base + count) % total * SPAN, LANES)],
            x_ref.at[:, pl.ds(tail, LANES)],
        ),
        (first_hbm, first_ref),
        (last_hbm, last_ref),
        (taps_hbm, taps_ref),
    ]
    if ends:
        sides += [
            (halo_refs[0], x_ref.at[:, pl.ds(middle - LANES, LANES)]),
            (halo_refs[1], x_ref.at[:, pl.ds(middle - 2 * LANES, LANES)]),
        ]
    else:
        sides += [
            (signal_ref.at[:, pl.ds(0, LANES)], edge_refs[0]),
            (signal_ref.at[:, pl.ds(width - LANES, LANES)], edge_refs[1]),
        ]
    sides = [pltpu.make_async_copy(a, b, side_sems.at[n]) for n, (a, b) in enumerate(sides)]
    for copy in sides[:5]:
        copy.start()
    for n in range(count):
        fetch(n).start()
    for copy in sides[5:]:
        copy.start()

    def give(n, kind):
        return pltpu.make_async_copy(
            fit_ref.at[kind, :, aligned(n * SPAN, SPAN)],
            (smooth_hbm, slope_hbm)[kind].at[:, aligned((base + n) % total * SPAN, SPAN)],
            out_sems.at[kind, n],
        )

    def piece(k):
        return pltpu.make_async_copy(resid_ref.at[k], outs[k], piece_sems.at[k])

    lane = lax.broadcasted_iota(jnp.int32, (ROWS, LANES), 1)
    low = lane < 64
    height = ROWS * BLOCKS

    for copy in sides:
        copy.wait()
    fetch(0).wait()

    row = lax.broadcasted_iota(jnp.int32, (ROWS, LANES), 0)
    first = jnp.zeros((ROWS, LANES), jnp.int32)
    last = jnp.zeros((ROWS, LANES), jnp.int32)
    for r in range(ROWS):
        first = jnp.where(row == r, first_ref[mine * ROWS + r], first)
        last = jnp.where(row == r, last_ref[mine * ROWS + r], last)

    def body(n, carry):
        at = place(n)
        k = (n // per + GROUPS - mine) % GROUPS
        mark = begin + (base + n) % total * SPAN
        out_at = n * SPAN
        piece_at = n % per * SPAN

        @pl.when(n + 1 < count)
        def _():
            fetch(n + 1).wait()

        x = x_ref[:, aligned(at - LANES, SPAN + 2 * LANES)]
        parts = thirds(x)

        def cut(m, b):
            return parts[m][:, b * LANES : (b + 1) * LANES]

        rows = [
            jnp.concatenate(
                [cut(m, b + 1), jnp.where(low, cut(m, b + 2), cut(m, b))], axis=1
            )
            for m in range(3)
            for b in range(BLOCKS)
        ]
        fit = jnp.dot(
            jnp.concatenate(rows, axis=0), taps_ref[...], preferred_element_type=jnp.float32
        )
        fit = fit[:height] + (fit[height : 2 * height] + fit[2 * height :])
        since = first - mark
        until = last - mark
        for b in range(BLOCKS):
            part = fit[b * ROWS : (b + 1) * ROWS]
            moment = lane + b * LANES
            inside = (moment >= since) & (moment < until)
            smooth = part[:, :LANES] * SMOOTH_SCALE
            resid = x[:, (b + 1) * LANES : (b + 2) * LANES] - smooth
            to = aligned(out_at + b * LANES, LANES)
            fit_ref[0, :, to] = jnp.where(inside, smooth, 0.0)
            fit_ref[1, :, to] = jnp.where(inside, part[:, LANES:] * SLOPE_SCALE, 0.0)
            resid_ref[k, :, aligned(piece_at + b * LANES, LANES)] = jnp.where(inside, resid, 0.0)

        def starts_here(a):
            return (a > mark - HALF) & (a < mark + SPAN)

        def stops_here(z):
            return (z > mark) & (z < mark + SPAN + HALF)

        holds = False
        for r in range(ROWS):
            holds = holds | starts_here(first_ref[mine * ROWS + r])
            holds = holds | stops_here(last_ref[mine * ROWS + r])

        @pl.when(holds)
        def _():
            def mend(r, left, centre, side):
                b = (left + LANES) // LANES - 1
                v = x_ref[:, aligned(at + b * LANES, 2 * LANES)]
                j = lax.broadcasted_iota(jnp.int32, (ROWS, 2 * LANES), 1) + (b * LANES - centre)
                w = jnp.where((j >= -HALF) & (j <= HALF), v, 0.0)
                f = jnp.clip(j, -HALF, HALF).astype(jnp.float32)
                level = jnp.sum(w, axis=1, keepdims=True) * (1.0 / TAPS)
                tilt = jnp.sum(w * f, axis=1, keepdims=True) * (1.0 / SECOND)
                curve = f * f - CENTRE_SQ
                bend = jnp.sum(w * curve, axis=1, keepdims=True) * (1.0 / FOURTH)
                smooth = level + tilt * f + bend * curve
                slope = HALF * (tilt + 2.0 * f * bend)
                held = (j * side >= 1) & (j * side <= HALF)
                for h in range(2):

                    @pl.when((b + h >= 0) & (b + h < BLOCKS))
                    def _():
                        part = slice(h * LANES, (h + 1) * LANES)
                        mine_held = held[:, part] & (row == r)
                        to = aligned(out_at + (b + h) * LANES, LANES)
                        fit_ref[0, :, to] = jnp.where(mine_held, smooth[:, part], fit_ref[0, :, to])
                        fit_ref[1, :, to] = jnp.where(mine_held, slope[:, part], fit_ref[1, :, to])
                        to = aligned(piece_at + (b + h) * LANES, LANES)
                        resid_ref[k, :, to] = jnp.where(
                            mine_held, v[:, part] - smooth[:, part], resid_ref[k, :, to]
                        )

            def series(r, carry):
                a = first_ref[mine * ROWS + r]
                z = last_ref[mine * ROWS + r]

                @pl.when(starts_here(a))
                def _():
                    mend(r, a - mark, a - mark + HALF, -1)

                @pl.when(stops_here(z))
                def _():
                    mend(r, z - mark - TAPS, z - mark - HALF - 1, 1)

                return carry

            lax.fori_loop(0, ROWS, series, 0)

        give(n, 0).start()
        give(n, 1).start()
        for kk in range(GROUPS):

            @pl.when((k == kk) & (n % per == per - 1))
            def _():
                piece(kk).start()

        return carry

    lax.fori_loop(0, count, body, 0)
    for kk in range(GROUPS):
        piece(kk).wait()

    def drain(n, carry):
        give(n, 0).wait()
        give(n, 1).wait()
        return carry

    lax.fori_loop(0, count, drain, 0)


def fit_steps(base, count, first, last, signal, taps, halos, held):
    rows, width = signal.shape
    ends = halos is not None
    chain = held is not None
    hbm = pl.BlockSpec(memory_space=pltpu.HBM)
    loose = pl.BlockSpec(memory_space=pl.ANY)
    args = [pltpu.with_memory_space_constraint(a, pltpu.HBM) for a in (first, last, signal, taps)]
    args += list(halos or ()) + list(held or ())
    aliases = {len(args) - 2: 0, len(args) - 1: 1} if chain else {}
    wide = jax.ShapeDtypeStruct((rows, width), jnp.float32)
    part = jax.ShapeDtypeStruct((rows, count // GROUPS * SPAN), jnp.float32)
    edge = jax.ShapeDtypeStruct((rows, LANES), jnp.float32)
    out_shape = [wide, wide] + [part] * GROUPS + ([] if ends else [edge] * 2)
    return pl.pallas_call(
        functools.partial(fit_kernel, base, count, ends, chain),
        in_specs=[hbm] * 4 + [loose] * len(halos or ()) + [hbm] * len(held or ()),
        out_specs=[hbm] * 2 + [loose] * GROUPS + [loose] * (0 if ends else 2),
        out_shape=out_shape,
        scratch_shapes=[
            pltpu.VMEM((rows, count * SPAN + (4 if ends else 2) * LANES), jnp.float32),
            pltpu.VMEM((2, rows, count * SPAN), jnp.float32),
            pltpu.VMEM((GROUPS, rows, count // GROUPS * SPAN), jnp.float32),
            pltpu.VMEM(taps.shape, taps.dtype),
            pltpu.SMEM(first.shape, jnp.int32),
            pltpu.SMEM(last.shape, jnp.int32),
            pltpu.SemaphoreType.DMA((count,)),
            pltpu.SemaphoreType.DMA((2, count)),
            pltpu.SemaphoreType.DMA((GROUPS,)),
            pltpu.SemaphoreType.DMA((7,)),
        ],
        input_output_aliases=aliases,
        compiler_params=pltpu.CompilerParams(vmem_limit_bytes=12 * MIB),
        cost_estimate=pl.CostEstimate(
            flops=count * 3 * rows * BLOCKS * 256 * 256 * 2,
            bytes_accessed=count * rows * SPAN * 4 * 4,
            transcendentals=0,
        ),
    )(*args)


def gram_kernel(spread, *refs):
    parts, refs = refs[:GROUPS], refs[GROUPS:]
    if spread:
        so_far_ref, refs = refs[0], refs[1:]
    out_ref, stack_ref = refs
    mine = lax.axis_index("series")
    for k in range(GROUPS):
        at = pl.multiple_of((mine + GROUPS - k) % GROUPS * ROWS, ROWS)
        x = parts[k][...]
        a = x.astype(jnp.bfloat16)
        b = (x - a.astype(jnp.float32)).astype(jnp.bfloat16)
        stack_ref[pl.ds(at, ROWS)] = a
        stack_ref[pl.ds(64 + at, ROWS)] = a
        stack_ref[pl.ds(128 + at, ROWS)] = b
        stack_ref[pl.ds(192 + at, ROWS)] = b
    both = lax.dot_general(
        stack_ref[64:192],
        stack_ref[...],
        (((1,), (1,)), ((), ())),
        preferred_element_type=jnp.float32,
    )
    gram = both[:64, :128] + (both[64:, :128] + both[:64, 128:] + both[64:, 128:])
    low = lax.broadcasted_iota(jnp.int32, (8, LANES), 1) < 64
    for g in range(GROUPS):
        rows = jnp.where(low, gram[16 * g : 16 * g + 8], gram[16 * g + 8 : 16 * g + 16])
        if spread:
            rows = rows + so_far_ref[g]
            for n in range(spread):
                out_ref[n, g] = rows
        else:
            out_ref[g] = rows


def gram_of(parts, so_far, spread):
    width = parts[0].shape[1]
    vmem = pl.BlockSpec(memory_space=pltpu.VMEM)
    args = list(parts) + ([so_far] if spread else [])
    lead = (spread,) if spread else ()
    return pl.pallas_call(
        functools.partial(gram_kernel, spread),
        in_specs=[vmem] * len(args),
        out_specs=vmem,
        out_shape=jax.ShapeDtypeStruct((*lead, GROUPS, 8, LANES), jnp.float32),
        scratch_shapes=[pltpu.VMEM((256, width), jnp.bfloat16)],
        compiler_params=pltpu.CompilerParams(vmem_limit_bytes=12 * MIB),
        cost_estimate=pl.CostEstimate(
            flops=128 * 256 * width * 2, bytes_accessed=64 * width * 4, transcendentals=0
        ),
        name="gram_last" if spread else "gram_first",
    )(*args)


def packed(rows):
    return jnp.concatenate([rows[:8], rows[8:]], axis=1)


def exchanged(pieces):
    parts = [pieces[0]]
    for k in (2, 1, 3):
        pairs = [(s, (s + k) % GROUPS) for s in range(GROUPS)]
        parts.append(lax.ppermute(pieces[k], "series", pairs))
    return [parts[0], parts[2], parts[1], parts[3]]


def shards(taps, signal, valid_start, valid_end):
    rows, width = signal.shape
    steps = width // SPAN
    devices = lax.axis_size(TIME)
    taps = jnp.asarray(taps, jnp.bfloat16)
    mine = lax.axis_index("series")

    first = lax.dynamic_slice_in_dim(valid_start, mine * rows, rows)[:, None]
    last = lax.dynamic_slice_in_dim(valid_end, mine * rows, rows)[:, None]
    shared = jnp.minimum(last, valid_end[None, :]) - jnp.maximum(first, valid_start[None, :])
    shared = packed(shared.astype(jnp.float32))

    quarter = steps // 4
    out = fit_steps(quarter, steps // 2, valid_start, valid_end, signal, taps, None, None)
    held, front, back = out[:2], out[6], out[7]
    parts = exchanged(out[2:6])
    left = lax.ppermute(back, TIME, [(t, t + 1) for t in range(devices - 1)])
    right = lax.ppermute(front, TIME, [(t + 1, t) for t in range(devices - 1)])
    out = fit_steps(
        3 * quarter, steps // 2, valid_start, valid_end, signal, taps, (left, right), held
    )
    held = out[:2]
    gram = gram_of(parts, None, 0)
    parts = exchanged(out[2:6])
    copies = gram_of(parts, gram, devices).reshape(devices * GROUPS, 8, LANES)
    copies = lax.all_to_all(copies, (*TIME, "series"), 0, 0, tiled=True)
    cov = jnp.sum(copies, axis=0) / shared
    return (*held, jnp.concatenate([cov[:, :64], cov[:, 64:]], axis=0))


def solution(mesh):
    split = Mesh(mesh.devices.reshape(4, 4, 2, GROUPS), (*TIME, "series"))
    return jax.shard_map(
        functools.partial(shards, filter_matrix()),
        mesh=split,
        in_specs=(P("series", TIME), P(), P()),
        out_specs=(P("series", TIME), P("series", TIME), P("series", None)),
        check_vma=False,
    )
```

```python
import functools

import jax
import jax.numpy as jnp
import numpy as np
from jax import lax
from jax.experimental import pallas as pl
from jax.experimental.pallas import tpu as pltpu
from jax.sharding import Mesh
from jax.sharding import PartitionSpec as P


HALF = 16
TAPS = 2 * HALF + 1
ROWS = 16
GROUPS = 4
LANES = 128
TIME = ("y", "z", "core")
MIB = 1 << 20

SECOND = float(sum(j * j for j in range(-HALF, HALF + 1)))
CENTRE_SQ = SECOND / TAPS
FOURTH = float(sum((j * j - CENTRE_SQ) ** 2 for j in range(-HALF, HALF + 1)))
SMOOTH_SCALE = 2048.0 / 2387.0
SLOPE_SCALE = HALF * 16.0 / SECOND


def filter_matrix():
    place = np.concatenate([np.arange(128), np.arange(128, 192), np.arange(-64, 0)])
    j = place[:, None] - np.arange(LANES)[None, :]
    near = np.abs(j) <= HALF
    smooth = np.where(near, (163 - j * j) / 2048.0, 0.0)
    slope = np.where(near, j / 16.0, 0.0)
    return np.concatenate([smooth, slope], axis=1).astype(np.float32)


def thirds(x):
    a = x.astype(jnp.bfloat16)
    rest = x - a.astype(jnp.float32)
    b = rest.astype(jnp.bfloat16)
    c = (rest - b.astype(jnp.float32)).astype(jnp.bfloat16)
    return a, b, c


def aligned(start, size):
    return pl.ds(pl.multiple_of(start, LANES), size)


def fit_kernel(plan, fits, resids, ends, edges, chain, *refs):
    base, span, count = plan
    blocks = span // LANES
    refs = list(refs)
    first_hbm, last_hbm, signal_ref, taps_hbm = refs[:4]
    refs = refs[4:]
    if ends:
        halo_refs, refs = refs[:2], refs[2:]
    if chain:
        refs = refs[2:]
    if fits:
        fit_hbm, refs = refs[:2], refs[2:]
    if resids:
        outs, refs = refs[:GROUPS], refs[GROUPS:]
    if edges:
        edge_refs, refs = refs[:2], refs[2:]
    x_ref, taps_ref, first_ref, last_ref, in_sems, side_sems = refs[:6]
    refs = refs[6:]
    if fits:
        fit_ref, out_sems = refs[:2]
        refs = refs[2:]
    if resids:
        resid_ref, piece_sems = refs

    width = signal_ref.shape[1]
    per = count // GROUPS
    half = count // 2
    mine = lax.axis_index("series")
    begin = lax.axis_index(TIME) * width

    def place(n):
        return LANES + n * span + (2 * LANES * (n // half) if ends else 0)

    def source(n):
        return lax.rem(base + n * span, width) if ends else base + n * span

    def fetch(n):
        return pltpu.make_async_copy(
            signal_ref.at[:, aligned(source(n), span)],
            x_ref.at[:, aligned(place(n), span)],
            in_sems.at[n],
        )

    middle = place(half)
    tail = place(count - 1) + span
    after = (base + count * span) % width
    sides = [
        (signal_ref.at[:, pl.ds(base - LANES, LANES)], x_ref.at[:, pl.ds(0, LANES)]),
        (signal_ref.at[:, pl.ds(after, LANES)], x_ref.at[:, pl.ds(tail, LANES)]),
        (first_hbm, first_ref),
        (last_hbm, last_ref),
        (taps_hbm, taps_ref),
    ]
    if ends:
        sides += [
            (halo_refs[0], x_ref.at[:, pl.ds(middle - LANES, LANES)]),
            (halo_refs[1], x_ref.at[:, pl.ds(middle - 2 * LANES, LANES)]),
        ]
    if edges:
        sides += [
            (signal_ref.at[:, pl.ds(0, LANES)], edge_refs[0]),
            (signal_ref.at[:, pl.ds(width - LANES, LANES)], edge_refs[1]),
        ]
    sides = [pltpu.make_async_copy(a, b, side_sems.at[n]) for n, (a, b) in enumerate(sides)]
    for copy in sides[:5]:
        copy.start()
    for n in range(count):
        fetch(n).start()
    for copy in sides[5:]:
        copy.start()

    def give(n, kind):
        return pltpu.make_async_copy(
            fit_ref.at[kind, :, aligned(n * span, span)],
            fit_hbm[kind].at[:, aligned(source(n), span)],
            out_sems.at[kind, n],
        )

    def piece(k):
        return pltpu.make_async_copy(resid_ref.at[k], outs[k], piece_sems.at[k])

    lane = lax.broadcasted_iota(jnp.int32, (ROWS, LANES), 1)
    low = lane < 64
    height = ROWS * blocks
    late = len(sides) - (2 if edges else 0)

    for copy in sides[:late]:
        copy.wait()
    fetch(0).wait()

    row = lax.broadcasted_iota(jnp.int32, (ROWS, LANES), 0)
    first = jnp.zeros((ROWS, LANES), jnp.int32)
    last = jnp.zeros((ROWS, LANES), jnp.int32)
    for r in range(ROWS):
        first = jnp.where(row == r, first_ref[mine * ROWS + r], first)
        last = jnp.where(row == r, last_ref[mine * ROWS + r], last)

    def body(n, carry):
        at = place(n)
        k = (n // per + GROUPS - mine) % GROUPS
        mark = begin + source(n)
        out_at = n * span
        piece_at = n % per * span

        @pl.when(n + 1 < count)
        def _():
            fetch(n + 1).wait()

        x = x_ref[:, aligned(at - LANES, span + 2 * LANES)]
        parts = thirds(x)

        def cut(m, b):
            return parts[m][:, b * LANES : (b + 1) * LANES]

        rows = [
            jnp.concatenate(
                [cut(m, b + 1), jnp.where(low, cut(m, b + 2), cut(m, b))], axis=1
            )
            for m in range(3)
            for b in range(blocks)
        ]
        fit = jnp.dot(
            jnp.concatenate(rows, axis=0), taps_ref[...], preferred_element_type=jnp.float32
        )
        fit = fit[:height] + (fit[height : 2 * height] + fit[2 * height :])
        since = first - mark
        until = last - mark
        for b in range(blocks):
            part = fit[b * ROWS : (b + 1) * ROWS]
            moment = lane + b * LANES
            inside = (moment >= since) & (moment < until)
            smooth = part[:, :LANES] * SMOOTH_SCALE
            if fits:
                to = aligned(out_at + b * LANES, LANES)
                fit_ref[0, :, to] = jnp.where(inside, smooth, 0.0)
                fit_ref[1, :, to] = jnp.where(inside, part[:, LANES:] * SLOPE_SCALE, 0.0)
            if resids:
                resid = x[:, (b + 1) * LANES : (b + 2) * LANES] - smooth
                resid_ref[k, :, aligned(piece_at + b * LANES, LANES)] = jnp.where(inside, resid, 0.0)

        def starts_here(a):
            return (a > mark - HALF) & (a < mark + span)

        def stops_here(z):
            return (z > mark) & (z < mark + span + HALF)

        holds = False
        for r in range(ROWS):
            holds = holds | starts_here(first_ref[mine * ROWS + r])
            holds = holds | stops_here(last_ref[mine * ROWS + r])

        @pl.when(holds)
        def _():
            def mend(r, left, centre, side):
                b = (left + LANES) // LANES - 1
                v = x_ref[:, aligned(at + b * LANES, 2 * LANES)]
                j = lax.broadcasted_iota(jnp.int32, (ROWS, 2 * LANES), 1) + (b * LANES - centre)
                w = jnp.where((j >= -HALF) & (j <= HALF), v, 0.0)
                f = jnp.clip(j, -HALF, HALF).astype(jnp.float32)
                level = jnp.sum(w, axis=1, keepdims=True) * (1.0 / TAPS)
                tilt = jnp.sum(w * f, axis=1, keepdims=True) * (1.0 / SECOND)
                curve = f * f - CENTRE_SQ
                bend = jnp.sum(w * curve, axis=1, keepdims=True) * (1.0 / FOURTH)
                smooth = level + tilt * f + bend * curve
                slope = HALF * (tilt + 2.0 * f * bend)
                held = (j * side >= 1) & (j * side <= HALF)
                for h in range(2):

                    @pl.when((b + h >= 0) & (b + h < blocks))
                    def _():
                        part = slice(h * LANES, (h + 1) * LANES)
                        to = held[:, part] & (row == r)
                        if fits:
                            at_fit = aligned(out_at + (b + h) * LANES, LANES)
                            fit_ref[0, :, at_fit] = jnp.where(
                                to, smooth[:, part], fit_ref[0, :, at_fit]
                            )
                            fit_ref[1, :, at_fit] = jnp.where(
                                to, slope[:, part], fit_ref[1, :, at_fit]
                            )
                        if resids:
                            at_piece = aligned(piece_at + (b + h) * LANES, LANES)
                            resid_ref[k, :, at_piece] = jnp.where(
                                to, v[:, part] - smooth[:, part], resid_ref[k, :, at_piece]
                            )

            def series(r, carry):
                a = first_ref[mine * ROWS + r]
                z = last_ref[mine * ROWS + r]

                @pl.when(starts_here(a))
                def _():
                    mend(r, a - mark, a - mark + HALF, -1)

                @pl.when(stops_here(z))
                def _():
                    mend(r, z - mark - TAPS, z - mark - HALF - 1, 1)

                return carry

            lax.fori_loop(0, ROWS, series, 0)

        if fits:
            give(n, 0).start()
            give(n, 1).start()
        if resids:
            for kk in range(GROUPS):

                @pl.when((k == kk) & (n % per == per - 1))
                def _():
                    piece(kk).start()

        return carry

    lax.fori_loop(0, count, body, 0)
    for copy in sides[late:]:
        copy.wait()
    if resids:
        for kk in range(GROUPS):
            piece(kk).wait()
    if fits:
        for n in range(count):
            give(n, 0).wait()
            give(n, 1).wait()


def fit_steps(plan, first, last, signal, taps, fits, resids, halos, edges, held):
    _, span, count = plan
    rows, width = signal.shape
    ends = halos is not None
    chain = held is not None
    hbm = pl.BlockSpec(memory_space=pltpu.HBM)
    loose = pl.BlockSpec(memory_space=pl.ANY)
    args = [pltpu.with_memory_space_constraint(a, pltpu.HBM) for a in (first, last, signal, taps)]
    args += list(halos or ()) + list(held or ())
    aliases = {len(args) - 2: 0, len(args) - 1: 1} if chain else {}
    wide = jax.ShapeDtypeStruct((rows, width), jnp.float32)
    part = jax.ShapeDtypeStruct((rows, count // GROUPS * span), jnp.float32)
    edge = jax.ShapeDtypeStruct((rows, LANES), jnp.float32)
    out_shape = [wide] * (2 * fits) + [part] * (GROUPS * resids) + [edge] * (2 * edges)
    scratch = [
        pltpu.VMEM((rows, count * span + (4 if ends else 2) * LANES), jnp.float32),
        pltpu.VMEM(taps.shape, taps.dtype),
        pltpu.SMEM(first.shape, jnp.int32),
        pltpu.SMEM(last.shape, jnp.int32),
        pltpu.SemaphoreType.DMA((count,)),
        pltpu.SemaphoreType.DMA((9,)),
    ]
    if fits:
        scratch += [
            pltpu.VMEM((2, rows, count * span), jnp.float32),
            pltpu.SemaphoreType.DMA((2, count)),
        ]
    if resids:
        scratch += [
            pltpu.VMEM((GROUPS, rows, count // GROUPS * span), jnp.float32),
            pltpu.SemaphoreType.DMA((GROUPS,)),
        ]
    return pl.pallas_call(
        functools.partial(fit_kernel, plan, fits, resids, ends, edges, chain),
        in_specs=[hbm] * 4 + [loose] * len(halos or ()) + [hbm] * len(held or ()),
        out_specs=[hbm] * (2 * fits) + [loose] * (GROUPS * resids + 2 * edges),
        out_shape=out_shape,
        scratch_shapes=scratch,
        input_output_aliases=aliases,
        compiler_params=pltpu.CompilerParams(vmem_limit_bytes=12 * MIB),
        cost_estimate=pl.CostEstimate(
            flops=count * 3 * rows * span * 256 * 4,
            bytes_accessed=count * rows * span * 4 * 4,
            transcendentals=0,
        ),
    )(*args)


def gram_kernel(add, spread, *refs):
    parts, refs = refs[:GROUPS], refs[GROUPS:]
    if add:
        so_far_ref, refs = refs[0], refs[1:]
    out_ref, stack_ref = refs
    mine = lax.axis_index("series")
    for k in range(GROUPS):
        at = pl.multiple_of((mine + GROUPS - k) % GROUPS * ROWS, ROWS)
        x = parts[k][...]
        a = x.astype(jnp.bfloat16)
        b = (x - a.astype(jnp.float32)).astype(jnp.bfloat16)
        stack_ref[pl.ds(at, ROWS)] = a
        stack_ref[pl.ds(64 + at, ROWS)] = a
        stack_ref[pl.ds(128 + at, ROWS)] = b
        stack_ref[pl.ds(192 + at, ROWS)] = b
    both = lax.dot_general(
        stack_ref[64:192],
        stack_ref[...],
        (((1,), (1,)), ((), ())),
        preferred_element_type=jnp.float32,
    )
    gram = both[:64, :128] + (both[64:, :128] + both[:64, 128:] + both[64:, 128:])
    low = lax.broadcasted_iota(jnp.int32, (8, LANES), 1) < 64
    for g in range(GROUPS):
        rows = jnp.where(low, gram[16 * g : 16 * g + 8], gram[16 * g + 8 : 16 * g + 16])
        if add:
            rows = rows + so_far_ref[g]
        if spread:
            for n in range(spread):
                out_ref[n, g] = rows
        else:
            out_ref[g] = rows


def gram_of(parts, so_far, spread):
    width = parts[0].shape[1]
    vmem = pl.BlockSpec(memory_space=pltpu.VMEM)
    args = list(parts) + ([] if so_far is None else [so_far])
    lead = (spread,) if spread else ()
    return pl.pallas_call(
        functools.partial(gram_kernel, so_far is not None, spread),
        in_specs=[vmem] * len(args),
        out_specs=vmem,
        out_shape=jax.ShapeDtypeStruct((*lead, GROUPS, 8, LANES), jnp.float32),
        scratch_shapes=[pltpu.VMEM((256, width), jnp.bfloat16)],
        compiler_params=pltpu.CompilerParams(vmem_limit_bytes=12 * MIB),
        cost_estimate=pl.CostEstimate(
            flops=128 * 256 * width * 2, bytes_accessed=64 * width * 4, transcendentals=0
        ),
    )(*args)


def packed(rows):
    return jnp.concatenate([rows[:8], rows[8:]], axis=1)


def exchanged(pieces):
    parts = [pieces[0]]
    for k in (2, 1, 3):
        pairs = [(s, (s + k) % GROUPS) for s in range(GROUPS)]
        parts.append(lax.ppermute(pieces[k], "series", pairs))
    return [parts[0], parts[2], parts[1], parts[3]]


def shards(taps, signal, valid_start, valid_end):
    rows, width = signal.shape
    devices = lax.axis_size(TIME)
    taps = jnp.asarray(taps, jnp.bfloat16)
    mine = lax.axis_index("series")
    edge = width // 16
    early, mid, late = (
        (edge, edge * 3 // 2, 4),
        (edge * 7, edge, 8),
        (edge * 15, edge // 2, 4),
    )

    def fit(plan, fits, resids, halos=None, edges=False, held=None):
        return fit_steps(
            plan, valid_start, valid_end, signal, taps, fits, resids, halos, edges, held
        )

    first = lax.dynamic_slice_in_dim(valid_start, mine * rows, rows)[:, None]
    last = lax.dynamic_slice_in_dim(valid_end, mine * rows, rows)[:, None]
    shared = jnp.minimum(last, valid_end[None, :]) - jnp.maximum(first, valid_start[None, :])
    shared = packed(shared.astype(jnp.float32))

    *pieces, front, back = fit(early, False, True, edges=True)
    parts = exchanged(pieces)
    *pieces, = fit(mid, True, True)
    held, pieces = pieces[:2], pieces[2:]
    parts_mid = exchanged(pieces)
    left = lax.ppermute(back, TIME, [(t, t + 1) for t in range(devices - 1)])
    right = lax.ppermute(front, TIME, [(t + 1, t) for t in range(devices - 1)])
    gram = gram_of(parts, None, None)
    pieces = fit(late, True, True, halos=(left, right), held=held)
    held, pieces = pieces[:2], pieces[2:]
    parts = exchanged(pieces)
    gram = gram_of(parts_mid, gram, None)
    copies = gram_of(parts, gram, devices).reshape(devices * GROUPS, 8, LANES)
    copies = lax.all_to_all(copies, (*TIME, "series"), 0, 0, tiled=True)
    held = fit(early, True, False, held=held)
    cov = jnp.sum(copies, axis=0) / shared
    return (*held, jnp.concatenate([cov[:, :64], cov[:, 64:]], axis=0))


def solution(mesh):
    split = Mesh(mesh.devices.reshape(4, 4, 2, GROUPS), (*TIME, "series"))
    return jax.shard_map(
        functools.partial(shards, filter_matrix()),
        mesh=split,
        in_specs=(P("series", TIME), P(), P()),
        out_specs=(P("series", TIME), P("series", TIME), P("series", None)),
        check_vma=False,
    )
```

```python
import functools

import jax
import jax.numpy as jnp
import numpy as np
from jax import lax
from jax.experimental import pallas as pl
from jax.experimental.pallas import tpu as pltpu
from jax.sharding import Mesh
from jax.sharding import PartitionSpec as P


HALF = 16
TAPS = 2 * HALF + 1
ROWS = 16
GROUPS = 4
LANES = 128
TIME = ("y", "z", "core")
MIB = 1 << 20

SECOND = float(sum(j * j for j in range(-HALF, HALF + 1)))
CENTRE_SQ = SECOND / TAPS
FOURTH = float(sum((j * j - CENTRE_SQ) ** 2 for j in range(-HALF, HALF + 1)))
SMOOTH_SCALE = 2048.0 / 2387.0
SLOPE_SCALE = HALF * 16.0 / SECOND


def filter_matrix():
    place = np.concatenate([np.arange(128), np.arange(128, 192), np.arange(-64, 0)])
    j = place[:, None] - np.arange(LANES)[None, :]
    near = np.abs(j) <= HALF
    smooth = np.where(near, (163 - j * j) / 2048.0, 0.0)
    slope = np.where(near, j / 16.0, 0.0)
    return np.concatenate([smooth, slope], axis=1).astype(np.float32)


def thirds(x):
    a = x.astype(jnp.bfloat16)
    rest = x - a.astype(jnp.float32)
    b = rest.astype(jnp.bfloat16)
    c = (rest - b.astype(jnp.float32)).astype(jnp.bfloat16)
    return a, b, c


def aligned(start, size):
    return pl.ds(pl.multiple_of(start, LANES), size)


def fit_kernel(plan, fits, resids, ends, *refs):
    base, span, count = plan
    blocks = span // LANES
    refs = list(refs)
    whole = ends and base == 0
    first_hbm, last_hbm, signal_ref, taps_hbm = refs[:4]
    refs = refs[4:]
    if ends:
        halo_refs, refs = refs[:2], refs[2:]
    if fits:
        fit_hbm, refs = refs[:2], refs[2:]
    if resids:
        outs, refs = refs[:GROUPS], refs[GROUPS:]
    x_ref, taps_ref, first_ref, last_ref, in_sems, side_sems = refs[:6]
    refs = refs[6:]
    if fits:
        fit_ref, out_sems = refs[:2]
        refs = refs[2:]
    if resids:
        resid_ref, piece_sems = refs

    width = signal_ref.shape[1]
    per = count // GROUPS
    half = count // 2
    mine = lax.axis_index("series")
    begin = lax.axis_index(TIME) * width

    def place(n):
        return LANES + n * span + (2 * LANES * (n // half) if ends and not whole else 0)

    def source(n):
        return lax.rem(base + n * span, width) if ends and not whole else base + n * span

    def fetch(n):
        return pltpu.make_async_copy(
            signal_ref.at[:, aligned(source(n), span)],
            x_ref.at[:, aligned(place(n), span)],
            in_sems.at[n],
        )

    middle = place(half)
    tail = place(count - 1) + span
    after = (base + count * span) % width
    sides = [(first_hbm, first_ref), (last_hbm, last_ref), (taps_hbm, taps_ref)]
    if not whole:
        sides += [
            (signal_ref.at[:, pl.ds(base - LANES, LANES)], x_ref.at[:, pl.ds(0, LANES)]),
            (signal_ref.at[:, pl.ds(after, LANES)], x_ref.at[:, pl.ds(tail, LANES)]),
        ]
    if ends:
        at_left, at_right = (0, tail) if whole else (middle - LANES, middle - 2 * LANES)
        sides += [
            (halo_refs[0], x_ref.at[:, pl.ds(at_left, LANES)]),
            (halo_refs[1], x_ref.at[:, pl.ds(at_right, LANES)]),
        ]
    sides = [pltpu.make_async_copy(a, b, side_sems.at[n]) for n, (a, b) in enumerate(sides)]
    for copy in sides:
        copy.start()
    for n in range(count):
        fetch(n).start()

    def give(n, kind):
        return pltpu.make_async_copy(
            fit_ref.at[kind, :, aligned(n * span, span)],
            fit_hbm[kind].at[:, aligned(source(n), span)],
            out_sems.at[kind, n],
        )

    def piece(k):
        return pltpu.make_async_copy(resid_ref.at[k], outs[k], piece_sems.at[k])

    lane = lax.broadcasted_iota(jnp.int32, (ROWS, LANES), 1)
    low = lane < 64
    height = ROWS * blocks

    for copy in sides:
        copy.wait()
    fetch(0).wait()

    row = lax.broadcasted_iota(jnp.int32, (ROWS, LANES), 0)
    first = jnp.zeros((ROWS, LANES), jnp.int32)
    last = jnp.zeros((ROWS, LANES), jnp.int32)
    for r in range(ROWS):
        first = jnp.where(row == r, first_ref[mine * ROWS + r], first)
        last = jnp.where(row == r, last_ref[mine * ROWS + r], last)

    def body(n, carry):
        at = place(n)
        k = (n // per + GROUPS - mine) % GROUPS
        mark = begin + source(n)
        out_at = n * span
        piece_at = n % per * span

        @pl.when(n + 1 < count)
        def _():
            fetch(n + 1).wait()

        x = x_ref[:, aligned(at - LANES, span + 2 * LANES)]
        parts = thirds(x)

        def cut(m, b):
            return parts[m][:, b * LANES : (b + 1) * LANES]

        rows = [
            jnp.concatenate(
                [cut(m, b + 1), jnp.where(low, cut(m, b + 2), cut(m, b))], axis=1
            )
            for m in range(3)
            for b in range(blocks)
        ]
        fit = jnp.dot(
            jnp.concatenate(rows, axis=0), taps_ref[...], preferred_element_type=jnp.float32
        )
        fit = fit[:height] + (fit[height : 2 * height] + fit[2 * height :])
        since = first - mark
        until = last - mark
        for b in range(blocks):
            part = fit[b * ROWS : (b + 1) * ROWS]
            moment = lane + b * LANES
            inside = (moment >= since) & (moment < until)
            smooth = part[:, :LANES] * SMOOTH_SCALE
            if fits:
                to = aligned(out_at + b * LANES, LANES)
                fit_ref[0, :, to] = jnp.where(inside, smooth, 0.0)
                fit_ref[1, :, to] = jnp.where(inside, part[:, LANES:] * SLOPE_SCALE, 0.0)
            if resids:
                resid = x[:, (b + 1) * LANES : (b + 2) * LANES] - smooth
                resid_ref[k, :, aligned(piece_at + b * LANES, LANES)] = jnp.where(inside, resid, 0.0)

        def starts_here(a):
            return (a > mark - HALF) & (a < mark + span)

        def stops_here(z):
            return (z > mark) & (z < mark + span + HALF)

        holds = False
        for r in range(ROWS):
            holds = holds | starts_here(first_ref[mine * ROWS + r])
            holds = holds | stops_here(last_ref[mine * ROWS + r])

        @pl.when(holds)
        def _():
            def mend(r, left, centre, side):
                b = (left + LANES) // LANES - 1
                v = x_ref[:, aligned(at + b * LANES, 2 * LANES)]
                j = lax.broadcasted_iota(jnp.int32, (ROWS, 2 * LANES), 1) + (b * LANES - centre)
                w = jnp.where((j >= -HALF) & (j <= HALF), v, 0.0)
                f = jnp.clip(j, -HALF, HALF).astype(jnp.float32)
                level = jnp.sum(w, axis=1, keepdims=True) * (1.0 / TAPS)
                tilt = jnp.sum(w * f, axis=1, keepdims=True) * (1.0 / SECOND)
                curve = f * f - CENTRE_SQ
                bend = jnp.sum(w * curve, axis=1, keepdims=True) * (1.0 / FOURTH)
                smooth = level + tilt * f + bend * curve
                slope = HALF * (tilt + 2.0 * f * bend)
                held = (j * side >= 1) & (j * side <= HALF)
                for h in range(2):

                    @pl.when((b + h >= 0) & (b + h < blocks))
                    def _():
                        part = slice(h * LANES, (h + 1) * LANES)
                        to = held[:, part] & (row == r)
                        if fits:
                            at_fit = aligned(out_at + (b + h) * LANES, LANES)
                            fit_ref[0, :, at_fit] = jnp.where(
                                to, smooth[:, part], fit_ref[0, :, at_fit]
                            )
                            fit_ref[1, :, at_fit] = jnp.where(
                                to, slope[:, part], fit_ref[1, :, at_fit]
                            )
                        if resids:
                            at_piece = aligned(piece_at + (b + h) * LANES, LANES)
                            resid_ref[k, :, at_piece] = jnp.where(
                                to, v[:, part] - smooth[:, part], resid_ref[k, :, at_piece]
                            )

            def series(r, carry):
                a = first_ref[mine * ROWS + r]
                z = last_ref[mine * ROWS + r]

                @pl.when(starts_here(a))
                def _():
                    mend(r, a - mark, a - mark + HALF, -1)

                @pl.when(stops_here(z))
                def _():
                    mend(r, z - mark - TAPS, z - mark - HALF - 1, 1)

                return carry

            lax.fori_loop(0, ROWS, series, 0)

        if fits:
            give(n, 0).start()
            give(n, 1).start()
        if resids:
            for kk in range(GROUPS):

                @pl.when((k == kk) & (n % per == per - 1))
                def _():
                    piece(kk).start()

        return carry

    lax.fori_loop(0, count, body, 0)
    if resids:
        for kk in range(GROUPS):
            piece(kk).wait()
    if fits:
        for n in range(count):
            give(n, 0).wait()
            give(n, 1).wait()


def fit_steps(plan, first, last, signal, taps, fits, resids, halos):
    base, span, count = plan
    rows, width = signal.shape
    ends = halos is not None
    margins = 4 if ends and base else 2
    if not fits:
        taps = taps[:, :LANES]
    hbm = pl.BlockSpec(memory_space=pltpu.HBM)
    loose = pl.BlockSpec(memory_space=pl.ANY)
    args = [pltpu.with_memory_space_constraint(a, pltpu.HBM) for a in (first, last, signal, taps)]
    args += list(halos or ())
    wide = jax.ShapeDtypeStruct((rows, width), jnp.float32)
    part = jax.ShapeDtypeStruct((rows, count // GROUPS * span), jnp.float32)
    scratch = [
        pltpu.VMEM((rows, count * span + margins * LANES), jnp.float32),
        pltpu.VMEM(taps.shape, taps.dtype),
        pltpu.SMEM(first.shape, jnp.int32),
        pltpu.SMEM(last.shape, jnp.int32),
        pltpu.SemaphoreType.DMA((count,)),
        pltpu.SemaphoreType.DMA((7,)),
    ]
    if fits:
        scratch += [
            pltpu.VMEM((2, rows, count * span), jnp.float32),
            pltpu.SemaphoreType.DMA((2, count)),
        ]
    if resids:
        scratch += [
            pltpu.VMEM((GROUPS, rows, count // GROUPS * span), jnp.float32),
            pltpu.SemaphoreType.DMA((GROUPS,)),
        ]
    return pl.pallas_call(
        functools.partial(fit_kernel, plan, fits, resids, ends),
        in_specs=[hbm] * 4 + [loose] * len(halos or ()),
        out_specs=[hbm] * (2 * fits) + [loose] * (GROUPS * resids),
        out_shape=[wide] * (2 * fits) + [part] * (GROUPS * resids),
        scratch_shapes=scratch,
        compiler_params=pltpu.CompilerParams(vmem_limit_bytes=16 * MIB),
        cost_estimate=pl.CostEstimate(
            flops=count * 3 * rows * span * 256 * 4,
            bytes_accessed=count * rows * span * 4 * 4,
            transcendentals=0,
        ),
    )(*args)


def gram_kernel(add, spread, *refs):
    parts, refs = refs[:GROUPS], refs[GROUPS:]
    if add:
        so_far_ref, refs = refs[0], refs[1:]
    out_ref, stack_ref = refs
    mine = lax.axis_index("series")
    for k in range(GROUPS):
        at = pl.multiple_of((mine + GROUPS - k) % GROUPS * ROWS, ROWS)
        x = parts[k][...]
        a = x.astype(jnp.bfloat16)
        b = (x - a.astype(jnp.float32)).astype(jnp.bfloat16)
        stack_ref[pl.ds(at, ROWS)] = a
        stack_ref[pl.ds(64 + at, ROWS)] = b
    both = lax.dot_general(
        stack_ref[...],
        stack_ref[...],
        (((1,), (1,)), ((), ())),
        preferred_element_type=jnp.float32,
    )
    gram = both[:64] + both[64:]
    gram = gram + pltpu.roll(gram, 64, 1)
    low = lax.broadcasted_iota(jnp.int32, (8, LANES), 1) < 64
    for g in range(GROUPS):
        rows = jnp.where(low, gram[16 * g : 16 * g + 8], gram[16 * g + 8 : 16 * g + 16])
        if add:
            rows = rows + so_far_ref[g]
        if spread:
            for n in range(spread):
                out_ref[n, g] = rows
        else:
            out_ref[g] = rows


def gram_of(parts, so_far, spread):
    width = parts[0].shape[1]
    vmem = pl.BlockSpec(memory_space=pltpu.VMEM)
    args = list(parts) + ([] if so_far is None else [so_far])
    lead = (spread,) if spread else ()
    return pl.pallas_call(
        functools.partial(gram_kernel, so_far is not None, spread),
        in_specs=[vmem] * len(args),
        out_specs=vmem,
        out_shape=jax.ShapeDtypeStruct((*lead, GROUPS, 8, LANES), jnp.float32),
        scratch_shapes=[pltpu.VMEM((128, width), jnp.bfloat16)],
        compiler_params=pltpu.CompilerParams(vmem_limit_bytes=12 * MIB),
        cost_estimate=pl.CostEstimate(
            flops=128 * 128 * width * 2, bytes_accessed=64 * width * 4, transcendentals=0
        ),
    )(*args)


def packed(rows):
    return jnp.concatenate([rows[:8], rows[8:]], axis=1)


def exchanged(pieces):
    parts = [pieces[0]]
    for k in (2, 1, 3):
        pairs = [(s, (s + k) % GROUPS) for s in range(GROUPS)]
        parts.append(lax.ppermute(pieces[k], "series", pairs))
    return [parts[0], parts[2], parts[1], parts[3]]


def shards(taps, signal, valid_start, valid_end):
    rows, width = signal.shape
    devices = lax.axis_size(TIME)
    taps = jnp.asarray(taps, jnp.bfloat16)
    mine = lax.axis_index("series")
    span = width // 8
    early, late, whole = (2 * span, span, 4), (6 * span, span, 4), (0, span, 8)

    def fit(plan, fits, resids, halos=None):
        return fit_steps(plan, valid_start, valid_end, signal, taps, fits, resids, halos)

    first = lax.dynamic_slice_in_dim(valid_start, mine * rows, rows)[:, None]
    last = lax.dynamic_slice_in_dim(valid_end, mine * rows, rows)[:, None]
    shared = jnp.minimum(last, valid_end[None, :]) - jnp.maximum(first, valid_start[None, :])
    shared = packed(shared.astype(jnp.float32))

    left = lax.ppermute(signal[:, width - LANES :], TIME, [(t, t + 1) for t in range(devices - 1)])
    right = lax.ppermute(
        signal[:, :LANES], TIME, [(t + 1, t) for t in range(devices - 1)]
    )
    halos = (left, right)
    parts = exchanged(fit(early, False, True))
    parts_late = exchanged(fit(late, False, True, halos))
    gram = gram_of(parts, None, None)
    smooth, slope = fit(whole, True, False, halos)
    copies = gram_of(parts_late, gram, devices)
    copies = copies.reshape(devices * GROUPS, 8, LANES)
    copies = lax.all_to_all(copies, (*TIME, "series"), 0, 0, tiled=True)
    cov = jnp.sum(copies, axis=0) / shared
    return smooth, slope, jnp.concatenate([cov[:, :64], cov[:, 64:]], axis=0)


def solution(mesh):
    split = Mesh(mesh.devices.reshape(4, 4, 2, GROUPS), (*TIME, "series"))
    return jax.shard_map(
        functools.partial(shards, filter_matrix()),
        mesh=split,
        in_specs=(P("series", TIME), P(), P()),
        out_specs=(P("series", TIME), P("series", TIME), P("series", None)),
        check_vma=False,
    )
```

```python
import functools

import jax
import jax.numpy as jnp
import numpy as np
from jax import lax
from jax.experimental import pallas as pl
from jax.experimental.pallas import tpu as pltpu
from jax.sharding import Mesh
from jax.sharding import PartitionSpec as P


HALF = 16
TAPS = 2 * HALF + 1
ROWS = 16
GROUPS = 4
LANES = 128
TIME = ("y", "z", "core")
MIB = 1 << 20

SECOND = float(sum(j * j for j in range(-HALF, HALF + 1)))
CENTRE_SQ = SECOND / TAPS
FOURTH = float(sum((j * j - CENTRE_SQ) ** 2 for j in range(-HALF, HALF + 1)))
SMOOTH_SCALE = 2048.0 / 2387.0
SLOPE_SCALE = HALF * 16.0 / SECOND


def filter_matrix():
    place = np.concatenate([np.arange(128), np.arange(128, 192), np.arange(-64, 0)])
    j = place[:, None] - np.arange(LANES)[None, :]
    near = np.abs(j) <= HALF
    smooth = np.where(near, (163 - j * j) / 2048.0, 0.0)
    slope = np.where(near, j / 16.0, 0.0)
    return np.concatenate([smooth, slope], axis=1).astype(np.float32)


def thirds(x):
    a = x.astype(jnp.bfloat16)
    rest = x - a.astype(jnp.float32)
    b = rest.astype(jnp.bfloat16)
    c = (rest - b.astype(jnp.float32)).astype(jnp.bfloat16)
    return a, b, c


def aligned(start, size):
    return pl.ds(pl.multiple_of(start, LANES), size)


def fit_kernel(plan, fits, resids, ends, edges, *refs):
    base, span, count = plan
    blocks = span // LANES
    refs = list(refs)
    whole = ends and base == 0
    first_hbm, last_hbm, signal_ref, taps_hbm = refs[:4]
    refs = refs[4:]
    if ends:
        halo_refs, refs = refs[:2], refs[2:]
    if fits:
        fit_hbm, refs = refs[:2], refs[2:]
    if resids:
        outs, refs = refs[:GROUPS], refs[GROUPS:]
    if edges:
        edge_refs, refs = refs[:2], refs[2:]
    x_ref, taps_ref, first_ref, last_ref, in_sems, side_sems = refs[:6]
    refs = refs[6:]
    if fits:
        fit_ref, out_sems = refs[:2]
        refs = refs[2:]
    if resids:
        resid_ref, piece_sems = refs

    width = signal_ref.shape[1]
    per = count // GROUPS
    half = count // 2
    mine = lax.axis_index("series")
    begin = lax.axis_index(TIME) * width

    def place(n):
        return LANES + n * span + (2 * LANES * (n // half) if ends and not whole else 0)

    def source(n):
        return lax.rem(base + n * span, width) if ends and not whole else base + n * span

    def fetch(n):
        return pltpu.make_async_copy(
            signal_ref.at[:, aligned(source(n), span)],
            x_ref.at[:, aligned(place(n), span)],
            in_sems.at[n],
        )

    middle = place(half)
    tail = place(count - 1) + span
    after = (base + count * span) % width
    sides = [(first_hbm, first_ref), (last_hbm, last_ref), (taps_hbm, taps_ref)]
    if not whole:
        sides += [
            (signal_ref.at[:, pl.ds(base - LANES, LANES)], x_ref.at[:, pl.ds(0, LANES)]),
            (signal_ref.at[:, pl.ds(after, LANES)], x_ref.at[:, pl.ds(tail, LANES)]),
        ]
    if ends:
        at_left, at_right = (0, tail) if whole else (middle - LANES, middle - 2 * LANES)
        sides += [
            (halo_refs[0], x_ref.at[:, pl.ds(at_left, LANES)]),
            (halo_refs[1], x_ref.at[:, pl.ds(at_right, LANES)]),
        ]
    needed = len(sides)
    if edges:
        sides += [
            (signal_ref.at[:, pl.ds(0, LANES)], edge_refs[0]),
            (signal_ref.at[:, pl.ds(width - LANES, LANES)], edge_refs[1]),
        ]
    sides = [pltpu.make_async_copy(a, b, side_sems.at[n]) for n, (a, b) in enumerate(sides)]
    for copy in sides[:needed]:
        copy.start()
    for n in range(count):
        fetch(n).start()
    for copy in sides[needed:]:
        copy.start()

    def give(n, kind):
        return pltpu.make_async_copy(
            fit_ref.at[kind, :, aligned(n * span, span)],
            fit_hbm[kind].at[:, aligned(source(n), span)],
            out_sems.at[kind, n],
        )

    def piece(k):
        return pltpu.make_async_copy(resid_ref.at[k], outs[k], piece_sems.at[k])

    lane = lax.broadcasted_iota(jnp.int32, (ROWS, LANES), 1)
    low = lane < 64
    height = ROWS * blocks

    for copy in sides[:needed]:
        copy.wait()
    fetch(0).wait()

    row = lax.broadcasted_iota(jnp.int32, (ROWS, LANES), 0)
    first = jnp.zeros((ROWS, LANES), jnp.int32)
    last = jnp.zeros((ROWS, LANES), jnp.int32)
    for r in range(ROWS):
        first = jnp.where(row == r, first_ref[mine * ROWS + r], first)
        last = jnp.where(row == r, last_ref[mine * ROWS + r], last)

    def body(n, carry):
        at = place(n)
        k = (n // per + GROUPS - mine) % GROUPS
        mark = begin + source(n)
        out_at = n * span
        piece_at = n % per * span

        @pl.when(n + 1 < count)
        def _():
            fetch(n + 1).wait()

        x = x_ref[:, aligned(at - LANES, span + 2 * LANES)]
        parts = thirds(x)

        def cut(m, b):
            return parts[m][:, b * LANES : (b + 1) * LANES]

        rows = [
            jnp.concatenate(
                [cut(m, b + 1), jnp.where(low, cut(m, b + 2), cut(m, b))], axis=1
            )
            for m in range(3)
            for b in range(blocks)
        ]
        fit = jnp.dot(
            jnp.concatenate(rows, axis=0), taps_ref[...], preferred_element_type=jnp.float32
        )
        fit = fit[:height] + (fit[height : 2 * height] + fit[2 * height :])
        since = first - mark
        until = last - mark
        for b in range(blocks):
            part = fit[b * ROWS : (b + 1) * ROWS]
            moment = lane + b * LANES
            inside = (moment >= since) & (moment < until)
            smooth = part[:, :LANES] * SMOOTH_SCALE
            if fits:
                to = aligned(out_at + b * LANES, LANES)
                fit_ref[0, :, to] = jnp.where(inside, smooth, 0.0)
                fit_ref[1, :, to] = jnp.where(inside, part[:, LANES:] * SLOPE_SCALE, 0.0)
            if resids:
                resid = x[:, (b + 1) * LANES : (b + 2) * LANES] - smooth
                resid_ref[k, :, aligned(piece_at + b * LANES, LANES)] = jnp.where(inside, resid, 0.0)

        def starts_here(a):
            return (a > mark - HALF) & (a < mark + span)

        def stops_here(z):
            return (z > mark) & (z < mark + span + HALF)

        holds = False
        for r in range(ROWS):
            holds = holds | starts_here(first_ref[mine * ROWS + r])
            holds = holds | stops_here(last_ref[mine * ROWS + r])

        @pl.when(holds)
        def _():
            def mend(r, left, centre, side):
                b = (left + LANES) // LANES - 1
                v = x_ref[:, aligned(at + b * LANES, 2 * LANES)]
                j = lax.broadcasted_iota(jnp.int32, (ROWS, 2 * LANES), 1) + (b * LANES - centre)
                w = jnp.where((j >= -HALF) & (j <= HALF), v, 0.0)
                f = jnp.clip(j, -HALF, HALF).astype(jnp.float32)
                level = jnp.sum(w, axis=1, keepdims=True) * (1.0 / TAPS)
                tilt = jnp.sum(w * f, axis=1, keepdims=True) * (1.0 / SECOND)
                curve = f * f - CENTRE_SQ
                bend = jnp.sum(w * curve, axis=1, keepdims=True) * (1.0 / FOURTH)
                smooth = level + tilt * f + bend * curve
                slope = HALF * (tilt + 2.0 * f * bend)
                held = (j * side >= 1) & (j * side <= HALF)
                for h in range(2):

                    @pl.when((b + h >= 0) & (b + h < blocks))
                    def _():
                        part = slice(h * LANES, (h + 1) * LANES)
                        to = held[:, part] & (row == r)
                        if fits:
                            at_fit = aligned(out_at + (b + h) * LANES, LANES)
                            fit_ref[0, :, at_fit] = jnp.where(
                                to, smooth[:, part], fit_ref[0, :, at_fit]
                            )
                            fit_ref[1, :, at_fit] = jnp.where(
                                to, slope[:, part], fit_ref[1, :, at_fit]
                            )
                        if resids:
                            at_piece = aligned(piece_at + (b + h) * LANES, LANES)
                            resid_ref[k, :, at_piece] = jnp.where(
                                to, v[:, part] - smooth[:, part], resid_ref[k, :, at_piece]
                            )

            def series(r, carry):
                a = first_ref[mine * ROWS + r]
                z = last_ref[mine * ROWS + r]

                @pl.when(starts_here(a))
                def _():
                    mend(r, a - mark, a - mark + HALF, -1)

                @pl.when(stops_here(z))
                def _():
                    mend(r, z - mark - TAPS, z - mark - HALF - 1, 1)

                return carry

            lax.fori_loop(0, ROWS, series, 0)

        if fits:
            give(n, 0).start()
            give(n, 1).start()
        if resids:
            for kk in range(GROUPS):

                @pl.when((k == kk) & (n % per == per - 1))
                def _():
                    piece(kk).start()

        return carry

    lax.fori_loop(0, count, body, 0)
    for copy in sides[needed:]:
        copy.wait()
    if resids:
        for kk in range(GROUPS):
            piece(kk).wait()
    if fits:
        for n in range(count):
            give(n, 0).wait()
            give(n, 1).wait()


def fit_steps(plan, first, last, signal, taps, fits, resids, halos, edges):
    base, span, count = plan
    rows, width = signal.shape
    ends = halos is not None
    margins = 4 if ends and base else 2
    if not fits:
        taps = taps[:, :LANES]
    hbm = pl.BlockSpec(memory_space=pltpu.HBM)
    loose = pl.BlockSpec(memory_space=pl.ANY)
    args = [pltpu.with_memory_space_constraint(a, pltpu.HBM) for a in (first, last, signal, taps)]
    args += list(halos or ())
    wide = jax.ShapeDtypeStruct((rows, width), jnp.float32)
    part = jax.ShapeDtypeStruct((rows, count // GROUPS * span), jnp.float32)
    edge = jax.ShapeDtypeStruct((rows, LANES), jnp.float32)
    scratch = [
        pltpu.VMEM((rows, count * span + margins * LANES), jnp.float32),
        pltpu.VMEM(taps.shape, taps.dtype),
        pltpu.SMEM(first.shape, jnp.int32),
        pltpu.SMEM(last.shape, jnp.int32),
        pltpu.SemaphoreType.DMA((count,)),
        pltpu.SemaphoreType.DMA((7,)),
    ]
    if fits:
        scratch += [
            pltpu.VMEM((2, rows, count * span), jnp.float32),
            pltpu.SemaphoreType.DMA((2, count)),
        ]
    if resids:
        scratch += [
            pltpu.VMEM((GROUPS, rows, count // GROUPS * span), jnp.float32),
            pltpu.SemaphoreType.DMA((GROUPS,)),
        ]
    return pl.pallas_call(
        functools.partial(fit_kernel, plan, fits, resids, ends, edges),
        in_specs=[hbm] * 4 + [loose] * len(halos or ()),
        out_specs=[hbm] * (2 * fits) + [loose] * (GROUPS * resids + 2 * edges),
        out_shape=[wide] * (2 * fits) + [part] * (GROUPS * resids) + [edge] * (2 * edges),
        scratch_shapes=scratch,
        compiler_params=pltpu.CompilerParams(vmem_limit_bytes=16 * MIB),
        cost_estimate=pl.CostEstimate(
            flops=count * 3 * rows * span * 256 * 4,
            bytes_accessed=count * rows * span * 4 * 4,
            transcendentals=0,
        ),
    )(*args)


def gram_kernel(add, spread, *refs):
    parts, refs = refs[:GROUPS], refs[GROUPS:]
    if add:
        so_far_ref, refs = refs[0], refs[1:]
    out_ref, stack_ref = refs
    mine = lax.axis_index("series")
    for k in range(GROUPS):
        at = pl.multiple_of((mine + GROUPS - k) % GROUPS * ROWS, ROWS)
        x = parts[k][...]
        a = x.astype(jnp.bfloat16)
        b = (x - a.astype(jnp.float32)).astype(jnp.bfloat16)
        stack_ref[pl.ds(at, ROWS)] = a
        stack_ref[pl.ds(64 + at, ROWS)] = b
    both = lax.dot_general(
        stack_ref[...],
        stack_ref[...],
        (((1,), (1,)), ((), ())),
        preferred_element_type=jnp.float32,
    )
    gram = both[:64] + both[64:]
    gram = gram + pltpu.roll(gram, 64, 1)
    low = lax.broadcasted_iota(jnp.int32, (8, LANES), 1) < 64
    for g in range(GROUPS):
        rows = jnp.where(low, gram[16 * g : 16 * g + 8], gram[16 * g + 8 : 16 * g + 16])
        if add:
            rows = rows + so_far_ref[g]
        if spread:
            for n in range(spread):
                out_ref[n, g] = rows
        else:
            out_ref[g] = rows


def gram_of(parts, so_far, spread):
    width = parts[0].shape[1]
    vmem = pl.BlockSpec(memory_space=pltpu.VMEM)
    args = list(parts) + ([] if so_far is None else [so_far])
    lead = (spread,) if spread else ()
    return pl.pallas_call(
        functools.partial(gram_kernel, so_far is not None, spread),
        in_specs=[vmem] * len(args),
        out_specs=vmem,
        out_shape=jax.ShapeDtypeStruct((*lead, GROUPS, 8, LANES), jnp.float32),
        scratch_shapes=[pltpu.VMEM((128, width), jnp.bfloat16)],
        compiler_params=pltpu.CompilerParams(vmem_limit_bytes=12 * MIB),
        cost_estimate=pl.CostEstimate(
            flops=128 * 128 * width * 2, bytes_accessed=64 * width * 4, transcendentals=0
        ),
    )(*args)


def packed(rows):
    return jnp.concatenate([rows[:8], rows[8:]], axis=1)


def exchanged(pieces):
    parts = [pieces[0]]
    for k in (2, 1, 3):
        pairs = [(s, (s + k) % GROUPS) for s in range(GROUPS)]
        parts.append(lax.ppermute(pieces[k], "series", pairs))
    return [parts[0], parts[2], parts[1], parts[3]]


def shards(taps, signal, valid_start, valid_end):
    rows, width = signal.shape
    devices = lax.axis_size(TIME)
    taps = jnp.asarray(taps, jnp.bfloat16)
    mine = lax.axis_index("series")
    span = width // 8
    early, late, whole = (2 * span, span, 4), (6 * span, span, 4), (0, span, 8)

    def fit(plan, fits, resids, halos=None, edges=False):
        return fit_steps(plan, valid_start, valid_end, signal, taps, fits, resids, halos, edges)

    first = lax.dynamic_slice_in_dim(valid_start, mine * rows, rows)[:, None]
    last = lax.dynamic_slice_in_dim(valid_end, mine * rows, rows)[:, None]
    shared = jnp.minimum(last, valid_end[None, :]) - jnp.maximum(first, valid_start[None, :])
    shared = packed(shared.astype(jnp.float32))

    *pieces, front, back = fit(early, False, True, edges=True)
    parts = exchanged(pieces)
    left = lax.ppermute(back, TIME, [(t, t + 1) for t in range(devices - 1)])
    right = lax.ppermute(front, TIME, [(t + 1, t) for t in range(devices - 1)])
    halos = (left, right)
    parts_late = exchanged(fit(late, False, True, halos))
    gram = gram_of(parts, None, None)
    smooth, slope = fit(whole, True, False, halos)
    copies = gram_of(parts_late, gram, devices)
    copies = copies.reshape(devices * GROUPS, 8, LANES)
    copies = lax.all_to_all(copies, (*TIME, "series"), 0, 0, tiled=True)
    cov = jnp.sum(copies, axis=0) / shared
    return smooth, slope, jnp.concatenate([cov[:, :64], cov[:, 64:]], axis=0)


def solution(mesh):
    split = Mesh(mesh.devices.reshape(4, 4, 2, GROUPS), (*TIME, "series"))
    return jax.shard_map(
        functools.partial(shards, filter_matrix()),
        mesh=split,
        in_specs=(P("series", TIME), P(), P()),
        out_specs=(P("series", TIME), P("series", TIME), P("series", None)),
        check_vma=False,
    )
```

```python
import functools

import jax
import jax.numpy as jnp
import numpy as np
from jax import lax
from jax.experimental import pallas as pl
from jax.experimental.pallas import tpu as pltpu
from jax.sharding import Mesh
from jax.sharding import PartitionSpec as P


HALF = 16
TAPS = 2 * HALF + 1
ROWS = 16
GROUPS = 4
LANES = 128
TIME = ("y", "z", "core")
MIB = 1 << 20

SECOND = float(sum(j * j for j in range(-HALF, HALF + 1)))
CENTRE_SQ = SECOND / TAPS
FOURTH = float(sum((j * j - CENTRE_SQ) ** 2 for j in range(-HALF, HALF + 1)))
SMOOTH_SCALE = 2048.0 / 2387.0
SLOPE_SCALE = HALF * 16.0 / SECOND


def filter_matrix():
    place = np.concatenate([np.arange(128), np.arange(128, 192), np.arange(-64, 0)])
    j = place[:, None] - np.arange(LANES)[None, :]
    near = np.abs(j) <= HALF
    smooth = np.where(near, (163 - j * j) / 2048.0, 0.0)
    slope = np.where(near, j / 16.0, 0.0)
    return np.concatenate([smooth, slope], axis=1).astype(np.float32)


def thirds(x):
    a = x.astype(jnp.bfloat16)
    rest = x - a.astype(jnp.float32)
    b = rest.astype(jnp.bfloat16)
    c = (rest - b.astype(jnp.float32)).astype(jnp.bfloat16)
    return a, b, c


def aligned(start, size):
    return pl.ds(pl.multiple_of(start, LANES), size)


def fit_kernel(plan, fits, resids, ends, edges, *refs):
    base, span, count = plan
    blocks = span // LANES
    refs = list(refs)
    whole = ends and base == 0
    first_hbm, last_hbm, signal_ref, taps_hbm = refs[:4]
    refs = refs[4:]
    if ends:
        halo_refs, refs = refs[:2], refs[2:]
    if fits:
        fit_hbm, refs = refs[:2], refs[2:]
    if resids:
        outs, refs = refs[:GROUPS], refs[GROUPS:]
    if edges:
        edge_refs, refs = refs[:2], refs[2:]
    x_ref, taps_ref, first_ref, last_ref, in_sems, side_sems = refs[:6]
    refs = refs[6:]
    if fits:
        fit_ref, out_sems = refs[:2]
        refs = refs[2:]
    if resids:
        resid_ref, piece_sems = refs

    width = signal_ref.shape[1]
    per = count // GROUPS
    half = count // 2
    mine = lax.axis_index("series")
    begin = lax.axis_index(TIME) * width
    core = lax.axis_index("core")

    def place(n):
        return LANES + n * span + (2 * LANES * (n // half) if ends and not whole else 0)

    def source(n):
        return lax.rem(base + n * span, width) if ends and not whole else base + n * span

    def fetch(n):
        return pltpu.make_async_copy(
            signal_ref.at[:, aligned(source(n), span)],
            x_ref.at[:, aligned(place(n), span)],
            in_sems.at[n],
        )

    middle = place(half)
    tail = place(count - 1) + span
    after = (base + count * span) % width
    sides = [(first_hbm, first_ref), (last_hbm, last_ref), (taps_hbm, taps_ref)]
    if not whole:
        sides += [
            (signal_ref.at[:, pl.ds(base - LANES, LANES)], x_ref.at[:, pl.ds(0, LANES)]),
            (signal_ref.at[:, pl.ds(after, LANES)], x_ref.at[:, pl.ds(tail, LANES)]),
        ]
    if ends:
        at_left, at_right = (0, tail) if whole else (middle - LANES, middle - 2 * LANES)
        across = core * (at_left - at_right)
        sides += [
            (halo_refs[0], x_ref.at[:, aligned(at_right + across, LANES)]),
            (halo_refs[1], x_ref.at[:, aligned(at_left - across, LANES)]),
        ]
    needed = len(sides)
    if edges:
        sides += [
            (signal_ref.at[:, aligned((1 - core) * (width - LANES), LANES)], edge_refs[0]),
            (signal_ref.at[:, aligned(core * (width - LANES), LANES)], edge_refs[1]),
        ]
    sides = [pltpu.make_async_copy(a, b, side_sems.at[n]) for n, (a, b) in enumerate(sides)]
    for copy in sides[:needed]:
        copy.start()
    for n in range(count):
        fetch(n).start()
    for copy in sides[needed:]:
        copy.start()

    def give(n, kind):
        return pltpu.make_async_copy(
            fit_ref.at[kind, :, aligned(n * span, span)],
            fit_hbm[kind].at[:, aligned(source(n), span)],
            out_sems.at[kind, n],
        )

    def piece(k):
        return pltpu.make_async_copy(resid_ref.at[k], outs[k], piece_sems.at[k])

    lane = lax.broadcasted_iota(jnp.int32, (ROWS, LANES), 1)
    low = lane < 64
    height = ROWS * blocks

    for copy in sides[:needed]:
        copy.wait()
    fetch(0).wait()

    row = lax.broadcasted_iota(jnp.int32, (ROWS, LANES), 0)
    first = jnp.zeros((ROWS, LANES), jnp.int32)
    last = jnp.zeros((ROWS, LANES), jnp.int32)
    for r in range(ROWS):
        first = jnp.where(row == r, first_ref[mine * ROWS + r], first)
        last = jnp.where(row == r, last_ref[mine * ROWS + r], last)

    def body(n, carry):
        at = place(n)
        k = (n // per + GROUPS - mine) % GROUPS
        mark = begin + source(n)
        out_at = n * span
        piece_at = n % per * span

        @pl.when(n + 1 < count)
        def _():
            fetch(n + 1).wait()

        x = x_ref[:, aligned(at - LANES, span + 2 * LANES)]
        parts = thirds(x)

        def cut(m, b):
            return parts[m][:, b * LANES : (b + 1) * LANES]

        rows = [
            jnp.concatenate(
                [cut(m, b + 1), jnp.where(low, cut(m, b + 2), cut(m, b))], axis=1
            )
            for m in range(3)
            for b in range(blocks)
        ]
        fit = jnp.dot(
            jnp.concatenate(rows, axis=0), taps_ref[...], preferred_element_type=jnp.float32
        )
        fit = fit[:height] + (fit[height : 2 * height] + fit[2 * height :])
        since = first - mark
        until = last - mark
        for b in range(blocks):
            part = fit[b * ROWS : (b + 1) * ROWS]
            moment = lane + b * LANES
            inside = (moment >= since) & (moment < until)
            smooth = part[:, :LANES] * SMOOTH_SCALE
            if fits:
                to = aligned(out_at + b * LANES, LANES)
                fit_ref[0, :, to] = jnp.where(inside, smooth, 0.0)
                fit_ref[1, :, to] = jnp.where(inside, part[:, LANES:] * SLOPE_SCALE, 0.0)
            if resids:
                resid = x[:, (b + 1) * LANES : (b + 2) * LANES] - smooth
                resid_ref[k, :, aligned(piece_at + b * LANES, LANES)] = jnp.where(inside, resid, 0.0)

        def starts_here(a):
            return (a > mark - HALF) & (a < mark + span)

        def stops_here(z):
            return (z > mark) & (z < mark + span + HALF)

        holds = False
        for r in range(ROWS):
            holds = holds | starts_here(first_ref[mine * ROWS + r])
            holds = holds | stops_here(last_ref[mine * ROWS + r])

        @pl.when(holds)
        def _():
            def mend(r, left, centre, side):
                b = (left + LANES) // LANES - 1
                v = x_ref[:, aligned(at + b * LANES, 2 * LANES)]
                j = lax.broadcasted_iota(jnp.int32, (ROWS, 2 * LANES), 1) + (b * LANES - centre)
                w = jnp.where((j >= -HALF) & (j <= HALF), v, 0.0)
                f = jnp.clip(j, -HALF, HALF).astype(jnp.float32)
                level = jnp.sum(w, axis=1, keepdims=True) * (1.0 / TAPS)
                tilt = jnp.sum(w * f, axis=1, keepdims=True) * (1.0 / SECOND)
                curve = f * f - CENTRE_SQ
                bend = jnp.sum(w * curve, axis=1, keepdims=True) * (1.0 / FOURTH)
                smooth = level + tilt * f + bend * curve
                slope = HALF * (tilt + 2.0 * f * bend)
                held = (j * side >= 1) & (j * side <= HALF)
                for h in range(2):

                    @pl.when((b + h >= 0) & (b + h < blocks))
                    def _():
                        part = slice(h * LANES, (h + 1) * LANES)
                        to = held[:, part] & (row == r)
                        if fits:
                            at_fit = aligned(out_at + (b + h) * LANES, LANES)
                            fit_ref[0, :, at_fit] = jnp.where(
                                to, smooth[:, part], fit_ref[0, :, at_fit]
                            )
                            fit_ref[1, :, at_fit] = jnp.where(
                                to, slope[:, part], fit_ref[1, :, at_fit]
                            )
                        if resids:
                            at_piece = aligned(piece_at + (b + h) * LANES, LANES)
                            resid_ref[k, :, at_piece] = jnp.where(
                                to, v[:, part] - smooth[:, part], resid_ref[k, :, at_piece]
                            )

            def series(r, carry):
                a = first_ref[mine * ROWS + r]
                z = last_ref[mine * ROWS + r]

                @pl.when(starts_here(a))
                def _():
                    mend(r, a - mark, a - mark + HALF, -1)

                @pl.when(stops_here(z))
                def _():
                    mend(r, z - mark - TAPS, z - mark - HALF - 1, 1)

                return carry

            lax.fori_loop(0, ROWS, series, 0)

        if fits:
            give(n, 0).start()
            give(n, 1).start()
        if resids:
            for kk in range(GROUPS):

                @pl.when((k == kk) & (n % per == per - 1))
                def _():
                    piece(kk).start()

        return carry

    lax.fori_loop(0, count, body, 0)
    for copy in sides[needed:]:
        copy.wait()
    if resids:
        for kk in range(GROUPS):
            piece(kk).wait()
    if fits:
        for n in range(count):
            give(n, 0).wait()
            give(n, 1).wait()


def fit_steps(plan, first, last, signal, taps, fits, resids, halos, edges):
    base, span, count = plan
    rows, width = signal.shape
    ends = halos is not None
    margins = 4 if ends and base else 2
    if not fits:
        taps = taps[:, :LANES]
    hbm = pl.BlockSpec(memory_space=pltpu.HBM)
    loose = pl.BlockSpec(memory_space=pl.ANY)
    args = [pltpu.with_memory_space_constraint(a, pltpu.HBM) for a in (first, last, signal, taps)]
    args += list(halos or ())
    wide = jax.ShapeDtypeStruct((rows, width), jnp.float32)
    part = jax.ShapeDtypeStruct((rows, count // GROUPS * span), jnp.float32)
    edge = jax.ShapeDtypeStruct((rows, LANES), jnp.float32)
    scratch = [
        pltpu.VMEM((rows, count * span + margins * LANES), jnp.float32),
        pltpu.VMEM(taps.shape, taps.dtype),
        pltpu.SMEM(first.shape, jnp.int32),
        pltpu.SMEM(last.shape, jnp.int32),
        pltpu.SemaphoreType.DMA((count,)),
        pltpu.SemaphoreType.DMA((7,)),
    ]
    if fits:
        scratch += [
            pltpu.VMEM((2, rows, count * span), jnp.float32),
            pltpu.SemaphoreType.DMA((2, count)),
        ]
    if resids:
        scratch += [
            pltpu.VMEM((GROUPS, rows, count // GROUPS * span), jnp.float32),
            pltpu.SemaphoreType.DMA((GROUPS,)),
        ]
    return pl.pallas_call(
        functools.partial(fit_kernel, plan, fits, resids, ends, edges),
        in_specs=[hbm] * 4 + [loose] * len(halos or ()),
        out_specs=[hbm] * (2 * fits) + [loose] * (GROUPS * resids + 2 * edges),
        out_shape=[wide] * (2 * fits) + [part] * (GROUPS * resids) + [edge] * (2 * edges),
        scratch_shapes=scratch,
        compiler_params=pltpu.CompilerParams(vmem_limit_bytes=16 * MIB),
        cost_estimate=pl.CostEstimate(
            flops=count * 3 * rows * span * 256 * 4,
            bytes_accessed=count * rows * span * 4 * 4,
            transcendentals=0,
        ),
    )(*args)


def gram_kernel(add, spread, *refs):
    parts, refs = refs[:GROUPS], refs[GROUPS:]
    if add:
        so_far_ref, refs = refs[0], refs[1:]
    out_ref, stack_ref = refs
    mine = lax.axis_index("series")
    for k in range(GROUPS):
        at = pl.multiple_of((mine + GROUPS - k) % GROUPS * ROWS, ROWS)
        x = parts[k][...]
        a = x.astype(jnp.bfloat16)
        b = (x - a.astype(jnp.float32)).astype(jnp.bfloat16)
        stack_ref[pl.ds(at, ROWS)] = a
        stack_ref[pl.ds(64 + at, ROWS)] = b
    both = lax.dot_general(
        stack_ref[...],
        stack_ref[...],
        (((1,), (1,)), ((), ())),
        preferred_element_type=jnp.float32,
    )
    gram = both[:64] + both[64:]
    gram = gram + pltpu.roll(gram, 64, 1)
    low = lax.broadcasted_iota(jnp.int32, (8, LANES), 1) < 64
    for g in range(GROUPS):
        rows = jnp.where(low, gram[16 * g : 16 * g + 8], gram[16 * g + 8 : 16 * g + 16])
        if add:
            rows = rows + so_far_ref[g]
        if spread:
            for n in range(spread):
                out_ref[n, g] = rows
        else:
            out_ref[g] = rows


def gram_of(parts, so_far, spread):
    width = parts[0].shape[1]
    vmem = pl.BlockSpec(memory_space=pltpu.VMEM)
    args = list(parts) + ([] if so_far is None else [so_far])
    lead = (spread,) if spread else ()
    return pl.pallas_call(
        functools.partial(gram_kernel, so_far is not None, spread),
        in_specs=[vmem] * len(args),
        out_specs=vmem,
        out_shape=jax.ShapeDtypeStruct((*lead, GROUPS, 8, LANES), jnp.float32),
        scratch_shapes=[pltpu.VMEM((128, width), jnp.bfloat16)],
        compiler_params=pltpu.CompilerParams(vmem_limit_bytes=12 * MIB),
        cost_estimate=pl.CostEstimate(
            flops=128 * 128 * width * 2, bytes_accessed=64 * width * 4, transcendentals=0
        ),
    )(*args)


def packed(rows):
    return jnp.concatenate([rows[:8], rows[8:]], axis=1)


def exchanged(pieces):
    parts = [pieces[0]]
    for k in (2, 1, 3):
        pairs = [(s, (s + k) % GROUPS) for s in range(GROUPS)]
        parts.append(lax.ppermute(pieces[k], "series", pairs))
    return [parts[0], parts[2], parts[1], parts[3]]


def shards(taps, signal, valid_start, valid_end):
    rows, width = signal.shape
    devices = lax.axis_size(TIME)
    taps = jnp.asarray(taps, jnp.bfloat16)
    mine = lax.axis_index("series")
    span = width // 8
    early, late, whole = (2 * span, span, 4), (6 * span, span, 4), (0, span, 8)

    def fit(plan, fits, resids, halos=None, edges=False):
        return fit_steps(plan, valid_start, valid_end, signal, taps, fits, resids, halos, edges)

    first = lax.dynamic_slice_in_dim(valid_start, mine * rows, rows)[:, None]
    last = lax.dynamic_slice_in_dim(valid_end, mine * rows, rows)[:, None]
    shared = jnp.minimum(last, valid_end[None, :]) - jnp.maximum(first, valid_start[None, :])
    shared = packed(shared.astype(jnp.float32))

    *pieces, near, far = fit(early, False, True, edges=True)
    parts = exchanged(pieces)
    near = lax.ppermute(near, TIME, [(t, t ^ 1) for t in range(devices)])
    pairs = [(t, t + 1) for t in range(1, devices - 1, 2)]
    far = lax.ppermute(far, TIME, pairs + [(b, a) for a, b in pairs])
    halos = (near, far)
    parts_late = exchanged(fit(late, False, True, halos))
    gram = gram_of(parts, None, None)
    smooth, slope = fit(whole, True, False, halos)
    copies = gram_of(parts_late, gram, devices)
    copies = copies.reshape(devices * GROUPS, 8, LANES)
    copies = lax.all_to_all(copies, (*TIME, "series"), 0, 0, tiled=True)
    cov = jnp.sum(copies, axis=0) / shared
    return smooth, slope, jnp.concatenate([cov[:, :64], cov[:, 64:]], axis=0)


def solution(mesh):
    split = Mesh(mesh.devices.reshape(4, 4, 2, GROUPS), (*TIME, "series"))
    return jax.shard_map(
        functools.partial(shards, filter_matrix()),
        mesh=split,
        in_specs=(P("series", TIME), P(), P()),
        out_specs=(P("series", TIME), P("series", TIME), P("series", None)),
        check_vma=False,
    )
```

```python
import functools

import jax
import jax.numpy as jnp
import numpy as np
from jax import lax
from jax.experimental import pallas as pl
from jax.experimental.pallas import tpu as pltpu
from jax.sharding import Mesh
from jax.sharding import PartitionSpec as P


HALF = 16
TAPS = 2 * HALF + 1
ROWS = 16
GROUPS = 4
LANES = 128
TIME = ("y", "z", "core")
MIB = 1 << 20

SECOND = float(sum(j * j for j in range(-HALF, HALF + 1)))
CENTRE_SQ = SECOND / TAPS
FOURTH = float(sum((j * j - CENTRE_SQ) ** 2 for j in range(-HALF, HALF + 1)))
SMOOTH_SCALE = 2048.0 / 2387.0
SLOPE_SCALE = HALF * 16.0 / SECOND


def filter_matrix():
    place = np.concatenate([np.arange(128), np.arange(128, 192), np.arange(-64, 0)])
    j = place[:, None] - np.arange(LANES)[None, :]
    near = np.abs(j) <= HALF
    smooth = np.where(near, (163 - j * j) / 2048.0, 0.0)
    slope = np.where(near, j / 16.0, 0.0)
    return np.concatenate([smooth, slope], axis=1).astype(np.float32)


def thirds(x):
    a = x.astype(jnp.bfloat16)
    rest = x - a.astype(jnp.float32)
    b = rest.astype(jnp.bfloat16)
    c = (rest - b.astype(jnp.float32)).astype(jnp.bfloat16)
    return a, b, c


def aligned(start, size):
    return pl.ds(pl.multiple_of(start, LANES), size)


def fit_kernel(plan, fits, resids, ends, edges, *refs):
    base, span, count = plan
    blocks = span // LANES
    refs = list(refs)
    whole = ends and base == 0
    first_hbm, last_hbm, signal_ref, taps_hbm = refs[:4]
    refs = refs[4:]
    if ends:
        halo_refs, refs = refs[:2], refs[2:]
    if fits:
        fit_hbm, refs = refs[:2], refs[2:]
    if resids:
        outs, refs = refs[:GROUPS], refs[GROUPS:]
    if edges:
        edge_refs, refs = refs[:2], refs[2:]
    x_ref, taps_ref, first_ref, last_ref, in_sems, side_sems = refs[:6]
    refs = refs[6:]
    if fits:
        fit_ref, out_sems = refs[:2]
        refs = refs[2:]
    if resids:
        resid_ref, piece_sems = refs

    width = signal_ref.shape[1]
    per = count // GROUPS
    half = count // 2
    mine = lax.axis_index("series")
    begin = lax.axis_index(TIME) * width
    core = lax.axis_index("core")

    def place(n):
        return LANES + n * span + (2 * LANES * (n // half) if ends and not whole else 0)

    def source(n):
        return lax.rem(base + n * span, width) if ends and not whole else base + n * span

    def fetch(n):
        return pltpu.make_async_copy(
            signal_ref.at[:, aligned(source(n), span)],
            x_ref.at[:, aligned(place(n), span)],
            in_sems.at[n],
        )

    middle = place(half)
    tail = place(count - 1) + span
    after = (base + count * span) % width
    sides = [(first_hbm, first_ref), (last_hbm, last_ref), (taps_hbm, taps_ref)]
    if not whole:
        sides += [
            (signal_ref.at[:, pl.ds(base - LANES, LANES)], x_ref.at[:, pl.ds(0, LANES)]),
            (signal_ref.at[:, pl.ds(after, LANES)], x_ref.at[:, pl.ds(tail, LANES)]),
        ]
    if ends:
        at_left, at_right = (0, tail) if whole else (middle - LANES, middle - 2 * LANES)
        across = core * (at_left - at_right)
        sides += [
            (halo_refs[0], x_ref.at[:, aligned(at_right + across, LANES)]),
            (halo_refs[1], x_ref.at[:, aligned(at_left - across, LANES)]),
        ]
    needed = len(sides)
    if edges:
        sides += [
            (signal_ref.at[:, aligned((1 - core) * (width - LANES), LANES)], edge_refs[0]),
            (signal_ref.at[:, aligned(core * (width - LANES), LANES)], edge_refs[1]),
        ]
    sides = [pltpu.make_async_copy(a, b, side_sems.at[n]) for n, (a, b) in enumerate(sides)]
    for copy in sides[:needed]:
        copy.start()
    for n in range(count):
        fetch(n).start()
    for copy in sides[needed:]:
        copy.start()

    def give(n, kind):
        return pltpu.make_async_copy(
            fit_ref.at[kind, :, aligned(n * span, span)],
            fit_hbm[kind].at[:, aligned(source(n), span)],
            out_sems.at[kind, n],
        )

    def piece(k):
        return pltpu.make_async_copy(resid_ref.at[k], outs[k], piece_sems.at[k])

    lane = lax.broadcasted_iota(jnp.int32, (ROWS, LANES), 1)
    low = lane < 64
    height = ROWS * blocks

    for copy in sides[:needed]:
        copy.wait()
    fetch(0).wait()

    row = lax.broadcasted_iota(jnp.int32, (ROWS, LANES), 0)
    first = jnp.zeros((ROWS, LANES), jnp.int32)
    last = jnp.zeros((ROWS, LANES), jnp.int32)
    for r in range(ROWS):
        first = jnp.where(row == r, first_ref[mine * ROWS + r], first)
        last = jnp.where(row == r, last_ref[mine * ROWS + r], last)

    def body(n, carry):
        at = place(n)
        k = (n // per + GROUPS - mine) % GROUPS
        mark = begin + source(n)
        out_at = n * span
        piece_at = n % per * span

        @pl.when(n + 1 < count)
        def _():
            fetch(n + 1).wait()

        x = x_ref[:, aligned(at - LANES, span + 2 * LANES)]
        parts = thirds(x)

        def cut(m, b):
            return parts[m][:, b * LANES : (b + 1) * LANES]

        rows = [
            jnp.concatenate(
                [cut(m, b + 1), jnp.where(low, cut(m, b + 2), cut(m, b))], axis=1
            )
            for m in range(3)
            for b in range(blocks)
        ]
        fit = jnp.dot(
            jnp.concatenate(rows, axis=0), taps_ref[...], preferred_element_type=jnp.float32
        )
        fit = fit[:height] + (fit[height : 2 * height] + fit[2 * height :])
        since = first - mark
        until = last - mark
        for b in range(blocks):
            part = fit[b * ROWS : (b + 1) * ROWS]
            moment = lane + b * LANES
            inside = (moment >= since) & (moment < until)
            smooth = part[:, :LANES] * SMOOTH_SCALE
            if fits:
                to = aligned(out_at + b * LANES, LANES)
                fit_ref[0, :, to] = jnp.where(inside, smooth, 0.0)
                fit_ref[1, :, to] = jnp.where(inside, part[:, LANES:] * SLOPE_SCALE, 0.0)
            if resids:
                resid = x[:, (b + 1) * LANES : (b + 2) * LANES] - smooth
                resid_ref[k, :, aligned(piece_at + b * LANES, LANES)] = jnp.where(inside, resid, 0.0)

        def starts_here(a):
            return (a > mark - HALF) & (a < mark + span)

        def stops_here(z):
            return (z > mark) & (z < mark + span + HALF)

        holds = False
        for r in range(ROWS):
            holds = holds | starts_here(first_ref[mine * ROWS + r])
            holds = holds | stops_here(last_ref[mine * ROWS + r])

        @pl.when(holds)
        def _():
            def mend(r, left, centre, side):
                b = (left + LANES) // LANES - 1
                v = x_ref[:, aligned(at + b * LANES, 2 * LANES)]
                j = lax.broadcasted_iota(jnp.int32, (ROWS, 2 * LANES), 1) + (b * LANES - centre)
                w = jnp.where((j >= -HALF) & (j <= HALF), v, 0.0)
                f = jnp.clip(j, -HALF, HALF).astype(jnp.float32)
                level = jnp.sum(w, axis=1, keepdims=True) * (1.0 / TAPS)
                tilt = jnp.sum(w * f, axis=1, keepdims=True) * (1.0 / SECOND)
                curve = f * f - CENTRE_SQ
                bend = jnp.sum(w * curve, axis=1, keepdims=True) * (1.0 / FOURTH)
                smooth = level + tilt * f + bend * curve
                slope = HALF * (tilt + 2.0 * f * bend)
                held = (j * side >= 1) & (j * side <= HALF)
                for h in range(2):

                    @pl.when((b + h >= 0) & (b + h < blocks))
                    def _():
                        part = slice(h * LANES, (h + 1) * LANES)
                        to = held[:, part] & (row == r)
                        if fits:
                            at_fit = aligned(out_at + (b + h) * LANES, LANES)
                            fit_ref[0, :, at_fit] = jnp.where(
                                to, smooth[:, part], fit_ref[0, :, at_fit]
                            )
                            fit_ref[1, :, at_fit] = jnp.where(
                                to, slope[:, part], fit_ref[1, :, at_fit]
                            )
                        if resids:
                            at_piece = aligned(piece_at + (b + h) * LANES, LANES)
                            resid_ref[k, :, at_piece] = jnp.where(
                                to, v[:, part] - smooth[:, part], resid_ref[k, :, at_piece]
                            )

            def series(r, carry):
                a = first_ref[mine * ROWS + r]
                z = last_ref[mine * ROWS + r]

                @pl.when(starts_here(a))
                def _():
                    mend(r, a - mark, a - mark + HALF, -1)

                @pl.when(stops_here(z))
                def _():
                    mend(r, z - mark - TAPS, z - mark - HALF - 1, 1)

                return carry

            lax.fori_loop(0, ROWS, series, 0)

        if fits:
            give(n, 0).start()
            give(n, 1).start()
        if resids:
            for kk in range(GROUPS):

                @pl.when((k == kk) & (n % per == per - 1))
                def _():
                    piece(kk).start()

        return carry

    lax.fori_loop(0, count, body, 0)
    for copy in sides[needed:]:
        copy.wait()
    if resids:
        for kk in range(GROUPS):
            piece(kk).wait()
    if fits:
        for n in range(count):
            give(n, 0).wait()
            give(n, 1).wait()


def fit_steps(plan, first, last, signal, taps, fits, resids, halos, edges):
    base, span, count = plan
    rows, width = signal.shape
    ends = halos is not None
    margins = 4 if ends and base else 2
    if not fits:
        taps = taps[:, :LANES]
    hbm = pl.BlockSpec(memory_space=pltpu.HBM)
    loose = pl.BlockSpec(memory_space=pl.ANY)
    args = [pltpu.with_memory_space_constraint(a, pltpu.HBM) for a in (first, last, signal, taps)]
    args += list(halos or ())
    wide = jax.ShapeDtypeStruct((rows, width), jnp.float32)
    part = jax.ShapeDtypeStruct((rows, count // GROUPS * span), jnp.float32)
    edge = jax.ShapeDtypeStruct((rows, LANES), jnp.float32)
    scratch = [
        pltpu.VMEM((rows, count * span + margins * LANES), jnp.float32),
        pltpu.VMEM(taps.shape, taps.dtype),
        pltpu.SMEM(first.shape, jnp.int32),
        pltpu.SMEM(last.shape, jnp.int32),
        pltpu.SemaphoreType.DMA((count,)),
        pltpu.SemaphoreType.DMA((7,)),
    ]
    if fits:
        scratch += [
            pltpu.VMEM((2, rows, count * span), jnp.float32),
            pltpu.SemaphoreType.DMA((2, count)),
        ]
    if resids:
        scratch += [
            pltpu.VMEM((GROUPS, rows, count // GROUPS * span), jnp.float32),
            pltpu.SemaphoreType.DMA((GROUPS,)),
        ]
    return pl.pallas_call(
        functools.partial(fit_kernel, plan, fits, resids, ends, edges),
        in_specs=[hbm] * 4 + [loose] * len(halos or ()),
        out_specs=[hbm] * (2 * fits) + [loose] * (GROUPS * resids + 2 * edges),
        out_shape=[wide] * (2 * fits) + [part] * (GROUPS * resids) + [edge] * (2 * edges),
        scratch_shapes=scratch,
        compiler_params=pltpu.CompilerParams(vmem_limit_bytes=16 * MIB),
        cost_estimate=pl.CostEstimate(
            flops=count * 3 * rows * span * 256 * 4,
            bytes_accessed=count * rows * span * 4 * 4,
            transcendentals=0,
        ),
    )(*args)


def gram_kernel(add, spread, *refs):
    parts, refs = refs[:GROUPS], refs[GROUPS:]
    if add:
        so_far_ref, refs = refs[0], refs[1:]
    out_ref, stack_ref = refs
    mine = lax.axis_index("series")
    for k in range(GROUPS):
        at = pl.multiple_of((mine + GROUPS - k) % GROUPS * ROWS, ROWS)
        x = parts[k][...]
        a = x.astype(jnp.bfloat16)
        b = (x - a.astype(jnp.float32)).astype(jnp.bfloat16)
        stack_ref[pl.ds(at, ROWS)] = a
        stack_ref[pl.ds(64 + at, ROWS)] = b
    both = lax.dot_general(
        stack_ref[...],
        stack_ref[...],
        (((1,), (1,)), ((), ())),
        preferred_element_type=jnp.float32,
    )
    gram = both[:64] + both[64:]
    gram = gram + pltpu.roll(gram, 64, 1)
    low = lax.broadcasted_iota(jnp.int32, (8, LANES), 1) < 64
    for g in range(GROUPS):
        rows = jnp.where(low, gram[16 * g : 16 * g + 8], gram[16 * g + 8 : 16 * g + 16])
        if add:
            rows = rows + so_far_ref[g]
        if spread:
            for n in range(spread):
                out_ref[n, g] = rows
        else:
            out_ref[g] = rows


def gram_of(parts, so_far, spread):
    width = parts[0].shape[1]
    vmem = pl.BlockSpec(memory_space=pltpu.VMEM)
    args = list(parts) + ([] if so_far is None else [so_far])
    lead = (spread,) if spread else ()
    return pl.pallas_call(
        functools.partial(gram_kernel, so_far is not None, spread),
        in_specs=[vmem] * len(args),
        out_specs=vmem,
        out_shape=jax.ShapeDtypeStruct((*lead, GROUPS, 8, LANES), jnp.float32),
        scratch_shapes=[pltpu.VMEM((128, width), jnp.bfloat16)],
        compiler_params=pltpu.CompilerParams(vmem_limit_bytes=12 * MIB),
        cost_estimate=pl.CostEstimate(
            flops=128 * 128 * width * 2, bytes_accessed=64 * width * 4, transcendentals=0
        ),
    )(*args)


def packed(rows):
    return jnp.concatenate([rows[:8], rows[8:]], axis=1)


def exchanged(pieces):
    parts = [pieces[0]]
    for k in (2, 1, 3):
        pairs = [(s, (s + k) % GROUPS) for s in range(GROUPS)]
        parts.append(lax.ppermute(pieces[k], "series", pairs))
    return [parts[0], parts[2], parts[1], parts[3]]


def shards(taps, signal, valid_start, valid_end):
    rows, width = signal.shape
    devices = lax.axis_size(TIME)
    taps = jnp.asarray(taps, jnp.bfloat16)
    mine = lax.axis_index("series")
    unit = width // 32
    early, mid = (2 * unit, 3 * unit, GROUPS), (14 * unit, 4 * unit, GROUPS)
    late, whole = (30 * unit, unit, GROUPS), (0, 4 * unit, 8)

    def fit(plan, fits, resids, halos=None, edges=False):
        return fit_steps(plan, valid_start, valid_end, signal, taps, fits, resids, halos, edges)

    first = lax.dynamic_slice_in_dim(valid_start, mine * rows, rows)[:, None]
    last = lax.dynamic_slice_in_dim(valid_end, mine * rows, rows)[:, None]
    shared = jnp.minimum(last, valid_end[None, :]) - jnp.maximum(first, valid_start[None, :])
    shared = packed(shared.astype(jnp.float32))

    *pieces, near, far = fit(early, False, True, edges=True)
    parts = exchanged(pieces)
    parts_mid = exchanged(fit(mid, False, True))
    near = lax.ppermute(near, TIME, [(t, t ^ 1) for t in range(devices)])
    pairs = [(t, t + 1) for t in range(1, devices - 1, 2)]
    far = lax.ppermute(far, TIME, pairs + [(b, a) for a, b in pairs])
    halos = (near, far)
    gram = gram_of(parts, None, None)
    parts = exchanged(fit(late, False, True, halos))
    gram = gram_of(parts_mid, gram, None)
    copies = gram_of(parts, gram, devices)
    copies = copies.reshape(devices * GROUPS, 8, LANES)
    copies = lax.all_to_all(copies, (*TIME, "series"), 0, 0, tiled=True)
    smooth, slope = fit(whole, True, False, halos)
    cov = jnp.sum(copies, axis=0) / shared
    return smooth, slope, jnp.concatenate([cov[:, :64], cov[:, 64:]], axis=0)


def solution(mesh):
    split = Mesh(mesh.devices.reshape(4, 4, 2, GROUPS), (*TIME, "series"))
    return jax.shard_map(
        functools.partial(shards, filter_matrix()),
        mesh=split,
        in_specs=(P("series", TIME), P(), P()),
        out_specs=(P("series", TIME), P("series", TIME), P("series", None)),
        check_vma=False,
    )
```

```python
import functools

import jax
import jax.numpy as jnp
import numpy as np
from jax import lax
from jax.experimental import pallas as pl
from jax.experimental.pallas import tpu as pltpu
from jax.sharding import Mesh
from jax.sharding import PartitionSpec as P


HALF = 16
TAPS = 2 * HALF + 1
ROWS = 16
GROUPS = 4
LANES = 128
TIME = ("y", "z", "core")
MIB = 1 << 20

SECOND = float(sum(j * j for j in range(-HALF, HALF + 1)))
CENTRE_SQ = SECOND / TAPS
FOURTH = float(sum((j * j - CENTRE_SQ) ** 2 for j in range(-HALF, HALF + 1)))
SMOOTH_SCALE = 2048.0 / 2387.0
SLOPE_SCALE = HALF * 16.0 / SECOND


def filter_matrix():
    place = np.concatenate([np.arange(128), np.arange(128, 192), np.arange(-64, 0)])
    j = place[:, None] - np.arange(LANES)[None, :]
    near = np.abs(j) <= HALF
    smooth = np.where(near, (163 - j * j) / 2048.0, 0.0)
    slope = np.where(near, j / 16.0, 0.0)
    return np.concatenate([smooth, slope], axis=1).astype(np.float32)


def thirds(x):
    a = x.astype(jnp.bfloat16)
    rest = x - a.astype(jnp.float32)
    b = rest.astype(jnp.bfloat16)
    c = (rest - b.astype(jnp.float32)).astype(jnp.bfloat16)
    return a, b, c


def aligned(start, size):
    return pl.ds(pl.multiple_of(start, LANES), size)


def fit_kernel(plan, fits, resids, ends, edges, *refs):
    base, span, count = plan
    blocks = span // LANES
    refs = list(refs)
    whole = ends and base == 0
    first_hbm, last_hbm, signal_ref, taps_hbm = refs[:4]
    refs = refs[4:]
    if ends:
        halo_refs, refs = refs[:2], refs[2:]
    if fits:
        fit_hbm, refs = refs[:2], refs[2:]
    if resids:
        outs, refs = refs[:GROUPS], refs[GROUPS:]
    if edges:
        edge_refs, refs = refs[:2], refs[2:]
    x_ref, taps_ref, first_ref, last_ref, in_sems, side_sems = refs[:6]
    refs = refs[6:]
    if fits:
        fit_ref, out_sems = refs[:2]
        refs = refs[2:]
    if resids:
        resid_ref = refs[0]

    width = signal_ref.shape[1]
    per = count // GROUPS
    half = count // 2
    mine = lax.axis_index("series")
    begin = lax.axis_index(TIME) * width
    core = lax.axis_index("core")

    def place(n):
        return LANES + n * span + (2 * LANES * (n // half) if ends and not whole else 0)

    def source(n):
        return lax.rem(base + n * span, width) if ends and not whole else base + n * span

    def fetch(n):
        return pltpu.make_async_copy(
            signal_ref.at[:, aligned(source(n), span)],
            x_ref.at[:, aligned(place(n), span)],
            in_sems.at[n],
        )

    middle = place(half)
    tail = place(count - 1) + span
    after = (base + count * span) % width
    sides = [(first_hbm, first_ref), (last_hbm, last_ref), (taps_hbm, taps_ref)]
    if not whole:
        sides += [
            (signal_ref.at[:, pl.ds(base - LANES, LANES)], x_ref.at[:, pl.ds(0, LANES)]),
            (signal_ref.at[:, pl.ds(after, LANES)], x_ref.at[:, pl.ds(tail, LANES)]),
        ]
    if ends:
        at_left, at_right = (0, tail) if whole else (middle - LANES, middle - 2 * LANES)
        across = core * (at_left - at_right)
        sides += [
            (halo_refs[0], x_ref.at[:, aligned(at_right + across, LANES)]),
            (halo_refs[1], x_ref.at[:, aligned(at_left - across, LANES)]),
        ]
    needed = len(sides)
    if edges:
        sides += [
            (signal_ref.at[:, aligned((1 - core) * (width - LANES), LANES)], edge_refs[0]),
            (signal_ref.at[:, aligned(core * (width - LANES), LANES)], edge_refs[1]),
        ]
    sides = [pltpu.make_async_copy(a, b, side_sems.at[n]) for n, (a, b) in enumerate(sides)]
    for copy in sides[:needed]:
        copy.start()
    for n in range(count):
        fetch(n).start()
    for copy in sides[needed:]:
        copy.start()

    def give(n, kind):
        return pltpu.make_async_copy(
            fit_ref.at[kind, :, aligned(n * span, span)],
            fit_hbm[kind].at[:, aligned(source(n), span)],
            out_sems.at[kind, n],
        )

    lane = lax.broadcasted_iota(jnp.int32, (ROWS, LANES), 1)
    low = lane < 64
    height = ROWS * blocks

    for copy in sides[:needed]:
        copy.wait()
    fetch(0).wait()

    row = lax.broadcasted_iota(jnp.int32, (ROWS, LANES), 0)
    first = jnp.zeros((ROWS, LANES), jnp.int32)
    last = jnp.zeros((ROWS, LANES), jnp.int32)
    for r in range(ROWS):
        first = jnp.where(row == r, first_ref[mine * ROWS + r], first)
        last = jnp.where(row == r, last_ref[mine * ROWS + r], last)

    def body(n, carry):
        at = place(n)
        k = (n // per + GROUPS - mine) % GROUPS
        mark = begin + source(n)
        out_at = n * span
        piece_at = n % per * span

        @pl.when(n + 1 < count)
        def _():
            fetch(n + 1).wait()

        x = x_ref[:, aligned(at - LANES, span + 2 * LANES)]
        parts = thirds(x)

        def cut(m, b):
            return parts[m][:, b * LANES : (b + 1) * LANES]

        rows = [
            jnp.concatenate(
                [cut(m, b + 1), jnp.where(low, cut(m, b + 2), cut(m, b))], axis=1
            )
            for m in range(3)
            for b in range(blocks)
        ]
        fit = jnp.dot(
            jnp.concatenate(rows, axis=0), taps_ref[...], preferred_element_type=jnp.float32
        )
        fit = fit[:height] + (fit[height : 2 * height] + fit[2 * height :])
        since = first - mark
        until = last - mark
        for b in range(blocks):
            part = fit[b * ROWS : (b + 1) * ROWS]
            moment = lane + b * LANES
            inside = (moment >= since) & (moment < until)
            smooth = part[:, :LANES] * SMOOTH_SCALE
            if fits:
                to = aligned(out_at + b * LANES, LANES)
                fit_ref[0, :, to] = jnp.where(inside, smooth, 0.0)
                fit_ref[1, :, to] = jnp.where(inside, part[:, LANES:] * SLOPE_SCALE, 0.0)
            if resids:
                resid = x[:, (b + 1) * LANES : (b + 2) * LANES] - smooth
                resid_ref[k, :, aligned(piece_at + b * LANES, LANES)] = jnp.where(inside, resid, 0.0)

        def starts_here(a):
            return (a > mark - HALF) & (a < mark + span)

        def stops_here(z):
            return (z > mark) & (z < mark + span + HALF)

        holds = False
        for r in range(ROWS):
            holds = holds | starts_here(first_ref[mine * ROWS + r])
            holds = holds | stops_here(last_ref[mine * ROWS + r])

        @pl.when(holds)
        def _():
            def mend(r, left, centre, side):
                b = (left + LANES) // LANES - 1
                v = x_ref[:, aligned(at + b * LANES, 2 * LANES)]
                j = lax.broadcasted_iota(jnp.int32, (ROWS, 2 * LANES), 1) + (b * LANES - centre)
                w = jnp.where((j >= -HALF) & (j <= HALF), v, 0.0)
                f = jnp.clip(j, -HALF, HALF).astype(jnp.float32)
                level = jnp.sum(w, axis=1, keepdims=True) * (1.0 / TAPS)
                tilt = jnp.sum(w * f, axis=1, keepdims=True) * (1.0 / SECOND)
                curve = f * f - CENTRE_SQ
                bend = jnp.sum(w * curve, axis=1, keepdims=True) * (1.0 / FOURTH)
                smooth = level + tilt * f + bend * curve
                slope = HALF * (tilt + 2.0 * f * bend)
                held = (j * side >= 1) & (j * side <= HALF)
                for h in range(2):

                    @pl.when((b + h >= 0) & (b + h < blocks))
                    def _():
                        part = slice(h * LANES, (h + 1) * LANES)
                        to = held[:, part] & (row == r)
                        if fits:
                            at_fit = aligned(out_at + (b + h) * LANES, LANES)
                            fit_ref[0, :, at_fit] = jnp.where(
                                to, smooth[:, part], fit_ref[0, :, at_fit]
                            )
                            fit_ref[1, :, at_fit] = jnp.where(
                                to, slope[:, part], fit_ref[1, :, at_fit]
                            )
                        if resids:
                            at_piece = aligned(piece_at + (b + h) * LANES, LANES)
                            resid_ref[k, :, at_piece] = jnp.where(
                                to, v[:, part] - smooth[:, part], resid_ref[k, :, at_piece]
                            )

            def series(r, carry):
                a = first_ref[mine * ROWS + r]
                z = last_ref[mine * ROWS + r]

                @pl.when(starts_here(a))
                def _():
                    mend(r, a - mark, a - mark + HALF, -1)

                @pl.when(stops_here(z))
                def _():
                    mend(r, z - mark - TAPS, z - mark - HALF - 1, 1)

                return carry

            lax.fori_loop(0, ROWS, series, 0)

        if fits:
            give(n, 0).start()
            give(n, 1).start()
        return carry

    lax.fori_loop(0, count, body, 0)
    for copy in sides[needed:]:
        copy.wait()
    if resids:
        for kk in range(GROUPS):
            outs[kk][...] = resid_ref[kk]
    if fits:
        for n in range(count):
            give(n, 0).wait()
            give(n, 1).wait()


def fit_steps(plan, first, last, signal, taps, fits, resids, halos, edges):
    base, span, count = plan
    rows, width = signal.shape
    ends = halos is not None
    margins = 4 if ends and base else 2
    if not fits:
        taps = taps[:, :LANES]
    hbm = pl.BlockSpec(memory_space=pltpu.HBM)
    vmem = pl.BlockSpec(memory_space=pltpu.VMEM)
    loose = pl.BlockSpec(memory_space=pl.ANY)
    args = [pltpu.with_memory_space_constraint(a, pltpu.HBM) for a in (first, last, signal, taps)]
    args += list(halos or ())
    wide = jax.ShapeDtypeStruct((rows, width), jnp.float32)
    part = jax.ShapeDtypeStruct((rows, count // GROUPS * span), jnp.float32)
    edge = jax.ShapeDtypeStruct((rows, LANES), jnp.float32)
    scratch = [
        pltpu.VMEM((rows, count * span + margins * LANES), jnp.float32),
        pltpu.VMEM(taps.shape, taps.dtype),
        pltpu.SMEM(first.shape, jnp.int32),
        pltpu.SMEM(last.shape, jnp.int32),
        pltpu.SemaphoreType.DMA((count,)),
        pltpu.SemaphoreType.DMA((7,)),
    ]
    if fits:
        scratch += [
            pltpu.VMEM((2, rows, count * span), jnp.float32),
            pltpu.SemaphoreType.DMA((2, count)),
        ]
    if resids:
        scratch += [pltpu.VMEM((GROUPS, rows, count // GROUPS * span), jnp.float32)]
    return pl.pallas_call(
        functools.partial(fit_kernel, plan, fits, resids, ends, edges),
        in_specs=[hbm] * 4 + [loose] * len(halos or ()),
        out_specs=[hbm] * (2 * fits) + [vmem] * (GROUPS * resids) + [loose] * (2 * edges),
        out_shape=[wide] * (2 * fits) + [part] * (GROUPS * resids) + [edge] * (2 * edges),
        scratch_shapes=scratch,
        compiler_params=pltpu.CompilerParams(vmem_limit_bytes=16 * MIB),
        cost_estimate=pl.CostEstimate(
            flops=count * 3 * rows * span * 256 * 4,
            bytes_accessed=count * rows * span * 4 * 4,
            transcendentals=0,
        ),
    )(*args)


def gram_kernel(add, spread, *refs):
    parts, refs = refs[:GROUPS], refs[GROUPS:]
    if add:
        so_far_ref, refs = refs[0], refs[1:]
    out_ref, stack_ref = refs
    mine = lax.axis_index("series")
    for k in range(GROUPS):
        at = pl.multiple_of((mine + GROUPS - k) % GROUPS * ROWS, ROWS)
        x = parts[k][...]
        a = x.astype(jnp.bfloat16)
        b = (x - a.astype(jnp.float32)).astype(jnp.bfloat16)
        stack_ref[pl.ds(at, ROWS)] = a
        stack_ref[pl.ds(64 + at, ROWS)] = b
    both = lax.dot_general(
        stack_ref[...],
        stack_ref[...],
        (((1,), (1,)), ((), ())),
        preferred_element_type=jnp.float32,
    )
    gram = both[:64] + both[64:]
    gram = gram + pltpu.roll(gram, 64, 1)
    low = lax.broadcasted_iota(jnp.int32, (8, LANES), 1) < 64
    for g in range(GROUPS):
        rows = jnp.where(low, gram[16 * g : 16 * g + 8], gram[16 * g + 8 : 16 * g + 16])
        if add:
            rows = rows + so_far_ref[g]
        if spread:
            for n in range(spread):
                out_ref[n, g] = rows
        else:
            out_ref[g] = rows


def gram_of(parts, so_far, spread):
    width = parts[0].shape[1]
    vmem = pl.BlockSpec(memory_space=pltpu.VMEM)
    args = list(parts) + ([] if so_far is None else [so_far])
    lead = (spread,) if spread else ()
    return pl.pallas_call(
        functools.partial(gram_kernel, so_far is not None, spread),
        in_specs=[vmem] * len(args),
        out_specs=vmem,
        out_shape=jax.ShapeDtypeStruct((*lead, GROUPS, 8, LANES), jnp.float32),
        scratch_shapes=[pltpu.VMEM((128, width), jnp.bfloat16)],
        compiler_params=pltpu.CompilerParams(vmem_limit_bytes=12 * MIB),
        cost_estimate=pl.CostEstimate(
            flops=128 * 128 * width * 2, bytes_accessed=64 * width * 4, transcendentals=0
        ),
    )(*args)


def packed(rows):
    return jnp.concatenate([rows[:8], rows[8:]], axis=1)


def exchanged(pieces):
    parts = [pieces[0]]
    for k in (2, 1, 3):
        pairs = [(s, (s + k) % GROUPS) for s in range(GROUPS)]
        parts.append(lax.ppermute(pieces[k], "series", pairs))
    return [parts[0], parts[2], parts[1], parts[3]]


def shards(taps, signal, valid_start, valid_end):
    rows, width = signal.shape
    devices = lax.axis_size(TIME)
    taps = jnp.asarray(taps, jnp.bfloat16)
    mine = lax.axis_index("series")
    unit = width // 32
    early, mid = (2 * unit, 3 * unit, GROUPS), (14 * unit, 4 * unit, GROUPS)
    late, whole = (30 * unit, unit, GROUPS), (0, 4 * unit, 8)

    def fit(plan, fits, resids, halos=None, edges=False):
        return fit_steps(plan, valid_start, valid_end, signal, taps, fits, resids, halos, edges)

    first = lax.dynamic_slice_in_dim(valid_start, mine * rows, rows)[:, None]
    last = lax.dynamic_slice_in_dim(valid_end, mine * rows, rows)[:, None]
    shared = jnp.minimum(last, valid_end[None, :]) - jnp.maximum(first, valid_start[None, :])
    shared = packed(shared.astype(jnp.float32))

    *pieces, near, far = fit(early, False, True, edges=True)
    parts = exchanged(pieces)
    parts_mid = exchanged(fit(mid, False, True))
    near = lax.ppermute(near, TIME, [(t, t ^ 1) for t in range(devices)])
    pairs = [(t, t + 1) for t in range(1, devices - 1, 2)]
    far = lax.ppermute(far, TIME, pairs + [(b, a) for a, b in pairs])
    halos = (near, far)
    gram = gram_of(parts, None, None)
    parts = exchanged(fit(late, False, True, halos))
    gram = gram_of(parts_mid, gram, None)
    copies = gram_of(parts, gram, devices)
    copies = copies.reshape(devices * GROUPS, 8, LANES)
    copies = lax.all_to_all(copies, (*TIME, "series"), 0, 0, tiled=True)
    smooth, slope = fit(whole, True, False, halos)
    cov = jnp.sum(copies, axis=0) / shared
    return smooth, slope, jnp.concatenate([cov[:, :64], cov[:, 64:]], axis=0)


def solution(mesh):
    split = Mesh(mesh.devices.reshape(4, 4, 2, GROUPS), (*TIME, "series"))
    return jax.shard_map(
        functools.partial(shards, filter_matrix()),
        mesh=split,
        in_specs=(P("series", TIME), P(), P()),
        out_specs=(P("series", TIME), P("series", TIME), P("series", None)),
        check_vma=False,
    )
```

```python
import functools

import jax
import jax.numpy as jnp
import numpy as np
from jax import lax
from jax.experimental import pallas as pl
from jax.experimental.pallas import tpu as pltpu
from jax.sharding import Mesh
from jax.sharding import PartitionSpec as P


HALF = 16
TAPS = 2 * HALF + 1
ROWS = 16
GROUPS = 4
LANES = 128
TIME = ("y", "z", "core")
MIB = 1 << 20

SECOND = float(sum(j * j for j in range(-HALF, HALF + 1)))
CENTRE_SQ = SECOND / TAPS
FOURTH = float(sum((j * j - CENTRE_SQ) ** 2 for j in range(-HALF, HALF + 1)))
SMOOTH_SCALE = 2048.0 / 2387.0
SLOPE_SCALE = HALF * 16.0 / SECOND


def filter_matrix():
    place = np.concatenate([np.arange(128), np.arange(128, 192), np.arange(-64, 0)])
    j = place[:, None] - np.arange(LANES)[None, :]
    near = np.abs(j) <= HALF
    smooth = np.where(near, (163 - j * j) / 2048.0, 0.0)
    slope = np.where(near, j / 16.0, 0.0)
    return np.concatenate([smooth, slope], axis=1).astype(np.float32)


def thirds(x):
    a = x.astype(jnp.bfloat16)
    rest = x - a.astype(jnp.float32)
    b = rest.astype(jnp.bfloat16)
    c = (rest - b.astype(jnp.float32)).astype(jnp.bfloat16)
    return a, b, c


def aligned(start, size):
    return pl.ds(pl.multiple_of(start, LANES), size)


def fit_kernel(plan, fits, resids, ends, edges, *refs):
    base, span, count = plan
    blocks = span // LANES
    refs = list(refs)
    whole = ends and base == 0
    first_hbm, last_hbm, signal_ref, taps_hbm = refs[:4]
    refs = refs[4:]
    if ends:
        halo_refs, refs = refs[:2], refs[2:]
    if fits:
        fit_hbm, refs = refs[:2], refs[2:]
    if resids:
        outs, refs = refs[:GROUPS], refs[GROUPS:]
    if edges:
        edge_refs, refs = refs[:2], refs[2:]
    x_ref, taps_ref, first_ref, last_ref, in_sems, side_sems = refs[:6]
    refs = refs[6:]
    if fits:
        fit_ref, out_sems = refs[:2]
        refs = refs[2:]
    if resids:
        resid_ref = refs[0]

    width = signal_ref.shape[1]
    per = count // GROUPS
    half = count // 2
    mine = lax.axis_index("series")
    begin = lax.axis_index(TIME) * width
    core = lax.axis_index("core")

    def place(n):
        return LANES + n * span + (2 * LANES * (n // half) if ends and not whole else 0)

    def source(n):
        return lax.rem(base + n * span, width) if ends and not whole else base + n * span

    def fetch(n):
        return pltpu.make_async_copy(
            signal_ref.at[:, aligned(source(n), span)],
            x_ref.at[:, aligned(place(n), span)],
            in_sems.at[n],
        )

    middle = place(half)
    tail = place(count - 1) + span
    after = (base + count * span) % width
    sides = [(first_hbm, first_ref), (last_hbm, last_ref), (taps_hbm, taps_ref)]
    if not whole:
        sides += [
            (signal_ref.at[:, pl.ds(base - LANES, LANES)], x_ref.at[:, pl.ds(0, LANES)]),
            (signal_ref.at[:, pl.ds(after, LANES)], x_ref.at[:, pl.ds(tail, LANES)]),
        ]
    if ends:
        at_left, at_right = (0, tail) if whole else (middle - LANES, middle - 2 * LANES)
        across = core * (at_left - at_right)
        sides += [
            (halo_refs[0], x_ref.at[:, aligned(at_right + across, LANES)]),
            (halo_refs[1], x_ref.at[:, aligned(at_left - across, LANES)]),
        ]
    needed = len(sides)
    if edges:
        sides += [
            (signal_ref.at[:, aligned((1 - core) * (width - LANES), LANES)], edge_refs[0]),
            (signal_ref.at[:, aligned(core * (width - LANES), LANES)], edge_refs[1]),
        ]
    sides = [pltpu.make_async_copy(a, b, side_sems.at[n]) for n, (a, b) in enumerate(sides)]
    for copy in sides[:needed]:
        copy.start()
    for n in range(count):
        fetch(n).start()
    for copy in sides[needed:]:
        copy.start()

    def give(n, kind):
        return pltpu.make_async_copy(
            fit_ref.at[kind, :, aligned(n * span, span)],
            fit_hbm[kind].at[:, aligned(source(n), span)],
            out_sems.at[kind, n],
        )

    lane = lax.broadcasted_iota(jnp.int32, (ROWS, LANES), 1)
    low = lane < 64
    height = ROWS * blocks

    for copy in sides[:needed]:
        copy.wait()
    fetch(0).wait()

    row = lax.broadcasted_iota(jnp.int32, (ROWS, LANES), 0)
    first = jnp.zeros((ROWS, LANES), jnp.int32)
    last = jnp.zeros((ROWS, LANES), jnp.int32)
    for r in range(ROWS):
        first = jnp.where(row == r, first_ref[mine * ROWS + r], first)
        last = jnp.where(row == r, last_ref[mine * ROWS + r], last)

    def body(n, carry):
        at = place(n)
        k = (n // per + GROUPS - mine) % GROUPS
        mark = begin + source(n)
        out_at = n * span
        piece_at = n % per * span

        @pl.when(n + 1 < count)
        def _():
            fetch(n + 1).wait()

        x = x_ref[:, aligned(at - LANES, span + 2 * LANES)]
        parts = thirds(x)

        def cut(m, b):
            return parts[m][:, b * LANES : (b + 1) * LANES]

        rows = [
            jnp.concatenate(
                [cut(m, b + 1), jnp.where(low, cut(m, b + 2), cut(m, b))], axis=1
            )
            for m in range(3)
            for b in range(blocks)
        ]
        fit = jnp.dot(
            jnp.concatenate(rows, axis=0), taps_ref[...], preferred_element_type=jnp.float32
        )
        fit = fit[:height] + (fit[height : 2 * height] + fit[2 * height :])
        since = first - mark
        until = last - mark
        for b in range(blocks):
            part = fit[b * ROWS : (b + 1) * ROWS]
            moment = lane + b * LANES
            inside = (moment >= since) & (moment < until)
            smooth = part[:, :LANES] * SMOOTH_SCALE
            if fits:
                to = aligned(out_at + b * LANES, LANES)
                fit_ref[0, :, to] = jnp.where(inside, smooth, 0.0)
                fit_ref[1, :, to] = jnp.where(inside, part[:, LANES:] * SLOPE_SCALE, 0.0)
            if resids:
                resid = x[:, (b + 1) * LANES : (b + 2) * LANES] - smooth
                resid_ref[k, :, aligned(piece_at + b * LANES, LANES)] = jnp.where(inside, resid, 0.0)

        def starts_here(a):
            return (a > mark - HALF) & (a < mark + span)

        def stops_here(z):
            return (z > mark) & (z < mark + span + HALF)

        holds = False
        for r in range(ROWS):
            holds = holds | starts_here(first_ref[mine * ROWS + r])
            holds = holds | stops_here(last_ref[mine * ROWS + r])

        @pl.when(holds)
        def _():
            def mend(r, left, centre, side):
                b = (left + LANES) // LANES - 1
                v = x_ref[:, aligned(at + b * LANES, 2 * LANES)]
                j = lax.broadcasted_iota(jnp.int32, (ROWS, 2 * LANES), 1) + (b * LANES - centre)
                w = jnp.where((j >= -HALF) & (j <= HALF), v, 0.0)
                f = jnp.clip(j, -HALF, HALF).astype(jnp.float32)
                level = jnp.sum(w, axis=1, keepdims=True) * (1.0 / TAPS)
                tilt = jnp.sum(w * f, axis=1, keepdims=True) * (1.0 / SECOND)
                curve = f * f - CENTRE_SQ
                bend = jnp.sum(w * curve, axis=1, keepdims=True) * (1.0 / FOURTH)
                smooth = level + tilt * f + bend * curve
                slope = HALF * (tilt + 2.0 * f * bend)
                held = (j * side >= 1) & (j * side <= HALF)
                for h in range(2):

                    @pl.when((b + h >= 0) & (b + h < blocks))
                    def _():
                        part = slice(h * LANES, (h + 1) * LANES)
                        to = held[:, part] & (row == r)
                        if fits:
                            at_fit = aligned(out_at + (b + h) * LANES, LANES)
                            fit_ref[0, :, at_fit] = jnp.where(
                                to, smooth[:, part], fit_ref[0, :, at_fit]
                            )
                            fit_ref[1, :, at_fit] = jnp.where(
                                to, slope[:, part], fit_ref[1, :, at_fit]
                            )
                        if resids:
                            at_piece = aligned(piece_at + (b + h) * LANES, LANES)
                            resid_ref[k, :, at_piece] = jnp.where(
                                to, v[:, part] - smooth[:, part], resid_ref[k, :, at_piece]
                            )

            def series(r, carry):
                a = first_ref[mine * ROWS + r]
                z = last_ref[mine * ROWS + r]

                @pl.when(starts_here(a))
                def _():
                    mend(r, a - mark, a - mark + HALF, -1)

                @pl.when(stops_here(z))
                def _():
                    mend(r, z - mark - TAPS, z - mark - HALF - 1, 1)

                return carry

            lax.fori_loop(0, ROWS, series, 0)

        if fits:
            give(n, 0).start()
            give(n, 1).start()
        return carry

    lax.fori_loop(0, count, body, 0)
    for copy in sides[needed:]:
        copy.wait()
    if resids:
        for kk in range(GROUPS):
            outs[kk][...] = resid_ref[kk]
    if fits:
        for n in range(count):
            give(n, 0).wait()
            give(n, 1).wait()


def fit_steps(plan, first, last, signal, taps, fits, resids, halos, edges):
    base, span, count = plan
    rows, width = signal.shape
    ends = halos is not None
    margins = 4 if ends and base else 2
    if not fits:
        taps = taps[:, :LANES]
    hbm = pl.BlockSpec(memory_space=pltpu.HBM)
    vmem = pl.BlockSpec(memory_space=pltpu.VMEM)
    loose = pl.BlockSpec(memory_space=pl.ANY)
    args = [pltpu.with_memory_space_constraint(a, pltpu.HBM) for a in (first, last, signal, taps)]
    args += list(halos or ())
    wide = jax.ShapeDtypeStruct((rows, width), jnp.float32)
    part = jax.ShapeDtypeStruct((rows, count // GROUPS * span), jnp.float32)
    edge = jax.ShapeDtypeStruct((rows, LANES), jnp.float32)
    scratch = [
        pltpu.VMEM((rows, count * span + margins * LANES), jnp.float32),
        pltpu.VMEM(taps.shape, taps.dtype),
        pltpu.SMEM(first.shape, jnp.int32),
        pltpu.SMEM(last.shape, jnp.int32),
        pltpu.SemaphoreType.DMA((count,)),
        pltpu.SemaphoreType.DMA((7,)),
    ]
    if fits:
        scratch += [
            pltpu.VMEM((2, rows, count * span), jnp.float32),
            pltpu.SemaphoreType.DMA((2, count)),
        ]
    if resids:
        scratch += [pltpu.VMEM((GROUPS, rows, count // GROUPS * span), jnp.float32)]
    return pl.pallas_call(
        functools.partial(fit_kernel, plan, fits, resids, ends, edges),
        in_specs=[hbm] * 4 + [loose] * len(halos or ()),
        out_specs=[hbm] * (2 * fits) + [vmem] * (GROUPS * resids) + [loose] * (2 * edges),
        out_shape=[wide] * (2 * fits) + [part] * (GROUPS * resids) + [edge] * (2 * edges),
        scratch_shapes=scratch,
        compiler_params=pltpu.CompilerParams(vmem_limit_bytes=16 * MIB),
        cost_estimate=pl.CostEstimate(
            flops=count * 3 * rows * span * 256 * 4,
            bytes_accessed=count * rows * span * 4 * 4,
            transcendentals=0,
        ),
    )(*args)


def gram_kernel(add, spread, *refs):
    parts, refs = refs[:GROUPS], refs[GROUPS:]
    if add:
        so_far_ref, refs = refs[0], refs[1:]
    out_ref, stack_ref = refs
    mine = lax.axis_index("series")
    for k in range(GROUPS):
        at = pl.multiple_of((mine + GROUPS - k) % GROUPS * ROWS, ROWS)
        x = parts[k][...]
        a = x.astype(jnp.bfloat16)
        b = (x - a.astype(jnp.float32)).astype(jnp.bfloat16)
        stack_ref[pl.ds(at, ROWS)] = a
        stack_ref[pl.ds(64 + at, ROWS)] = b
    both = lax.dot_general(
        stack_ref[...],
        stack_ref[...],
        (((1,), (1,)), ((), ())),
        preferred_element_type=jnp.float32,
    )
    gram = both[:64] + both[64:]
    gram = gram + pltpu.roll(gram, 64, 1)
    low = lax.broadcasted_iota(jnp.int32, (8, LANES), 1) < 64
    for g in range(GROUPS):
        rows = jnp.where(low, gram[16 * g : 16 * g + 8], gram[16 * g + 8 : 16 * g + 16])
        if add:
            rows = rows + so_far_ref[g]
        if spread:
            for n in range(spread):
                out_ref[n, g] = rows
        else:
            out_ref[g] = rows


def gram_of(parts, so_far, spread):
    width = parts[0].shape[1]
    vmem = pl.BlockSpec(memory_space=pltpu.VMEM)
    args = list(parts) + ([] if so_far is None else [so_far])
    lead = (spread,) if spread else ()
    return pl.pallas_call(
        functools.partial(gram_kernel, so_far is not None, spread),
        in_specs=[vmem] * len(args),
        out_specs=vmem,
        out_shape=jax.ShapeDtypeStruct((*lead, GROUPS, 8, LANES), jnp.float32),
        scratch_shapes=[pltpu.VMEM((128, width), jnp.bfloat16)],
        compiler_params=pltpu.CompilerParams(vmem_limit_bytes=12 * MIB),
        cost_estimate=pl.CostEstimate(
            flops=128 * 128 * width * 2, bytes_accessed=64 * width * 4, transcendentals=0
        ),
    )(*args)


def packed(rows):
    return jnp.concatenate([rows[:8], rows[8:]], axis=1)


def exchanged(pieces):
    parts = [pieces[0]]
    for k in (2, 1, 3):
        pairs = [(s, (s + k) % GROUPS) for s in range(GROUPS)]
        parts.append(lax.ppermute(pieces[k], "series", pairs))
    return [parts[0], parts[2], parts[1], parts[3]]


def shards(taps, signal, valid_start, valid_end):
    rows, width = signal.shape
    devices = lax.axis_size(TIME)
    taps = jnp.asarray(taps, jnp.bfloat16)
    mine = lax.axis_index("series")
    unit = width // 32
    early, mid = (2 * unit, 4 * unit, GROUPS), (18 * unit, 3 * unit, GROUPS)
    late, whole = (30 * unit, unit, GROUPS), (0, 4 * unit, 8)

    def fit(plan, fits, resids, halos=None, edges=False):
        return fit_steps(plan, valid_start, valid_end, signal, taps, fits, resids, halos, edges)

    first = lax.dynamic_slice_in_dim(valid_start, mine * rows, rows)[:, None]
    last = lax.dynamic_slice_in_dim(valid_end, mine * rows, rows)[:, None]
    shared = jnp.minimum(last, valid_end[None, :])
    shared = shared - jnp.maximum(first, valid_start[None, :])
    shared = packed(shared.astype(jnp.float32))

    *pieces, near, far = fit(early, False, True, edges=True)
    parts = exchanged(pieces)
    parts_mid = exchanged(fit(mid, False, True))
    near = lax.ppermute(near, TIME, [(t, t ^ 1) for t in range(devices)])
    pairs = [(t, t + 1) for t in range(1, devices - 1, 2)]
    far = lax.ppermute(far, TIME, pairs + [(b, a) for a, b in pairs])
    halos = (near, far)
    gram = gram_of(parts, None, None)
    parts = exchanged(fit(late, False, True, halos))
    gram = gram_of(parts_mid, gram, None)
    copies = gram_of(parts, gram, devices)
    copies = copies.reshape(devices * GROUPS, 8, LANES)
    copies = lax.all_to_all(copies, (*TIME, "series"), 0, 0, tiled=True)
    smooth, slope = fit(whole, True, False, halos)
    cov = jnp.sum(copies, axis=0) / shared
    return smooth, slope, jnp.concatenate([cov[:, :64], cov[:, 64:]], axis=0)


def solution(mesh):
    split = Mesh(mesh.devices.reshape(4, 4, 2, GROUPS), (*TIME, "series"))
    return jax.shard_map(
        functools.partial(shards, filter_matrix()),
        mesh=split,
        in_specs=(P("series", TIME), P(), P()),
        out_specs=(P("series", TIME), P("series", TIME), P("series", None)),
        check_vma=False,
    )
```

```python
import functools

import jax
import jax.numpy as jnp
import numpy as np
from jax import lax
from jax.experimental import pallas as pl
from jax.experimental.pallas import tpu as pltpu
from jax.sharding import Mesh
from jax.sharding import PartitionSpec as P


HALF = 16
TAPS = 2 * HALF + 1
ROWS = 16
GROUPS = 4
LANES = 128
TIME = ("y", "z", "core")
MIB = 1 << 20

SECOND = float(sum(j * j for j in range(-HALF, HALF + 1)))
CENTRE_SQ = SECOND / TAPS
FOURTH = float(sum((j * j - CENTRE_SQ) ** 2 for j in range(-HALF, HALF + 1)))
SMOOTH_SCALE = 2048.0 / 2387.0
SLOPE_SCALE = HALF * 16.0 / SECOND


def filter_matrix():
    place = np.concatenate([np.arange(128), np.arange(128, 192), np.arange(-64, 0)])
    j = place[:, None] - np.arange(LANES)[None, :]
    near = np.abs(j) <= HALF
    smooth = np.where(near, (163 - j * j) / 2048.0, 0.0)
    slope = np.where(near, j / 16.0, 0.0)
    return np.concatenate([smooth, slope], axis=1).astype(np.float32)


def thirds(x):
    a = x.astype(jnp.bfloat16)
    rest = x - a.astype(jnp.float32)
    b = rest.astype(jnp.bfloat16)
    c = (rest - b.astype(jnp.float32)).astype(jnp.bfloat16)
    return a, b, c


def aligned(start, size):
    return pl.ds(pl.multiple_of(start, LANES), size)


def ends_of(group, first_ref, last_ref):
    row = lax.broadcasted_iota(jnp.int32, (ROWS, LANES), 0)
    first = jnp.zeros((ROWS, LANES), jnp.int32)
    last = jnp.zeros((ROWS, LANES), jnp.int32)
    for r in range(ROWS):
        first = jnp.where(row == r, first_ref[group * ROWS + r], first)
        last = jnp.where(row == r, last_ref[group * ROWS + r], last)
    return first, last


def fit_span(span, mark, group, samples, tables, to_fit, to_resid):
    blocks = span // LANES
    height = ROWS * blocks
    x_ref, at = samples
    taps_ref, first_ref, last_ref, first, last = tables
    if to_fit:
        fit_ref, out_at = to_fit
    if to_resid:
        resid_ref, k, piece_at = to_resid
    lane = lax.broadcasted_iota(jnp.int32, (ROWS, LANES), 1)
    row = lax.broadcasted_iota(jnp.int32, (ROWS, LANES), 0)
    low = lane < 64

    x = x_ref[:, aligned(at - LANES, span + 2 * LANES)]
    parts = thirds(x)

    def cut(m, b):
        return parts[m][:, b * LANES : (b + 1) * LANES]

    rows = [
        jnp.concatenate([cut(m, b + 1), jnp.where(low, cut(m, b + 2), cut(m, b))], axis=1)
        for m in range(3)
        for b in range(blocks)
    ]
    fit = jnp.dot(
        jnp.concatenate(rows, axis=0), taps_ref[...], preferred_element_type=jnp.float32
    )
    fit = fit[:height] + (fit[height : 2 * height] + fit[2 * height :])
    since = first - mark
    until = last - mark
    for b in range(blocks):
        part = fit[b * ROWS : (b + 1) * ROWS]
        moment = lane + b * LANES
        inside = (moment >= since) & (moment < until)
        smooth = part[:, :LANES] * SMOOTH_SCALE
        if to_fit:
            to = aligned(out_at + b * LANES, LANES)
            fit_ref[0, :, to] = jnp.where(inside, smooth, 0.0)
            fit_ref[1, :, to] = jnp.where(inside, part[:, LANES:] * SLOPE_SCALE, 0.0)
        if to_resid:
            resid = x[:, (b + 1) * LANES : (b + 2) * LANES] - smooth
            resid_ref[k, :, aligned(piece_at + b * LANES, LANES)] = jnp.where(inside, resid, 0.0)

    def starts_here(a):
        return (a > mark - HALF) & (a < mark + span)

    def stops_here(z):
        return (z > mark) & (z < mark + span + HALF)

    holds = False
    for r in range(ROWS):
        holds = holds | starts_here(first_ref[group * ROWS + r])
        holds = holds | stops_here(last_ref[group * ROWS + r])

    @pl.when(holds)
    def _():
        def mend(r, left, centre, side):
            b = (left + LANES) // LANES - 1
            v = x_ref[:, aligned(at + b * LANES, 2 * LANES)]
            j = lax.broadcasted_iota(jnp.int32, (ROWS, 2 * LANES), 1) + (b * LANES - centre)
            w = jnp.where((j >= -HALF) & (j <= HALF), v, 0.0)
            f = jnp.clip(j, -HALF, HALF).astype(jnp.float32)
            level = jnp.sum(w, axis=1, keepdims=True) * (1.0 / TAPS)
            tilt = jnp.sum(w * f, axis=1, keepdims=True) * (1.0 / SECOND)
            curve = f * f - CENTRE_SQ
            bend = jnp.sum(w * curve, axis=1, keepdims=True) * (1.0 / FOURTH)
            smooth = level + tilt * f + bend * curve
            slope = HALF * (tilt + 2.0 * f * bend)
            held = (j * side >= 1) & (j * side <= HALF)
            for h in range(2):

                @pl.when((b + h >= 0) & (b + h < blocks))
                def _():
                    part = slice(h * LANES, (h + 1) * LANES)
                    to = held[:, part] & (row == r)
                    if to_fit:
                        at_fit = aligned(out_at + (b + h) * LANES, LANES)
                        fit_ref[0, :, at_fit] = jnp.where(
                            to, smooth[:, part], fit_ref[0, :, at_fit]
                        )
                        fit_ref[1, :, at_fit] = jnp.where(to, slope[:, part], fit_ref[1, :, at_fit])
                    if to_resid:
                        at_piece = aligned(piece_at + (b + h) * LANES, LANES)
                        resid_ref[k, :, at_piece] = jnp.where(
                            to, v[:, part] - smooth[:, part], resid_ref[k, :, at_piece]
                        )

        def series(r, carry):
            a = first_ref[group * ROWS + r]
            z = last_ref[group * ROWS + r]

            @pl.when(starts_here(a))
            def _():
                mend(r, a - mark, a - mark + HALF, -1)

            @pl.when(stops_here(z))
            def _():
                mend(r, z - mark - TAPS, z - mark - HALF - 1, 1)

            return carry

        lax.fori_loop(0, ROWS, series, 0)


def cut_kernel(plan, signal_ref, *refs):
    base, span, _ = plan
    pieces, edges, sems = refs[:GROUPS], refs[GROUPS : GROUPS + 2], refs[-1]
    width = signal_ref.shape[1]
    mine = lax.axis_index("series")
    core = lax.axis_index("core")
    copies = [
        pltpu.make_async_copy(
            signal_ref.at[
                :, aligned(base - LANES + (mine + k) % GROUPS * span, span + 2 * LANES)
            ],
            pieces[k],
            sems.at[k],
        )
        for k in (2, 1, 3, 0)
    ]
    for n, start in enumerate(((1 - core) * (width - LANES), core * (width - LANES))):
        copies.append(
            pltpu.make_async_copy(
                signal_ref.at[:, aligned(start, LANES)], edges[n], sems.at[GROUPS + n]
            )
        )
    for copy in copies:
        copy.start()
    for copy in copies:
        copy.wait()


def cut_chunk(plan, signal):
    rows, _ = signal.shape
    part = jax.ShapeDtypeStruct((rows, plan[1] + 2 * LANES), jnp.float32)
    edge = jax.ShapeDtypeStruct((rows, LANES), jnp.float32)
    return pl.pallas_call(
        functools.partial(cut_kernel, plan),
        in_specs=[pl.BlockSpec(memory_space=pltpu.HBM)],
        out_specs=[pl.BlockSpec(memory_space=pltpu.VMEM)] * (GROUPS + 2),
        out_shape=[part] * GROUPS + [edge] * 2,
        scratch_shapes=[pltpu.SemaphoreType.DMA((GROUPS + 2,))],
        compiler_params=pltpu.CompilerParams(vmem_limit_bytes=8 * MIB),
        cost_estimate=pl.CostEstimate(
            flops=0, bytes_accessed=rows * plan[1] * 32, transcendentals=0
        ),
        name="cut_early",
    )(pltpu.with_memory_space_constraint(signal, pltpu.HBM))


def fit_kernel(plan, fits, resids, ends, *refs):
    base, span, count = plan
    refs = list(refs)
    whole = ends and base == 0
    first_hbm, last_hbm, signal_ref, taps_hbm = refs[:4]
    refs = refs[4:]
    if ends:
        halo_refs, refs = refs[:2], refs[2:]
    if fits:
        fit_hbm, refs = refs[:2], refs[2:]
    if resids:
        outs, refs = refs[:GROUPS], refs[GROUPS:]
    x_ref, taps_ref, first_ref, last_ref, in_sems, side_sems = refs[:6]
    refs = refs[6:]
    if fits:
        fit_ref, out_sems = refs[:2]
        refs = refs[2:]
    if resids:
        resid_ref = refs[0]

    width = signal_ref.shape[1]
    per = count // GROUPS
    half = count // 2
    mine = lax.axis_index("series")
    begin = lax.axis_index(TIME) * width
    core = lax.axis_index("core")

    def place(n):
        return LANES + n * span + (2 * LANES * (n // half) if ends and not whole else 0)

    def source(n):
        return lax.rem(base + n * span, width) if ends and not whole else base + n * span

    def fetch(n):
        return pltpu.make_async_copy(
            signal_ref.at[:, aligned(source(n), span)],
            x_ref.at[:, aligned(place(n), span)],
            in_sems.at[n],
        )

    middle = place(half)
    tail = place(count - 1) + span
    after = (base + count * span) % width
    sides = [(first_hbm, first_ref), (last_hbm, last_ref), (taps_hbm, taps_ref)]
    if not whole:
        sides += [
            (signal_ref.at[:, pl.ds(base - LANES, LANES)], x_ref.at[:, pl.ds(0, LANES)]),
            (signal_ref.at[:, pl.ds(after, LANES)], x_ref.at[:, pl.ds(tail, LANES)]),
        ]
    if ends:
        at_left, at_right = (0, tail) if whole else (middle - LANES, middle - 2 * LANES)
        across = core * (at_left - at_right)
        sides += [
            (halo_refs[0], x_ref.at[:, aligned(at_right + across, LANES)]),
            (halo_refs[1], x_ref.at[:, aligned(at_left - across, LANES)]),
        ]
    sides = [pltpu.make_async_copy(a, b, side_sems.at[n]) for n, (a, b) in enumerate(sides)]
    for copy in sides:
        copy.start()
    for n in range(count):
        fetch(n).start()

    def give(n, kind):
        return pltpu.make_async_copy(
            fit_ref.at[kind, :, aligned(n * span, span)],
            fit_hbm[kind].at[:, aligned(source(n), span)],
            out_sems.at[kind, n],
        )

    for copy in sides:
        copy.wait()
    fetch(0).wait()

    first, last = ends_of(mine, first_ref, last_ref)

    def body(n, carry):
        k = (n // per + GROUPS - mine) % GROUPS

        @pl.when(n + 1 < count)
        def _():
            fetch(n + 1).wait()

        fit_span(
            span,
            begin + source(n),
            mine,
            (x_ref, place(n)),
            (taps_ref, first_ref, last_ref, first, last),
            (fit_ref, n * span) if fits else None,
            (resid_ref, k, n % per * span) if resids else None,
        )
        if fits:
            give(n, 0).start()
            give(n, 1).start()
        return carry

    lax.fori_loop(0, count, body, 0)
    if resids:
        for kk in range(GROUPS):
            outs[kk][...] = resid_ref[kk]
    if fits:
        for n in range(count):
            give(n, 0).wait()
            give(n, 1).wait()


def fit_steps(plan, first, last, signal, taps, fits, resids, halos):
    base, span, count = plan
    rows, width = signal.shape
    ends = halos is not None
    margins = 4 if ends and base else 2
    if not fits:
        taps = taps[:, :LANES]
    hbm = pl.BlockSpec(memory_space=pltpu.HBM)
    vmem = pl.BlockSpec(memory_space=pltpu.VMEM)
    loose = pl.BlockSpec(memory_space=pl.ANY)
    args = [pltpu.with_memory_space_constraint(a, pltpu.HBM) for a in (first, last, signal, taps)]
    args += list(halos or ())
    wide = jax.ShapeDtypeStruct((rows, width), jnp.float32)
    part = jax.ShapeDtypeStruct((rows, count // GROUPS * span), jnp.float32)
    scratch = [
        pltpu.VMEM((rows, count * span + margins * LANES), jnp.float32),
        pltpu.VMEM(taps.shape, taps.dtype),
        pltpu.SMEM(first.shape, jnp.int32),
        pltpu.SMEM(last.shape, jnp.int32),
        pltpu.SemaphoreType.DMA((count,)),
        pltpu.SemaphoreType.DMA((7,)),
    ]
    if fits:
        scratch += [
            pltpu.VMEM((2, rows, count * span), jnp.float32),
            pltpu.SemaphoreType.DMA((2, count)),
        ]
    if resids:
        scratch += [pltpu.VMEM((GROUPS, rows, count // GROUPS * span), jnp.float32)]
    return pl.pallas_call(
        functools.partial(fit_kernel, plan, fits, resids, ends),
        in_specs=[hbm] * 4 + [loose] * len(halos or ()),
        out_specs=[hbm] * (2 * fits) + [vmem] * (GROUPS * resids),
        out_shape=[wide] * (2 * fits) + [part] * (GROUPS * resids),
        scratch_shapes=scratch,
        compiler_params=pltpu.CompilerParams(vmem_limit_bytes=16 * MIB),
        cost_estimate=pl.CostEstimate(
            flops=count * 3 * rows * span * 256 * 4,
            bytes_accessed=count * rows * span * 4 * 4,
            transcendentals=0,
        ),
    )(*args)


def stacked(stack_ref, group, x):
    at = pl.multiple_of(group * ROWS, ROWS)
    a = x.astype(jnp.bfloat16)
    stack_ref[pl.ds(at, ROWS)] = a
    stack_ref[pl.ds(64 + at, ROWS)] = (x - a.astype(jnp.float32)).astype(jnp.bfloat16)


def product(stack_ref, so_far_ref, spread, out_ref):
    both = lax.dot_general(
        stack_ref[...],
        stack_ref[...],
        (((1,), (1,)), ((), ())),
        preferred_element_type=jnp.float32,
    )
    gram = both[:64] + both[64:]
    gram = gram + pltpu.roll(gram, 64, 1)
    low = lax.broadcasted_iota(jnp.int32, (8, LANES), 1) < 64
    for g in range(GROUPS):
        rows = jnp.where(low, gram[16 * g : 16 * g + 8], gram[16 * g + 8 : 16 * g + 16])
        if so_far_ref is not None:
            rows = rows + so_far_ref[g]
        if spread:
            for n in range(spread):
                out_ref[n, g] = rows
        else:
            out_ref[g] = rows


def raw_gram_kernel(plan, width, first_hbm, last_hbm, taps_hbm, *refs):
    base, span, _ = plan
    pieces, refs = refs[:GROUPS], refs[GROUPS:]
    out_ref, x_ref, resid_ref, stack_ref, taps_ref, first_ref, last_ref, sems = refs
    mine = lax.axis_index("series")
    mark = lax.axis_index(TIME) * width + base + mine * span
    copies = [
        pltpu.make_async_copy(a, b, sems.at[n])
        for n, (a, b) in enumerate(
            ((first_hbm, first_ref), (last_hbm, last_ref), (taps_hbm, taps_ref))
        )
    ]
    for copy in copies:
        copy.start()
    for k in range(GROUPS):
        x_ref[k] = pieces[k][...]
    for copy in copies:
        copy.wait()

    def body(k, carry):
        group = (mine + GROUPS - k) % GROUPS
        first, last = ends_of(group, first_ref, last_ref)
        fit_span(
            span,
            mark,
            group,
            (x_ref.at[k], LANES),
            (taps_ref, first_ref, last_ref, first, last),
            None,
            (resid_ref, 0, 0),
        )
        stacked(stack_ref, group, resid_ref[0])
        return carry

    lax.fori_loop(0, GROUPS, body, 0)
    product(stack_ref, None, None, out_ref)


def raw_gram_of(plan, width, first, last, taps, pieces):
    _, span, _ = plan
    taps = taps[:, :LANES]
    hbm = pl.BlockSpec(memory_space=pltpu.HBM)
    vmem = pl.BlockSpec(memory_space=pltpu.VMEM)
    args = [pltpu.with_memory_space_constraint(a, pltpu.HBM) for a in (first, last, taps)]
    return pl.pallas_call(
        functools.partial(raw_gram_kernel, plan, width),
        in_specs=[hbm] * 3 + [vmem] * GROUPS,
        out_specs=vmem,
        out_shape=jax.ShapeDtypeStruct((GROUPS, 8, LANES), jnp.float32),
        scratch_shapes=[
            pltpu.VMEM((GROUPS, ROWS, span + 2 * LANES), jnp.float32),
            pltpu.VMEM((1, ROWS, span), jnp.float32),
            pltpu.VMEM((128, span), jnp.bfloat16),
            pltpu.VMEM(taps.shape, taps.dtype),
            pltpu.SMEM(first.shape, jnp.int32),
            pltpu.SMEM(last.shape, jnp.int32),
            pltpu.SemaphoreType.DMA((3,)),
        ],
        compiler_params=pltpu.CompilerParams(vmem_limit_bytes=16 * MIB),
        cost_estimate=pl.CostEstimate(
            flops=GROUPS * 3 * ROWS * span * 256 * 4,
            bytes_accessed=GROUPS * ROWS * span * 8,
            transcendentals=0,
        ),
    )(*args, *pieces)


def gram_kernel(add, spread, *refs):
    parts, refs = refs[:GROUPS], refs[GROUPS:]
    if add:
        so_far_ref, refs = refs[0], refs[1:]
    out_ref, stack_ref = refs
    mine = lax.axis_index("series")
    for k in range(GROUPS):
        stacked(stack_ref, (mine + GROUPS - k) % GROUPS, parts[k][...])
    product(stack_ref, so_far_ref if add else None, spread, out_ref)


def gram_of(parts, so_far, spread):
    width = parts[0].shape[1]
    vmem = pl.BlockSpec(memory_space=pltpu.VMEM)
    args = list(parts) + ([] if so_far is None else [so_far])
    lead = (spread,) if spread else ()
    return pl.pallas_call(
        functools.partial(gram_kernel, so_far is not None, spread),
        in_specs=[vmem] * len(args),
        out_specs=vmem,
        out_shape=jax.ShapeDtypeStruct((*lead, GROUPS, 8, LANES), jnp.float32),
        scratch_shapes=[pltpu.VMEM((128, width), jnp.bfloat16)],
        compiler_params=pltpu.CompilerParams(vmem_limit_bytes=12 * MIB),
        cost_estimate=pl.CostEstimate(
            flops=128 * 128 * width * 2, bytes_accessed=64 * width * 4, transcendentals=0
        ),
    )(*args)


def packed(rows):
    return jnp.concatenate([rows[:8], rows[8:]], axis=1)


def exchanged(pieces):
    parts = [pieces[0]]
    for k in (2, 1, 3):
        pairs = [(s, (s + k) % GROUPS) for s in range(GROUPS)]
        parts.append(lax.ppermute(pieces[k], "series", pairs))
    return [parts[0], parts[2], parts[1], parts[3]]


def shards(taps, signal, valid_start, valid_end):
    rows, width = signal.shape
    devices = lax.axis_size(TIME)
    taps = jnp.asarray(taps, jnp.bfloat16)
    mine = lax.axis_index("series")
    unit = width // 32
    early, mid = (2 * unit, 4 * unit, GROUPS), (18 * unit, 3 * unit, GROUPS)
    late, whole = (30 * unit, unit, GROUPS), (0, 4 * unit, 8)

    def fit(plan, fits, resids, halos=None):
        return fit_steps(plan, valid_start, valid_end, signal, taps, fits, resids, halos)

    first = lax.dynamic_slice_in_dim(valid_start, mine * rows, rows)[:, None]
    last = lax.dynamic_slice_in_dim(valid_end, mine * rows, rows)[:, None]
    shared = jnp.minimum(last, valid_end[None, :])
    shared = shared - jnp.maximum(first, valid_start[None, :])
    shared = packed(shared.astype(jnp.float32))

    *pieces, near, far = cut_chunk(early, signal)
    parts = exchanged(pieces)
    parts_mid = exchanged(fit(mid, False, True))
    near = lax.ppermute(near, TIME, [(t, t ^ 1) for t in range(devices)])
    pairs = [(t, t + 1) for t in range(1, devices - 1, 2)]
    far = lax.ppermute(far, TIME, pairs + [(b, a) for a, b in pairs])
    halos = (near, far)
    gram = raw_gram_of(early, width, valid_start, valid_end, taps, parts)
    parts = exchanged(fit(late, False, True, halos))
    gram = gram_of(parts_mid, gram, None)
    copies = gram_of(parts, gram, devices)
    copies = copies.reshape(devices * GROUPS, 8, LANES)
    copies = lax.all_to_all(copies, (*TIME, "series"), 0, 0, tiled=True)
    smooth, slope = fit(whole, True, False, halos)
    cov = jnp.sum(copies, axis=0) / shared
    return smooth, slope, jnp.concatenate([cov[:, :64], cov[:, 64:]], axis=0)


def solution(mesh):
    split = Mesh(mesh.devices.reshape(4, 4, 2, GROUPS), (*TIME, "series"))
    return jax.shard_map(
        functools.partial(shards, filter_matrix()),
        mesh=split,
        in_specs=(P("series", TIME), P(), P()),
        out_specs=(P("series", TIME), P("series", TIME), P("series", None)),
        check_vma=False,
    )
```

```python
import functools

import jax
import jax.numpy as jnp
import numpy as np
from jax import lax
from jax.experimental import pallas as pl
from jax.experimental.pallas import tpu as pltpu
from jax.sharding import Mesh
from jax.sharding import PartitionSpec as P


HALF = 16
TAPS = 2 * HALF + 1
ROWS = 16
GROUPS = 4
LANES = 128
TIME = ("y", "z", "core")
MIB = 1 << 20

SECOND = float(sum(j * j for j in range(-HALF, HALF + 1)))
CENTRE_SQ = SECOND / TAPS
FOURTH = float(sum((j * j - CENTRE_SQ) ** 2 for j in range(-HALF, HALF + 1)))
SMOOTH_SCALE = 2048.0 / 2387.0
SLOPE_SCALE = HALF * 16.0 / SECOND


def filter_matrix():
    place = np.concatenate([np.arange(128), np.arange(128, 192), np.arange(-64, 0)])
    j = place[:, None] - np.arange(LANES)[None, :]
    near = np.abs(j) <= HALF
    smooth = np.where(near, (163 - j * j) / 2048.0, 0.0)
    slope = np.where(near, j / 16.0, 0.0)
    return np.concatenate([smooth, slope], axis=1).astype(np.float32)


def thirds(x):
    a = x.astype(jnp.bfloat16)
    rest = x - a.astype(jnp.float32)
    b = rest.astype(jnp.bfloat16)
    c = (rest - b.astype(jnp.float32)).astype(jnp.bfloat16)
    return a, b, c


def aligned(start, size):
    return pl.ds(pl.multiple_of(start, LANES), size)


def ends_of(group, first_ref, last_ref):
    row = lax.broadcasted_iota(jnp.int32, (ROWS, LANES), 0)
    first = jnp.zeros((ROWS, LANES), jnp.int32)
    last = jnp.zeros((ROWS, LANES), jnp.int32)
    for r in range(ROWS):
        first = jnp.where(row == r, first_ref[group * ROWS + r], first)
        last = jnp.where(row == r, last_ref[group * ROWS + r], last)
    return first, last


def fit_span(span, mark, group, samples, tables, to_fit, to_resid):
    blocks = span // LANES
    height = ROWS * blocks
    x_ref, at = samples
    taps_ref, first_ref, last_ref, first, last = tables
    if to_fit:
        fit_ref, out_at = to_fit
    if to_resid:
        resid_ref, k, piece_at = to_resid
    lane = lax.broadcasted_iota(jnp.int32, (ROWS, LANES), 1)
    row = lax.broadcasted_iota(jnp.int32, (ROWS, LANES), 0)
    low = lane < 64

    x = x_ref[:, aligned(at - LANES, span + 2 * LANES)]
    parts = thirds(x)

    def cut(m, b):
        return parts[m][:, b * LANES : (b + 1) * LANES]

    rows = [
        jnp.concatenate([cut(m, b + 1), jnp.where(low, cut(m, b + 2), cut(m, b))], axis=1)
        for m in range(3)
        for b in range(blocks)
    ]
    fit = jnp.dot(
        jnp.concatenate(rows, axis=0), taps_ref[...], preferred_element_type=jnp.float32
    )
    fit = fit[:height] + (fit[height : 2 * height] + fit[2 * height :])
    since = first - mark
    until = last - mark
    for b in range(blocks):
        part = fit[b * ROWS : (b + 1) * ROWS]
        moment = lane + b * LANES
        inside = (moment >= since) & (moment < until)
        smooth = part[:, :LANES] * SMOOTH_SCALE
        if to_fit:
            to = aligned(out_at + b * LANES, LANES)
            fit_ref[0, :, to] = jnp.where(inside, smooth, 0.0)
            fit_ref[1, :, to] = jnp.where(inside, part[:, LANES:] * SLOPE_SCALE, 0.0)
        if to_resid:
            resid = x[:, (b + 1) * LANES : (b + 2) * LANES] - smooth
            resid_ref[k, :, aligned(piece_at + b * LANES, LANES)] = jnp.where(inside, resid, 0.0)

    def starts_here(a):
        return (a > mark - HALF) & (a < mark + span)

    def stops_here(z):
        return (z > mark) & (z < mark + span + HALF)

    holds = False
    for r in range(ROWS):
        holds = holds | starts_here(first_ref[group * ROWS + r])
        holds = holds | stops_here(last_ref[group * ROWS + r])

    @pl.when(holds)
    def _():
        def mend(r, left, centre, side):
            b = (left + LANES) // LANES - 1
            v = x_ref[:, aligned(at + b * LANES, 2 * LANES)]
            j = lax.broadcasted_iota(jnp.int32, (ROWS, 2 * LANES), 1) + (b * LANES - centre)
            w = jnp.where((j >= -HALF) & (j <= HALF), v, 0.0)
            f = jnp.clip(j, -HALF, HALF).astype(jnp.float32)
            level = jnp.sum(w, axis=1, keepdims=True) * (1.0 / TAPS)
            tilt = jnp.sum(w * f, axis=1, keepdims=True) * (1.0 / SECOND)
            curve = f * f - CENTRE_SQ
            bend = jnp.sum(w * curve, axis=1, keepdims=True) * (1.0 / FOURTH)
            smooth = level + tilt * f + bend * curve
            slope = HALF * (tilt + 2.0 * f * bend)
            held = (j * side >= 1) & (j * side <= HALF)
            for h in range(2):

                @pl.when((b + h >= 0) & (b + h < blocks))
                def _():
                    part = slice(h * LANES, (h + 1) * LANES)
                    to = held[:, part] & (row == r)
                    if to_fit:
                        at_fit = aligned(out_at + (b + h) * LANES, LANES)
                        fit_ref[0, :, at_fit] = jnp.where(
                            to, smooth[:, part], fit_ref[0, :, at_fit]
                        )
                        fit_ref[1, :, at_fit] = jnp.where(to, slope[:, part], fit_ref[1, :, at_fit])
                    if to_resid:
                        at_piece = aligned(piece_at + (b + h) * LANES, LANES)
                        resid_ref[k, :, at_piece] = jnp.where(
                            to, v[:, part] - smooth[:, part], resid_ref[k, :, at_piece]
                        )

        def series(r, carry):
            a = first_ref[group * ROWS + r]
            z = last_ref[group * ROWS + r]

            @pl.when(starts_here(a))
            def _():
                mend(r, a - mark, a - mark + HALF, -1)

            @pl.when(stops_here(z))
            def _():
                mend(r, z - mark - TAPS, z - mark - HALF - 1, 1)

            return carry

        def bunch(q, carry):
            some = False
            for r in range(4):
                some = some | starts_here(first_ref[group * ROWS + 4 * q + r])
                some = some | stops_here(last_ref[group * ROWS + 4 * q + r])

            @pl.when(some)
            def _():
                lax.fori_loop(4 * q, 4 * q + 4, series, 0)

            return carry

        lax.fori_loop(0, ROWS // 4, bunch, 0)


def cut_kernel(plan, signal_ref, *refs):
    base, span, _ = plan
    pieces, edges, (side_ref, sems) = refs[:GROUPS], refs[GROUPS : GROUPS + 2], refs[-2:]
    width = signal_ref.shape[1]
    mine = lax.axis_index("series")
    core = lax.axis_index("core")
    copies = []

    def move(start, size, to):
        copy = pltpu.make_async_copy(
            signal_ref.at[:, aligned(start, size)], to, sems.at[len(copies)]
        )
        copy.start()
        copies.append(copy)

    for k in (2, 1, 3, 0):
        start = base + (mine + k) % GROUPS * span
        move(start - LANES, LANES, side_ref.at[2 * k])
        move(start + span, LANES, side_ref.at[2 * k + 1])
        move(start, span, pieces[k].at[:, pl.ds(0, span)])
    move((1 - core) * (width - LANES), LANES, edges[0])
    move(core * (width - LANES), LANES, edges[1])
    for copy in copies:
        copy.wait()
    low = lax.broadcasted_iota(jnp.int32, edges[0].shape, 1) < 64
    for k in range(GROUPS):
        pieces[k][:, span:] = jnp.where(low, side_ref[2 * k + 1], side_ref[2 * k])


def cut_chunk(plan, signal):
    rows, _ = signal.shape
    part = jax.ShapeDtypeStruct((rows, plan[1] + LANES), jnp.float32)
    edge = jax.ShapeDtypeStruct((rows, LANES), jnp.float32)
    return pl.pallas_call(
        functools.partial(cut_kernel, plan),
        in_specs=[pl.BlockSpec(memory_space=pltpu.HBM)],
        out_specs=[pl.BlockSpec(memory_space=pltpu.VMEM)] * (GROUPS + 2),
        out_shape=[part] * GROUPS + [edge] * 2,
        scratch_shapes=[
            pltpu.VMEM((2 * GROUPS, rows, LANES), jnp.float32),
            pltpu.SemaphoreType.DMA((3 * GROUPS + 2,)),
        ],
        compiler_params=pltpu.CompilerParams(vmem_limit_bytes=8 * MIB),
        cost_estimate=pl.CostEstimate(
            flops=0, bytes_accessed=rows * plan[1] * 32, transcendentals=0
        ),
        name="cut_early",
    )(pltpu.with_memory_space_constraint(signal, pltpu.HBM))


def fit_kernel(plan, fits, resids, ends, *refs):
    base, span, count = plan
    refs = list(refs)
    whole = ends and base == 0
    first_hbm, last_hbm, signal_ref, taps_hbm = refs[:4]
    refs = refs[4:]
    if ends:
        halo_refs, refs = refs[:2], refs[2:]
    if fits:
        fit_hbm, refs = refs[:2], refs[2:]
    if resids:
        outs, refs = refs[:GROUPS], refs[GROUPS:]
    x_ref, taps_ref, first_ref, last_ref, in_sems, side_sems = refs[:6]
    refs = refs[6:]
    if fits:
        fit_ref, out_sems = refs[:2]
        refs = refs[2:]
    if resids:
        resid_ref = refs[0]

    width = signal_ref.shape[1]
    per = count // GROUPS
    half = count // 2
    mine = lax.axis_index("series")
    begin = lax.axis_index(TIME) * width
    core = lax.axis_index("core")

    def place(n):
        return LANES + n * span + (2 * LANES * (n // half) if ends and not whole else 0)

    def source(n):
        return lax.rem(base + n * span, width) if ends and not whole else base + n * span

    def fetch(n):
        return pltpu.make_async_copy(
            signal_ref.at[:, aligned(source(n), span)],
            x_ref.at[:, aligned(place(n), span)],
            in_sems.at[n],
        )

    middle = place(half)
    tail = place(count - 1) + span
    after = (base + count * span) % width
    sides = [(first_hbm, first_ref), (last_hbm, last_ref), (taps_hbm, taps_ref)]
    if not whole:
        sides += [
            (signal_ref.at[:, pl.ds(base - LANES, LANES)], x_ref.at[:, pl.ds(0, LANES)]),
            (signal_ref.at[:, pl.ds(after, LANES)], x_ref.at[:, pl.ds(tail, LANES)]),
        ]
    if ends:
        at_left, at_right = (0, tail) if whole else (middle - LANES, middle - 2 * LANES)
        across = core * (at_left - at_right)
        sides += [
            (halo_refs[0], x_ref.at[:, aligned(at_right + across, LANES)]),
            (halo_refs[1], x_ref.at[:, aligned(at_left - across, LANES)]),
        ]
    sides = [pltpu.make_async_copy(a, b, side_sems.at[n]) for n, (a, b) in enumerate(sides)]
    for copy in sides:
        copy.start()
    for n in range(count):
        fetch(n).start()

    def give(n, kind):
        return pltpu.make_async_copy(
            fit_ref.at[kind, :, aligned(n * span, span)],
            fit_hbm[kind].at[:, aligned(source(n), span)],
            out_sems.at[kind, n],
        )

    for copy in sides:
        copy.wait()
    fetch(0).wait()

    first, last = ends_of(mine, first_ref, last_ref)

    def body(n, carry):
        k = (n // per + GROUPS - mine) % GROUPS

        @pl.when(n + 1 < count)
        def _():
            fetch(n + 1).wait()

        fit_span(
            span,
            begin + source(n),
            mine,
            (x_ref, place(n)),
            (taps_ref, first_ref, last_ref, first, last),
            (fit_ref, n * span) if fits else None,
            (resid_ref, k, n % per * span) if resids else None,
        )
        if fits:
            give(n, 0).start()
            give(n, 1).start()
        return carry

    lax.fori_loop(0, count, body, 0)
    if resids:
        for kk in range(GROUPS):
            outs[kk][...] = resid_ref[kk]
    if fits:
        for n in range(count):
            give(n, 0).wait()
            give(n, 1).wait()


def fit_steps(plan, first, last, signal, taps, fits, resids, halos):
    base, span, count = plan
    rows, width = signal.shape
    ends = halos is not None
    margins = 4 if ends and base else 2
    if not fits:
        taps = taps[:, :LANES]
    hbm = pl.BlockSpec(memory_space=pltpu.HBM)
    vmem = pl.BlockSpec(memory_space=pltpu.VMEM)
    loose = pl.BlockSpec(memory_space=pl.ANY)
    args = [pltpu.with_memory_space_constraint(a, pltpu.HBM) for a in (first, last, signal, taps)]
    args += list(halos or ())
    wide = jax.ShapeDtypeStruct((rows, width), jnp.float32)
    part = jax.ShapeDtypeStruct((rows, count // GROUPS * span), jnp.float32)
    scratch = [
        pltpu.VMEM((rows, count * span + margins * LANES), jnp.float32),
        pltpu.VMEM(taps.shape, taps.dtype),
        pltpu.SMEM(first.shape, jnp.int32),
        pltpu.SMEM(last.shape, jnp.int32),
        pltpu.SemaphoreType.DMA((count,)),
        pltpu.SemaphoreType.DMA((7,)),
    ]
    if fits:
        scratch += [
            pltpu.VMEM((2, rows, count * span), jnp.float32),
            pltpu.SemaphoreType.DMA((2, count)),
        ]
    if resids:
        scratch += [pltpu.VMEM((GROUPS, rows, count // GROUPS * span), jnp.float32)]
    return pl.pallas_call(
        functools.partial(fit_kernel, plan, fits, resids, ends),
        in_specs=[hbm] * 4 + [loose] * len(halos or ()),
        out_specs=[hbm] * (2 * fits) + [vmem] * (GROUPS * resids),
        out_shape=[wide] * (2 * fits) + [part] * (GROUPS * resids),
        scratch_shapes=scratch,
        compiler_params=pltpu.CompilerParams(vmem_limit_bytes=16 * MIB),
        cost_estimate=pl.CostEstimate(
            flops=count * 3 * rows * span * 256 * 4,
            bytes_accessed=count * rows * span * 4 * 4,
            transcendentals=0,
        ),
    )(*args)


def stacked(stack_ref, group, x):
    at = pl.multiple_of(group * ROWS, ROWS)
    a = x.astype(jnp.bfloat16)
    stack_ref[pl.ds(at, ROWS)] = a
    stack_ref[pl.ds(64 + at, ROWS)] = (x - a.astype(jnp.float32)).astype(jnp.bfloat16)


def product(stack_ref, so_far_ref, spread, out_ref):
    both = lax.dot_general(
        stack_ref[...],
        stack_ref[...],
        (((1,), (1,)), ((), ())),
        preferred_element_type=jnp.float32,
    )
    gram = both[:64] + both[64:]
    gram = gram + pltpu.roll(gram, 64, 1)
    low = lax.broadcasted_iota(jnp.int32, (8, LANES), 1) < 64
    for g in range(GROUPS):
        rows = jnp.where(low, gram[16 * g : 16 * g + 8], gram[16 * g + 8 : 16 * g + 16])
        if so_far_ref is not None:
            rows = rows + so_far_ref[g]
        if spread:
            for n in range(spread):
                out_ref[n, g] = rows
        else:
            out_ref[g] = rows


def raw_gram_kernel(plan, width, first_hbm, last_hbm, taps_hbm, *refs):
    base, span, _ = plan
    pieces, refs = refs[:GROUPS], refs[GROUPS:]
    out_ref, x_ref, resid_ref, stack_ref, taps_ref, first_ref, last_ref, sems = refs
    mine = lax.axis_index("series")
    mark = lax.axis_index(TIME) * width + base + mine * span
    copies = [
        pltpu.make_async_copy(a, b, sems.at[n])
        for n, (a, b) in enumerate(
            ((first_hbm, first_ref), (last_hbm, last_ref), (taps_hbm, taps_ref))
        )
    ]
    for copy in copies:
        copy.start()
    for k in range(GROUPS):
        x_ref[k, :, :LANES] = pieces[k][:, span:]
        x_ref[k, :, LANES:] = pieces[k][...]
    for copy in copies:
        copy.wait()

    def body(k, carry):
        group = (mine + GROUPS - k) % GROUPS
        first, last = ends_of(group, first_ref, last_ref)
        fit_span(
            span,
            mark,
            group,
            (x_ref.at[k], LANES),
            (taps_ref, first_ref, last_ref, first, last),
            None,
            (resid_ref, 0, 0),
        )
        stacked(stack_ref, group, resid_ref[0])
        return carry

    lax.fori_loop(0, GROUPS, body, 0)
    product(stack_ref, None, None, out_ref)


def raw_gram_of(plan, width, first, last, taps, pieces):
    _, span, _ = plan
    taps = taps[:, :LANES]
    hbm = pl.BlockSpec(memory_space=pltpu.HBM)
    vmem = pl.BlockSpec(memory_space=pltpu.VMEM)
    args = [pltpu.with_memory_space_constraint(a, pltpu.HBM) for a in (first, last, taps)]
    return pl.pallas_call(
        functools.partial(raw_gram_kernel, plan, width),
        in_specs=[hbm] * 3 + [vmem] * GROUPS,
        out_specs=vmem,
        out_shape=jax.ShapeDtypeStruct((GROUPS, 8, LANES), jnp.float32),
        scratch_shapes=[
            pltpu.VMEM((GROUPS, ROWS, span + 2 * LANES), jnp.float32),
            pltpu.VMEM((1, ROWS, span), jnp.float32),
            pltpu.VMEM((128, span), jnp.bfloat16),
            pltpu.VMEM(taps.shape, taps.dtype),
            pltpu.SMEM(first.shape, jnp.int32),
            pltpu.SMEM(last.shape, jnp.int32),
            pltpu.SemaphoreType.DMA((3,)),
        ],
        compiler_params=pltpu.CompilerParams(vmem_limit_bytes=16 * MIB),
        cost_estimate=pl.CostEstimate(
            flops=GROUPS * 3 * ROWS * span * 256 * 4,
            bytes_accessed=GROUPS * ROWS * span * 8,
            transcendentals=0,
        ),
    )(*args, *pieces)


def gram_kernel(add, spread, *refs):
    parts, refs = refs[:GROUPS], refs[GROUPS:]
    if add:
        so_far_ref, refs = refs[0], refs[1:]
    out_ref, stack_ref = refs
    mine = lax.axis_index("series")
    for k in range(GROUPS):
        stacked(stack_ref, (mine + GROUPS - k) % GROUPS, parts[k][...])
    product(stack_ref, so_far_ref if add else None, spread, out_ref)


def gram_of(parts, so_far, spread):
    width = parts[0].shape[1]
    vmem = pl.BlockSpec(memory_space=pltpu.VMEM)
    args = list(parts) + ([] if so_far is None else [so_far])
    lead = (spread,) if spread else ()
    return pl.pallas_call(
        functools.partial(gram_kernel, so_far is not None, spread),
        in_specs=[vmem] * len(args),
        out_specs=vmem,
        out_shape=jax.ShapeDtypeStruct((*lead, GROUPS, 8, LANES), jnp.float32),
        scratch_shapes=[pltpu.VMEM((128, width), jnp.bfloat16)],
        compiler_params=pltpu.CompilerParams(vmem_limit_bytes=12 * MIB),
        cost_estimate=pl.CostEstimate(
            flops=128 * 128 * width * 2, bytes_accessed=64 * width * 4, transcendentals=0
        ),
    )(*args)


def packed(rows):
    return jnp.concatenate([rows[:8], rows[8:]], axis=1)


def exchanged(pieces):
    parts = [pieces[0]]
    for k in (2, 1, 3):
        pairs = [(s, (s + k) % GROUPS) for s in range(GROUPS)]
        parts.append(lax.ppermute(pieces[k], "series", pairs))
    return [parts[0], parts[2], parts[1], parts[3]]


def shards(taps, signal, valid_start, valid_end):
    rows, width = signal.shape
    devices = lax.axis_size(TIME)
    taps = jnp.asarray(taps, jnp.bfloat16)
    mine = lax.axis_index("series")
    unit = width // 32
    early, mid = (2 * unit, 4 * unit, GROUPS), (18 * unit, 3 * unit, GROUPS)
    late, whole = (30 * unit, unit, GROUPS), (0, 4 * unit, 8)

    def fit(plan, fits, resids, halos=None):
        return fit_steps(plan, valid_start, valid_end, signal, taps, fits, resids, halos)

    first = lax.dynamic_slice_in_dim(valid_start, mine * rows, rows)[:, None]
    last = lax.dynamic_slice_in_dim(valid_end, mine * rows, rows)[:, None]
    shared = jnp.minimum(last, valid_end[None, :])
    shared = shared - jnp.maximum(first, valid_start[None, :])
    shared = packed(shared.astype(jnp.float32))

    *pieces, near, far = cut_chunk(early, signal)
    parts = exchanged(pieces)
    parts_mid = exchanged(fit(mid, False, True))
    near = lax.ppermute(near, TIME, [(t, t ^ 1) for t in range(devices)])
    pairs = [(t, t + 1) for t in range(1, devices - 1, 2)]
    far = lax.ppermute(far, TIME, pairs + [(b, a) for a, b in pairs])
    halos = (near, far)
    gram = raw_gram_of(early, width, valid_start, valid_end, taps, parts)
    parts = exchanged(fit(late, False, True, halos))
    gram = gram_of(parts_mid, gram, None)
    copies = gram_of(parts, gram, devices)
    copies = copies.reshape(devices * GROUPS, 8, LANES)
    copies = lax.all_to_all(copies, (*TIME, "series"), 0, 0, tiled=True)
    smooth, slope = fit(whole, True, False, halos)
    cov = jnp.sum(copies, axis=0) / shared
    return smooth, slope, jnp.concatenate([cov[:, :64], cov[:, 64:]], axis=0)


def solution(mesh):
    split = Mesh(mesh.devices.reshape(4, 4, 2, GROUPS), (*TIME, "series"))
    return jax.shard_map(
        functools.partial(shards, filter_matrix()),
        mesh=split,
        in_specs=(P("series", TIME), P(), P()),
        out_specs=(P("series", TIME), P("series", TIME), P("series", None)),
        check_vma=False,
    )
```

```python
import functools

import jax
import jax.numpy as jnp
import numpy as np
from jax import lax
from jax.experimental import pallas as pl
from jax.experimental.pallas import tpu as pltpu
from jax.sharding import Mesh
from jax.sharding import PartitionSpec as P


HALF = 16
TAPS = 2 * HALF + 1
ROWS = 16
GROUPS = 4
LANES = 128
TIME = ("y", "z", "core")
MIB = 1 << 20

SECOND = float(sum(j * j for j in range(-HALF, HALF + 1)))
CENTRE_SQ = SECOND / TAPS
FOURTH = float(sum((j * j - CENTRE_SQ) ** 2 for j in range(-HALF, HALF + 1)))
SMOOTH_SCALE = 2048.0 / 2387.0
SLOPE_SCALE = HALF * 16.0 / SECOND


def filter_matrix():
    place = np.concatenate([np.arange(128), np.arange(128, 192), np.arange(-64, 0)])
    j = place[:, None] - np.arange(LANES)[None, :]
    near = np.abs(j) <= HALF
    smooth = np.where(near, (163 - j * j) / 2048.0, 0.0)
    slope = np.where(near, j / 16.0, 0.0)
    return np.concatenate([smooth, slope], axis=1).astype(np.float32)


def thirds(x):
    a = x.astype(jnp.bfloat16)
    rest = x - a.astype(jnp.float32)
    b = rest.astype(jnp.bfloat16)
    c = (rest - b.astype(jnp.float32)).astype(jnp.bfloat16)
    return a, b, c


def aligned(start, size):
    return pl.ds(pl.multiple_of(start, LANES), size)


def ends_of(group, first_ref, last_ref):
    row = lax.broadcasted_iota(jnp.int32, (ROWS, LANES), 0)
    first = jnp.zeros((ROWS, LANES), jnp.int32)
    last = jnp.zeros((ROWS, LANES), jnp.int32)
    for r in range(ROWS):
        first = jnp.where(row == r, first_ref[group * ROWS + r], first)
        last = jnp.where(row == r, last_ref[group * ROWS + r], last)
    return first, last


def fit_span(span, mark, group, samples, tables, to_fit, to_resid):
    blocks = span // LANES
    height = ROWS * blocks
    x_ref, at = samples
    taps_ref, first_ref, last_ref, first, last = tables
    if to_fit:
        fit_ref, out_at = to_fit
    if to_resid:
        resid_ref, k, piece_at = to_resid
    lane = lax.broadcasted_iota(jnp.int32, (ROWS, LANES), 1)
    row = lax.broadcasted_iota(jnp.int32, (ROWS, LANES), 0)
    low = lane < 64

    x = x_ref[:, aligned(at - LANES, span + 2 * LANES)]
    parts = thirds(x)

    def cut(m, b):
        return parts[m][:, b * LANES : (b + 1) * LANES]

    rows = [
        jnp.concatenate([cut(m, b + 1), jnp.where(low, cut(m, b + 2), cut(m, b))], axis=1)
        for m in range(3)
        for b in range(blocks)
    ]
    fit = jnp.dot(
        jnp.concatenate(rows, axis=0), taps_ref[...], preferred_element_type=jnp.float32
    )
    fit = fit[:height] + (fit[height : 2 * height] + fit[2 * height :])
    since = first - mark
    until = last - mark
    for b in range(blocks):
        part = fit[b * ROWS : (b + 1) * ROWS]
        moment = lane + b * LANES
        inside = (moment >= since) & (moment < until)
        smooth = part[:, :LANES] * SMOOTH_SCALE
        if to_fit:
            to = aligned(out_at + b * LANES, LANES)
            fit_ref[0, :, to] = jnp.where(inside, smooth, 0.0)
            fit_ref[1, :, to] = jnp.where(inside, part[:, LANES:] * SLOPE_SCALE, 0.0)
        if to_resid:
            resid = x[:, (b + 1) * LANES : (b + 2) * LANES] - smooth
            resid_ref[k, :, aligned(piece_at + b * LANES, LANES)] = jnp.where(inside, resid, 0.0)

    def starts_here(a):
        return (a > mark - HALF) & (a < mark + span)

    def stops_here(z):
        return (z > mark) & (z < mark + span + HALF)

    holds = False
    for r in range(ROWS):
        holds = holds | starts_here(first_ref[group * ROWS + r])
        holds = holds | stops_here(last_ref[group * ROWS + r])

    @pl.when(holds)
    def _():
        def mend(r, left, centre, side):
            b = (left + LANES) // LANES - 1
            v = x_ref[:, aligned(at + b * LANES, 2 * LANES)]
            j = lax.broadcasted_iota(jnp.int32, (ROWS, 2 * LANES), 1) + (b * LANES - centre)
            w = jnp.where((j >= -HALF) & (j <= HALF), v, 0.0)
            f = jnp.clip(j, -HALF, HALF).astype(jnp.float32)
            level = jnp.sum(w, axis=1, keepdims=True) * (1.0 / TAPS)
            tilt = jnp.sum(w * f, axis=1, keepdims=True) * (1.0 / SECOND)
            curve = f * f - CENTRE_SQ
            bend = jnp.sum(w * curve, axis=1, keepdims=True) * (1.0 / FOURTH)
            smooth = level + tilt * f + bend * curve
            slope = HALF * (tilt + 2.0 * f * bend)
            held = (j * side >= 1) & (j * side <= HALF)
            for h in range(2):

                @pl.when((b + h >= 0) & (b + h < blocks))
                def _():
                    part = slice(h * LANES, (h + 1) * LANES)
                    to = held[:, part] & (row == r)
                    if to_fit:
                        at_fit = aligned(out_at + (b + h) * LANES, LANES)
                        fit_ref[0, :, at_fit] = jnp.where(
                            to, smooth[:, part], fit_ref[0, :, at_fit]
                        )
                        fit_ref[1, :, at_fit] = jnp.where(to, slope[:, part], fit_ref[1, :, at_fit])
                    if to_resid:
                        at_piece = aligned(piece_at + (b + h) * LANES, LANES)
                        resid_ref[k, :, at_piece] = jnp.where(
                            to, v[:, part] - smooth[:, part], resid_ref[k, :, at_piece]
                        )

        def series(r, carry):
            a = first_ref[group * ROWS + r]
            z = last_ref[group * ROWS + r]

            @pl.when(starts_here(a))
            def _():
                mend(r, a - mark, a - mark + HALF, -1)

            @pl.when(stops_here(z))
            def _():
                mend(r, z - mark - TAPS, z - mark - HALF - 1, 1)

            return carry

        def bunch(q, carry):
            some = False
            for r in range(4):
                some = some | starts_here(first_ref[group * ROWS + 4 * q + r])
                some = some | stops_here(last_ref[group * ROWS + 4 * q + r])

            @pl.when(some)
            def _():
                lax.fori_loop(4 * q, 4 * q + 4, series, 0)

            return carry

        lax.fori_loop(0, ROWS // 4, bunch, 0)


def cut_kernel(plan, signal_ref, *refs):
    base, span, _ = plan
    pieces, edges, (side_ref, sems) = refs[:GROUPS], refs[GROUPS : GROUPS + 2], refs[-2:]
    width = signal_ref.shape[1]
    mine = lax.axis_index("series")
    core = lax.axis_index("core")
    copies = []

    def move(start, size, to):
        copy = pltpu.make_async_copy(
            signal_ref.at[:, aligned(start, size)], to, sems.at[len(copies)]
        )
        copy.start()
        copies.append(copy)

    for k in (2, 1, 3, 0):
        start = base + (mine + k) % GROUPS * span
        move(start - LANES, LANES, side_ref.at[2 * k])
        move(start + span, LANES, side_ref.at[2 * k + 1])
        move(start, span, pieces[k].at[:, pl.ds(0, span)])
    move((1 - core) * (width - LANES), LANES, edges[0])
    move(core * (width - LANES), LANES, edges[1])
    for copy in copies:
        copy.wait()
    low = lax.broadcasted_iota(jnp.int32, edges[0].shape, 1) < 64
    for k in range(GROUPS):
        pieces[k][:, span:] = jnp.where(low, side_ref[2 * k + 1], side_ref[2 * k])


def cut_chunk(plan, signal):
    rows, _ = signal.shape
    part = jax.ShapeDtypeStruct((rows, plan[1] + LANES), jnp.float32)
    edge = jax.ShapeDtypeStruct((rows, LANES), jnp.float32)
    return pl.pallas_call(
        functools.partial(cut_kernel, plan),
        in_specs=[pl.BlockSpec(memory_space=pltpu.HBM)],
        out_specs=[pl.BlockSpec(memory_space=pltpu.VMEM)] * (GROUPS + 2),
        out_shape=[part] * GROUPS + [edge] * 2,
        scratch_shapes=[
            pltpu.VMEM((2 * GROUPS, rows, LANES), jnp.float32),
            pltpu.SemaphoreType.DMA((3 * GROUPS + 2,)),
        ],
        compiler_params=pltpu.CompilerParams(vmem_limit_bytes=8 * MIB),
        cost_estimate=pl.CostEstimate(
            flops=0, bytes_accessed=rows * plan[1] * 32, transcendentals=0
        ),
        name="cut_early",
    )(pltpu.with_memory_space_constraint(signal, pltpu.HBM))


def fit_kernel(plan, fits, resids, ends, chain, *refs):
    base, span, count = plan
    refs = list(refs)
    first_hbm, last_hbm, signal_ref, taps_hbm = refs[:4]
    refs = refs[4:]
    if ends:
        halo_refs, refs = refs[:2], refs[2:]
    if chain:
        refs = refs[2:]
    if fits:
        fit_hbm, refs = refs[:2], refs[2:]
    if resids:
        outs, refs = refs[:GROUPS], refs[GROUPS:]
    x_ref, taps_ref, first_ref, last_ref, in_sems, side_sems = refs[:6]
    refs = refs[6:]
    if fits:
        fit_ref, out_sems = refs[:2]
        refs = refs[2:]
    if resids:
        resid_ref = refs[0]

    width = signal_ref.shape[1]
    per = count // GROUPS
    half = count // 2
    mine = lax.axis_index("series")
    begin = lax.axis_index(TIME) * width
    core = lax.axis_index("core")

    def place(n):
        return LANES + n * span + (2 * LANES * (n // half) if ends else 0)

    def source(n):
        return lax.rem(base + n * span, width) if ends else base + n * span

    def fetch(n):
        return pltpu.make_async_copy(
            signal_ref.at[:, aligned(source(n), span)],
            x_ref.at[:, aligned(place(n), span)],
            in_sems.at[n],
        )

    middle = place(half)
    tail = place(count - 1) + span
    after = (base + count * span) % width
    sides = [
        (first_hbm, first_ref),
        (last_hbm, last_ref),
        (taps_hbm, taps_ref),
        (signal_ref.at[:, pl.ds(base - LANES, LANES)], x_ref.at[:, pl.ds(0, LANES)]),
        (signal_ref.at[:, pl.ds(after, LANES)], x_ref.at[:, pl.ds(tail, LANES)]),
    ]
    if ends:
        at_left, at_right = middle - LANES, middle - 2 * LANES
        across = core * (at_left - at_right)
        sides += [
            (halo_refs[0], x_ref.at[:, aligned(at_right + across, LANES)]),
            (halo_refs[1], x_ref.at[:, aligned(at_left - across, LANES)]),
        ]
    sides = [pltpu.make_async_copy(a, b, side_sems.at[n]) for n, (a, b) in enumerate(sides)]
    for copy in sides:
        copy.start()
    for n in range(count):
        fetch(n).start()

    def give(n, kind):
        return pltpu.make_async_copy(
            fit_ref.at[kind, :, aligned(n * span, span)],
            fit_hbm[kind].at[:, aligned(source(n), span)],
            out_sems.at[kind, n],
        )

    for copy in sides:
        copy.wait()
    fetch(0).wait()

    first, last = ends_of(mine, first_ref, last_ref)

    def body(n, carry):
        k = (n // per + GROUPS - mine) % GROUPS

        @pl.when(n + 1 < count)
        def _():
            fetch(n + 1).wait()

        fit_span(
            span,
            begin + source(n),
            mine,
            (x_ref, place(n)),
            (taps_ref, first_ref, last_ref, first, last),
            (fit_ref, n * span) if fits else None,
            (resid_ref, k, n % per * span) if resids else None,
        )
        if fits:
            give(n, 0).start()
            give(n, 1).start()
        return carry

    lax.fori_loop(0, count, body, 0)
    if resids:
        for kk in range(GROUPS):
            outs[kk][...] = resid_ref[kk]
    if fits:
        for n in range(count):
            give(n, 0).wait()
            give(n, 1).wait()


def fit_steps(plan, first, last, signal, taps, fits, resids, halos, held):
    _, span, count = plan
    rows, width = signal.shape
    ends = halos is not None
    margins = 4 if ends else 2
    if not fits:
        taps = taps[:, :LANES]
    hbm = pl.BlockSpec(memory_space=pltpu.HBM)
    vmem = pl.BlockSpec(memory_space=pltpu.VMEM)
    loose = pl.BlockSpec(memory_space=pl.ANY)
    args = [pltpu.with_memory_space_constraint(a, pltpu.HBM) for a in (first, last, signal, taps)]
    args += list(halos or ()) + list(held or ())
    aliases = {len(args) - 2: 0, len(args) - 1: 1} if held else {}
    wide = jax.ShapeDtypeStruct((rows, width), jnp.float32)
    part = jax.ShapeDtypeStruct((rows, count // GROUPS * span), jnp.float32)
    scratch = [
        pltpu.VMEM((rows, count * span + margins * LANES), jnp.float32),
        pltpu.VMEM(taps.shape, taps.dtype),
        pltpu.SMEM(first.shape, jnp.int32),
        pltpu.SMEM(last.shape, jnp.int32),
        pltpu.SemaphoreType.DMA((count,)),
        pltpu.SemaphoreType.DMA((7,)),
    ]
    if fits:
        scratch += [
            pltpu.VMEM((2, rows, count * span), jnp.float32),
            pltpu.SemaphoreType.DMA((2, count)),
        ]
    if resids:
        scratch += [pltpu.VMEM((GROUPS, rows, count // GROUPS * span), jnp.float32)]
    return pl.pallas_call(
        functools.partial(fit_kernel, plan, fits, resids, ends, bool(held)),
        in_specs=[hbm] * 4 + [loose] * len(halos or ()) + [hbm] * len(held or ()),
        out_specs=[hbm] * (2 * fits) + [vmem] * (GROUPS * resids),
        out_shape=[wide] * (2 * fits) + [part] * (GROUPS * resids),
        scratch_shapes=scratch,
        input_output_aliases=aliases,
        compiler_params=pltpu.CompilerParams(vmem_limit_bytes=16 * MIB),
        cost_estimate=pl.CostEstimate(
            flops=count * 3 * rows * span * 256 * 4,
            bytes_accessed=count * rows * span * 4 * 4,
            transcendentals=0,
        ),
    )(*args)


def stacked(stack_ref, group, x):
    at = pl.multiple_of(group * ROWS, ROWS)
    a = x.astype(jnp.bfloat16)
    stack_ref[pl.ds(at, ROWS)] = a
    stack_ref[pl.ds(64 + at, ROWS)] = (x - a.astype(jnp.float32)).astype(jnp.bfloat16)


def product(stack_ref, so_far_ref, spread, out_ref):
    both = lax.dot_general(
        stack_ref[...],
        stack_ref[...],
        (((1,), (1,)), ((), ())),
        preferred_element_type=jnp.float32,
    )
    gram = both[:64] + both[64:]
    gram = gram + pltpu.roll(gram, 64, 1)
    low = lax.broadcasted_iota(jnp.int32, (8, LANES), 1) < 64
    for g in range(GROUPS):
        rows = jnp.where(low, gram[16 * g : 16 * g + 8], gram[16 * g + 8 : 16 * g + 16])
        if so_far_ref is not None:
            rows = rows + so_far_ref[g]
        if spread:
            for n in range(spread):
                out_ref[n, g] = rows
        else:
            out_ref[g] = rows


def raw_gram_kernel(plan, width, first_hbm, last_hbm, taps_hbm, *refs):
    base, span, _ = plan
    pieces, refs = refs[:GROUPS], refs[GROUPS:]
    out_ref, x_ref, resid_ref, stack_ref, taps_ref, first_ref, last_ref, sems = refs
    mine = lax.axis_index("series")
    mark = lax.axis_index(TIME) * width + base + mine * span
    copies = [
        pltpu.make_async_copy(a, b, sems.at[n])
        for n, (a, b) in enumerate(
            ((first_hbm, first_ref), (last_hbm, last_ref), (taps_hbm, taps_ref))
        )
    ]
    for copy in copies:
        copy.start()
    for k in range(GROUPS):
        x_ref[k, :, :LANES] = pieces[k][:, span:]
        x_ref[k, :, LANES:] = pieces[k][...]
    for copy in copies:
        copy.wait()

    def body(k, carry):
        group = (mine + GROUPS - k) % GROUPS
        first, last = ends_of(group, first_ref, last_ref)
        fit_span(
            span,
            mark,
            group,
            (x_ref.at[k], LANES),
            (taps_ref, first_ref, last_ref, first, last),
            None,
            (resid_ref, 0, 0),
        )
        stacked(stack_ref, group, resid_ref[0])
        return carry

    lax.fori_loop(0, GROUPS, body, 0)
    product(stack_ref, None, None, out_ref)


def raw_gram_of(plan, width, first, last, taps, pieces):
    _, span, _ = plan
    taps = taps[:, :LANES]
    hbm = pl.BlockSpec(memory_space=pltpu.HBM)
    vmem = pl.BlockSpec(memory_space=pltpu.VMEM)
    args = [pltpu.with_memory_space_constraint(a, pltpu.HBM) for a in (first, last, taps)]
    return pl.pallas_call(
        functools.partial(raw_gram_kernel, plan, width),
        in_specs=[hbm] * 3 + [vmem] * GROUPS,
        out_specs=vmem,
        out_shape=jax.ShapeDtypeStruct((GROUPS, 8, LANES), jnp.float32),
        scratch_shapes=[
            pltpu.VMEM((GROUPS, ROWS, span + 2 * LANES), jnp.float32),
            pltpu.VMEM((1, ROWS, span), jnp.float32),
            pltpu.VMEM((128, span), jnp.bfloat16),
            pltpu.VMEM(taps.shape, taps.dtype),
            pltpu.SMEM(first.shape, jnp.int32),
            pltpu.SMEM(last.shape, jnp.int32),
            pltpu.SemaphoreType.DMA((3,)),
        ],
        compiler_params=pltpu.CompilerParams(vmem_limit_bytes=16 * MIB),
        cost_estimate=pl.CostEstimate(
            flops=GROUPS * 3 * ROWS * span * 256 * 4,
            bytes_accessed=GROUPS * ROWS * span * 8,
            transcendentals=0,
        ),
    )(*args, *pieces)


def gram_kernel(add, spread, *refs):
    parts, refs = refs[:GROUPS], refs[GROUPS:]
    if add:
        so_far_ref, refs = refs[0], refs[1:]
    out_ref, stack_ref = refs
    mine = lax.axis_index("series")
    for k in range(GROUPS):
        stacked(stack_ref, (mine + GROUPS - k) % GROUPS, parts[k][...])
    product(stack_ref, so_far_ref if add else None, spread, out_ref)


def gram_of(parts, so_far, spread):
    width = parts[0].shape[1]
    vmem = pl.BlockSpec(memory_space=pltpu.VMEM)
    args = list(parts) + ([] if so_far is None else [so_far])
    lead = (spread,) if spread else ()
    return pl.pallas_call(
        functools.partial(gram_kernel, so_far is not None, spread),
        in_specs=[vmem] * len(args),
        out_specs=vmem,
        out_shape=jax.ShapeDtypeStruct((*lead, GROUPS, 8, LANES), jnp.float32),
        scratch_shapes=[pltpu.VMEM((128, width), jnp.bfloat16)],
        compiler_params=pltpu.CompilerParams(vmem_limit_bytes=12 * MIB),
        cost_estimate=pl.CostEstimate(
            flops=128 * 128 * width * 2, bytes_accessed=64 * width * 4, transcendentals=0
        ),
    )(*args)


def exchanged(pieces):
    parts = [pieces[0]]
    for k in (2, 1, 3):
        pairs = [(s, (s + k) % GROUPS) for s in range(GROUPS)]
        parts.append(lax.ppermute(pieces[k], "series", pairs))
    return [parts[0], parts[2], parts[1], parts[3]]


def shards(taps, signal, valid_start, valid_end):
    rows, width = signal.shape
    devices = lax.axis_size(TIME)
    taps = jnp.asarray(taps, jnp.bfloat16)
    mine = lax.axis_index("series")
    unit = width // 32
    early, mid = (2 * unit, 4 * unit, GROUPS), (18 * unit, 3 * unit, GROUPS)
    late = (30 * unit, unit, GROUPS)

    def fit(plan, resids, halos=None, held=None):
        out = fit_steps(plan, valid_start, valid_end, signal, taps, True, resids, halos, held)
        return out[:2], out[2:]

    first = lax.dynamic_slice_in_dim(valid_start, mine * rows, rows)[:, None]
    last = lax.dynamic_slice_in_dim(valid_end, mine * rows, rows)[:, None]
    shared = jnp.minimum(last, valid_end[None, :])
    shared = shared - jnp.maximum(first, valid_start[None, :])
    shared = shared.astype(jnp.float32)

    *pieces, near, far = cut_chunk(early, signal)
    parts = exchanged(pieces)
    held, pieces = fit(mid, True)
    parts_mid = exchanged(pieces)
    near = lax.ppermute(near, TIME, [(t, t ^ 1) for t in range(devices)])
    pairs = [(t, t + 1) for t in range(1, devices - 1, 2)]
    far = lax.ppermute(far, TIME, pairs + [(b, a) for a, b in pairs])
    halos = (near, far)
    gram = raw_gram_of(early, width, valid_start, valid_end, taps, parts)
    held, pieces = fit(late, True, halos, held)
    parts = exchanged(pieces)
    gram = gram_of(parts_mid, gram, None)
    copies = gram_of(parts, gram, devices // 2)
    copies = copies.reshape(devices * GROUPS, 4, LANES)
    copies = lax.all_to_all(copies, (*TIME[:2], "series", "core"), 0, 0, tiled=True)
    (smooth, slope), _ = fit(early, False, held=held)
    own = jnp.sum(copies, axis=0)
    other = lax.ppermute(own, "core", [(0, 1), (1, 0)])
    lead = lax.axis_index("core") == 0
    p, q = jnp.where(lead, own, other), jnp.where(lead, other, own)
    gram = jnp.concatenate([p[:, :64], q[:, :64], p[:, 64:], q[:, 64:]], axis=0)
    return smooth, slope, gram / shared


def solution(mesh):
    split = Mesh(mesh.devices.reshape(4, 4, 2, GROUPS), (*TIME, "series"))
    return jax.shard_map(
        functools.partial(shards, filter_matrix()),
        mesh=split,
        in_specs=(P("series", TIME), P(), P()),
        out_specs=(P("series", TIME), P("series", TIME), P("series", None)),
        check_vma=False,
    )
```

```python
import functools

import jax
import jax.numpy as jnp
import numpy as np
from jax import lax
from jax.experimental import pallas as pl
from jax.experimental.pallas import tpu as pltpu
from jax.sharding import Mesh
from jax.sharding import PartitionSpec as P


HALF = 16
TAPS = 2 * HALF + 1
ROWS = 16
GROUPS = 4
LANES = 128
TIME = ("y", "z", "core")
MIB = 1 << 20

SECOND = float(sum(j * j for j in range(-HALF, HALF + 1)))
CENTRE_SQ = SECOND / TAPS
FOURTH = float(sum((j * j - CENTRE_SQ) ** 2 for j in range(-HALF, HALF + 1)))
SMOOTH_SCALE = 2048.0 / 2387.0
SLOPE_SCALE = HALF * 16.0 / SECOND


def filter_matrix():
    place = np.concatenate([np.arange(128), np.arange(128, 192), np.arange(-64, 0)])
    j = place[:, None] - np.arange(LANES)[None, :]
    near = np.abs(j) <= HALF
    smooth = np.where(near, (163 - j * j) / 2048.0, 0.0)
    slope = np.where(near, j / 16.0, 0.0)
    return np.concatenate([smooth, slope], axis=1).astype(np.float32)


def thirds(x):
    a = x.astype(jnp.bfloat16)
    rest = x - a.astype(jnp.float32)
    b = rest.astype(jnp.bfloat16)
    c = (rest - b.astype(jnp.float32)).astype(jnp.bfloat16)
    return a, b, c


def aligned(start, size):
    return pl.ds(pl.multiple_of(start, LANES), size)


def ends_of(group, first_ref, last_ref):
    row = lax.broadcasted_iota(jnp.int32, (ROWS, LANES), 0)
    first = jnp.zeros((ROWS, LANES), jnp.int32)
    last = jnp.zeros((ROWS, LANES), jnp.int32)
    for r in range(ROWS):
        first = jnp.where(row == r, first_ref[group * ROWS + r], first)
        last = jnp.where(row == r, last_ref[group * ROWS + r], last)
    return first, last


def fit_span(span, mark, group, samples, tables, to_fit, to_resid):
    blocks = span // LANES
    x_ref, at = samples
    taps_ref, first_ref, last_ref, first, last = tables
    if to_fit:
        fit_ref, out_at = to_fit
    if to_resid:
        resid_ref, k, piece_at = to_resid
    lane = lax.broadcasted_iota(jnp.int32, (ROWS, LANES), 1)
    row = lax.broadcasted_iota(jnp.int32, (ROWS, LANES), 0)
    low = lane < 64

    since = first - mark
    until = last - mark
    group_blocks = 16 if to_fit else 8
    for begin in range(0, blocks, group_blocks):
        gather = min(group_blocks, blocks - begin)
        height = ROWS * gather
        x = x_ref[:, aligned(at + (begin - 1) * LANES, (gather + 2) * LANES)]
        parts = thirds(x)

        def cut(m, b):
            return parts[m][:, b * LANES : (b + 1) * LANES]

        rows = [
            jnp.concatenate([cut(m, b + 1), jnp.where(low, cut(m, b + 2), cut(m, b))], axis=1)
            for m in range(3)
            for b in range(gather)
        ]
        fit = jnp.dot(
            jnp.concatenate(rows, axis=0), taps_ref[...], preferred_element_type=jnp.float32
        )
        fit = fit[:height] + (fit[height : 2 * height] + fit[2 * height :])
        for n in range(gather):
            b = begin + n
            part = fit[n * ROWS : (n + 1) * ROWS]
            moment = lane + b * LANES
            inside = (moment >= since) & (moment < until)
            smooth = part[:, :LANES] * SMOOTH_SCALE
            if to_fit:
                to = aligned(out_at + b * LANES, LANES)
                fit_ref[0, :, to] = jnp.where(inside, smooth, 0.0)
                fit_ref[1, :, to] = jnp.where(inside, part[:, LANES:] * SLOPE_SCALE, 0.0)
            if to_resid:
                resid = x[:, (n + 1) * LANES : (n + 2) * LANES] - smooth
                to = aligned(piece_at + b * LANES, LANES)
                resid_ref[k, :, to] = jnp.where(inside, resid, 0.0)

    def starts_here(a):
        return (a > mark - HALF) & (a < mark + span)

    def stops_here(z):
        return (z > mark) & (z < mark + span + HALF)

    holds = False
    for r in range(ROWS):
        holds = holds | starts_here(first_ref[group * ROWS + r])
        holds = holds | stops_here(last_ref[group * ROWS + r])

    @pl.when(holds)
    def _():
        def mend(r, left, centre, side):
            b = (left + LANES) // LANES - 1
            v = x_ref[:, aligned(at + b * LANES, 2 * LANES)]
            j = lax.broadcasted_iota(jnp.int32, (ROWS, 2 * LANES), 1) + (b * LANES - centre)
            w = jnp.where((j >= -HALF) & (j <= HALF), v, 0.0)
            f = jnp.clip(j, -HALF, HALF).astype(jnp.float32)
            level = jnp.sum(w, axis=1, keepdims=True) * (1.0 / TAPS)
            tilt = jnp.sum(w * f, axis=1, keepdims=True) * (1.0 / SECOND)
            curve = f * f - CENTRE_SQ
            bend = jnp.sum(w * curve, axis=1, keepdims=True) * (1.0 / FOURTH)
            smooth = level + tilt * f + bend * curve
            slope = HALF * (tilt + 2.0 * f * bend)
            held = (j * side >= 1) & (j * side <= HALF)
            for h in range(2):

                @pl.when((b + h >= 0) & (b + h < blocks))
                def _():
                    part = slice(h * LANES, (h + 1) * LANES)
                    to = held[:, part] & (row == r)
                    if to_fit:
                        at_fit = aligned(out_at + (b + h) * LANES, LANES)
                        fit_ref[0, :, at_fit] = jnp.where(
                            to, smooth[:, part], fit_ref[0, :, at_fit]
                        )
                        fit_ref[1, :, at_fit] = jnp.where(to, slope[:, part], fit_ref[1, :, at_fit])
                    if to_resid:
                        at_piece = aligned(piece_at + (b + h) * LANES, LANES)
                        resid_ref[k, :, at_piece] = jnp.where(
                            to, v[:, part] - smooth[:, part], resid_ref[k, :, at_piece]
                        )

        def series(r, carry):
            a = first_ref[group * ROWS + r]
            z = last_ref[group * ROWS + r]

            @pl.when(starts_here(a))
            def _():
                mend(r, a - mark, a - mark + HALF, -1)

            @pl.when(stops_here(z))
            def _():
                mend(r, z - mark - TAPS, z - mark - HALF - 1, 1)

            return carry

        def bunch(q, carry):
            some = False
            for r in range(4):
                some = some | starts_here(first_ref[group * ROWS + 4 * q + r])
                some = some | stops_here(last_ref[group * ROWS + 4 * q + r])

            @pl.when(some)
            def _():
                lax.fori_loop(4 * q, 4 * q + 4, series, 0)

            return carry

        lax.fori_loop(0, ROWS // 4, bunch, 0)


def cut_kernel(plan, signal_ref, *refs):
    base, span, _ = plan
    pieces, edges, (side_ref, sems) = refs[:GROUPS], refs[GROUPS : GROUPS + 2], refs[-2:]
    width = signal_ref.shape[1]
    mine = lax.axis_index("series")
    core = lax.axis_index("core")
    copies = []

    def move(start, size, to):
        copy = pltpu.make_async_copy(
            signal_ref.at[:, aligned(start, size)], to, sems.at[len(copies)]
        )
        copy.start()
        copies.append(copy)

    for k in (2, 1, 3, 0):
        start = base + (mine + k) % GROUPS * span
        move(start - LANES, LANES, side_ref.at[2 * k])
        move(start + span, LANES, side_ref.at[2 * k + 1])
        move(start, span, pieces[k].at[:, pl.ds(0, span)])
    move((1 - core) * (width - LANES), LANES, edges[0])
    move(core * (width - LANES), LANES, edges[1])
    for copy in copies:
        copy.wait()
    low = lax.broadcasted_iota(jnp.int32, edges[0].shape, 1) < 64
    for k in range(GROUPS):
        pieces[k][:, span:] = jnp.where(low, side_ref[2 * k + 1], side_ref[2 * k])


def cut_chunk(plan, signal):
    rows, _ = signal.shape
    part = jax.ShapeDtypeStruct((rows, plan[1] + LANES), jnp.float32)
    edge = jax.ShapeDtypeStruct((rows, LANES), jnp.float32)
    return pl.pallas_call(
        functools.partial(cut_kernel, plan),
        in_specs=[pl.BlockSpec(memory_space=pltpu.HBM)],
        out_specs=[pl.BlockSpec(memory_space=pltpu.VMEM)] * (GROUPS + 2),
        out_shape=[part] * GROUPS + [edge] * 2,
        scratch_shapes=[
            pltpu.VMEM((2 * GROUPS, rows, LANES), jnp.float32),
            pltpu.SemaphoreType.DMA((3 * GROUPS + 2,)),
        ],
        compiler_params=pltpu.CompilerParams(vmem_limit_bytes=8 * MIB),
        cost_estimate=pl.CostEstimate(
            flops=0, bytes_accessed=rows * plan[1] * 32, transcendentals=0
        ),
        name="cut_early",
    )(pltpu.with_memory_space_constraint(signal, pltpu.HBM))


def fit_kernel(plan, fits, resids, ends, *refs):
    base, span, count = plan
    refs = list(refs)
    whole = ends and base == 0
    first_hbm, last_hbm, signal_ref, taps_hbm = refs[:4]
    refs = refs[4:]
    if ends:
        halo_refs, refs = refs[:2], refs[2:]
    if fits:
        fit_hbm, refs = refs[:2], refs[2:]
    if resids:
        outs, refs = refs[:GROUPS], refs[GROUPS:]
    x_ref, taps_ref, first_ref, last_ref, in_sems, side_sems = refs[:6]
    refs = refs[6:]
    if fits:
        fit_ref, out_sems = refs[:2]
        refs = refs[2:]
    if resids:
        resid_ref = refs[0]

    width = signal_ref.shape[1]
    per = count // GROUPS
    half = count // 2
    mine = lax.axis_index("series")
    begin = lax.axis_index(TIME) * width
    core = lax.axis_index("core")

    def place(n):
        return LANES + n * span + (2 * LANES * (n // half) if ends and not whole else 0)

    def source(n):
        return lax.rem(base + n * span, width) if ends and not whole else base + n * span

    def fetch(n):
        return pltpu.make_async_copy(
            signal_ref.at[:, aligned(source(n), span)],
            x_ref.at[:, aligned(place(n), span)],
            in_sems.at[n],
        )

    middle = place(half)
    tail = place(count - 1) + span
    after = (base + count * span) % width
    sides = [(first_hbm, first_ref), (last_hbm, last_ref), (taps_hbm, taps_ref)]
    if not whole:
        sides += [
            (signal_ref.at[:, pl.ds(base - LANES, LANES)], x_ref.at[:, pl.ds(0, LANES)]),
            (signal_ref.at[:, pl.ds(after, LANES)], x_ref.at[:, pl.ds(tail, LANES)]),
        ]
    if ends:
        at_left, at_right = (0, tail) if whole else (middle - LANES, middle - 2 * LANES)
        across = core * (at_left - at_right)
        sides += [
            (halo_refs[0], x_ref.at[:, aligned(at_right + across, LANES)]),
            (halo_refs[1], x_ref.at[:, aligned(at_left - across, LANES)]),
        ]
    sides = [pltpu.make_async_copy(a, b, side_sems.at[n]) for n, (a, b) in enumerate(sides)]
    for copy in sides:
        copy.start()
    for n in range(count):
        fetch(n).start()

    def give(n, kind):
        return pltpu.make_async_copy(
            fit_ref.at[kind, :, aligned(n * span, span)],
            fit_hbm[kind].at[:, aligned(source(n), span)],
            out_sems.at[kind, n],
        )

    for copy in sides:
        copy.wait()
    fetch(0).wait()

    first, last = ends_of(mine, first_ref, last_ref)

    def body(n, carry):
        k = (n // per + GROUPS - mine) % GROUPS

        @pl.when(n + 1 < count)
        def _():
            fetch(n + 1).wait()

        fit_span(
            span,
            begin + source(n),
            mine,
            (x_ref, place(n)),
            (taps_ref, first_ref, last_ref, first, last),
            (fit_ref, n * span) if fits else None,
            (resid_ref, k, n % per * span) if resids else None,
        )
        if fits:
            give(n, 0).start()
            give(n, 1).start()
        return carry

    lax.fori_loop(0, count, body, 0)
    if resids:
        for kk in range(GROUPS):
            outs[kk][...] = resid_ref[kk]
    if fits:
        for n in range(count):
            give(n, 0).wait()
            give(n, 1).wait()


def fit_steps(plan, first, last, signal, taps, fits, resids, halos):
    base, span, count = plan
    rows, width = signal.shape
    ends = halos is not None
    margins = 4 if ends and base else 2
    if not fits:
        taps = taps[:, :LANES]
    hbm = pl.BlockSpec(memory_space=pltpu.HBM)
    vmem = pl.BlockSpec(memory_space=pltpu.VMEM)
    loose = pl.BlockSpec(memory_space=pl.ANY)
    args = [pltpu.with_memory_space_constraint(a, pltpu.HBM) for a in (first, last, signal, taps)]
    args += list(halos or ())
    wide = jax.ShapeDtypeStruct((rows, width), jnp.float32)
    part = jax.ShapeDtypeStruct((rows, count // GROUPS * span), jnp.float32)
    scratch = [
        pltpu.VMEM((rows, count * span + margins * LANES), jnp.float32),
        pltpu.VMEM(taps.shape, taps.dtype),
        pltpu.SMEM(first.shape, jnp.int32),
        pltpu.SMEM(last.shape, jnp.int32),
        pltpu.SemaphoreType.DMA((count,)),
        pltpu.SemaphoreType.DMA((7,)),
    ]
    if fits:
        scratch += [
            pltpu.VMEM((2, rows, count * span), jnp.float32),
            pltpu.SemaphoreType.DMA((2, count)),
        ]
    if resids:
        scratch += [pltpu.VMEM((GROUPS, rows, count // GROUPS * span), jnp.float32)]
    return pl.pallas_call(
        functools.partial(fit_kernel, plan, fits, resids, ends),
        in_specs=[hbm] * 4 + [loose] * len(halos or ()),
        out_specs=[hbm] * (2 * fits) + [vmem] * (GROUPS * resids),
        out_shape=[wide] * (2 * fits) + [part] * (GROUPS * resids),
        scratch_shapes=scratch,
        compiler_params=pltpu.CompilerParams(vmem_limit_bytes=16 * MIB),
        cost_estimate=pl.CostEstimate(
            flops=count * 3 * rows * span * 256 * 4,
            bytes_accessed=count * rows * span * 4 * 4,
            transcendentals=0,
        ),
    )(*args)


def stacked(stack_ref, group, x):
    at = pl.multiple_of(group * ROWS, ROWS)
    a = x.astype(jnp.bfloat16)
    stack_ref[pl.ds(at, ROWS)] = a
    stack_ref[pl.ds(64 + at, ROWS)] = (x - a.astype(jnp.float32)).astype(jnp.bfloat16)


def product(stack_ref, so_far_ref, spread, out_ref):
    both = lax.dot_general(
        stack_ref[...],
        stack_ref[...],
        (((1,), (1,)), ((), ())),
        preferred_element_type=jnp.float32,
    )
    gram = both[:64] + both[64:]
    gram = gram + pltpu.roll(gram, 64, 1)
    low = lax.broadcasted_iota(jnp.int32, (8, LANES), 1) < 64
    for g in range(GROUPS):
        rows = jnp.where(low, gram[16 * g : 16 * g + 8], gram[16 * g + 8 : 16 * g + 16])
        if so_far_ref is not None:
            rows = rows + so_far_ref[g]
        if spread:
            for n in range(spread):
                out_ref[n, g] = rows
        else:
            out_ref[g] = rows


def raw_gram_kernel(plan, width, first_hbm, last_hbm, taps_hbm, *refs):
    base, span, _ = plan
    pieces, refs = refs[:GROUPS], refs[GROUPS:]
    out_ref, x_ref, resid_ref, stack_ref, taps_ref, first_ref, last_ref, sems = refs
    mine = lax.axis_index("series")
    mark = lax.axis_index(TIME) * width + base + mine * span
    copies = [
        pltpu.make_async_copy(a, b, sems.at[n])
        for n, (a, b) in enumerate(
            ((first_hbm, first_ref), (last_hbm, last_ref), (taps_hbm, taps_ref))
        )
    ]
    for copy in copies:
        copy.start()
    for k in range(GROUPS):
        x_ref[k, :, :LANES] = pieces[k][:, span:]
        x_ref[k, :, LANES:] = pieces[k][...]
    for copy in copies:
        copy.wait()

    def body(k, carry):
        group = (mine + GROUPS - k) % GROUPS
        first, last = ends_of(group, first_ref, last_ref)
        fit_span(
            span,
            mark,
            group,
            (x_ref.at[k], LANES),
            (taps_ref, first_ref, last_ref, first, last),
            None,
            (resid_ref, 0, 0),
        )
        stacked(stack_ref, group, resid_ref[0])
        return carry

    lax.fori_loop(0, GROUPS, body, 0)
    product(stack_ref, None, None, out_ref)


def raw_gram_of(plan, width, first, last, taps, pieces):
    _, span, _ = plan
    taps = taps[:, :LANES]
    hbm = pl.BlockSpec(memory_space=pltpu.HBM)
    vmem = pl.BlockSpec(memory_space=pltpu.VMEM)
    args = [pltpu.with_memory_space_constraint(a, pltpu.HBM) for a in (first, last, taps)]
    return pl.pallas_call(
        functools.partial(raw_gram_kernel, plan, width),
        in_specs=[hbm] * 3 + [vmem] * GROUPS,
        out_specs=vmem,
        out_shape=jax.ShapeDtypeStruct((GROUPS, 8, LANES), jnp.float32),
        scratch_shapes=[
            pltpu.VMEM((GROUPS, ROWS, span + 2 * LANES), jnp.float32),
            pltpu.VMEM((1, ROWS, span), jnp.float32),
            pltpu.VMEM((128, span), jnp.bfloat16),
            pltpu.VMEM(taps.shape, taps.dtype),
            pltpu.SMEM(first.shape, jnp.int32),
            pltpu.SMEM(last.shape, jnp.int32),
            pltpu.SemaphoreType.DMA((3,)),
        ],
        compiler_params=pltpu.CompilerParams(vmem_limit_bytes=16 * MIB),
        cost_estimate=pl.CostEstimate(
            flops=GROUPS * 3 * ROWS * span * 256 * 4,
            bytes_accessed=GROUPS * ROWS * span * 8,
            transcendentals=0,
        ),
    )(*args, *pieces)


def gram_kernel(add, spread, *refs):
    parts, refs = refs[:GROUPS], refs[GROUPS:]
    if add:
        so_far_ref, refs = refs[0], refs[1:]
    out_ref, stack_ref = refs
    mine = lax.axis_index("series")
    for k in range(GROUPS):
        stacked(stack_ref, (mine + GROUPS - k) % GROUPS, parts[k][...])
    product(stack_ref, so_far_ref if add else None, spread, out_ref)


def gram_of(parts, so_far, spread):
    width = parts[0].shape[1]
    vmem = pl.BlockSpec(memory_space=pltpu.VMEM)
    args = list(parts) + ([] if so_far is None else [so_far])
    lead = (spread,) if spread else ()
    return pl.pallas_call(
        functools.partial(gram_kernel, so_far is not None, spread),
        in_specs=[vmem] * len(args),
        out_specs=vmem,
        out_shape=jax.ShapeDtypeStruct((*lead, GROUPS, 8, LANES), jnp.float32),
        scratch_shapes=[pltpu.VMEM((128, width), jnp.bfloat16)],
        compiler_params=pltpu.CompilerParams(vmem_limit_bytes=12 * MIB),
        cost_estimate=pl.CostEstimate(
            flops=128 * 128 * width * 2, bytes_accessed=64 * width * 4, transcendentals=0
        ),
    )(*args)


def exchanged(pieces):
    parts = [pieces[0]]
    for k in (2, 1, 3):
        pairs = [(s, (s + k) % GROUPS) for s in range(GROUPS)]
        parts.append(lax.ppermute(pieces[k], "series", pairs))
    return [parts[0], parts[2], parts[1], parts[3]]


def shards(taps, signal, valid_start, valid_end):
    rows, width = signal.shape
    devices = lax.axis_size(TIME)
    taps = jnp.asarray(taps, jnp.bfloat16)
    mine = lax.axis_index("series")
    unit = width // 32
    early, mid = (2 * unit, 4 * unit, GROUPS), (18 * unit, 3 * unit, GROUPS)
    late, whole = (30 * unit, unit, GROUPS), (0, 4 * unit, 8)

    def fit(plan, fits, resids, halos=None):
        return fit_steps(plan, valid_start, valid_end, signal, taps, fits, resids, halos)

    first = lax.dynamic_slice_in_dim(valid_start, mine * rows, rows)[:, None]
    last = lax.dynamic_slice_in_dim(valid_end, mine * rows, rows)[:, None]
    shared = jnp.minimum(last, valid_end[None, :])
    shared = shared - jnp.maximum(first, valid_start[None, :])
    shared = shared.astype(jnp.float32)

    *pieces, near, far = cut_chunk(early, signal)
    parts = exchanged(pieces)
    parts_mid = exchanged(fit(mid, False, True))
    near = lax.ppermute(near, TIME, [(t, t ^ 1) for t in range(devices)])
    pairs = [(t, t + 1) for t in range(1, devices - 1, 2)]
    far = lax.ppermute(far, TIME, pairs + [(b, a) for a, b in pairs])
    halos = (near, far)
    gram = raw_gram_of(early, width, valid_start, valid_end, taps, parts)
    parts = exchanged(fit(late, False, True, halos))
    gram = gram_of(parts_mid, gram, None)
    copies = gram_of(parts, gram, devices // 2)
    copies = copies.reshape(devices * GROUPS, 4, LANES)
    copies = lax.all_to_all(copies, (*TIME[:2], "series", "core"), 0, 0, tiled=True)
    smooth, slope = fit(whole, True, False, halos)
    own = jnp.sum(copies, axis=0)
    other = lax.ppermute(own, "core", [(0, 1), (1, 0)])
    lead = lax.axis_index("core") == 0
    p, q = jnp.where(lead, own, other), jnp.where(lead, other, own)
    gram = jnp.concatenate([p[:, :64], q[:, :64], p[:, 64:], q[:, 64:]], axis=0)
    return smooth, slope, gram / shared


def solution(mesh):
    split = Mesh(mesh.devices.reshape(4, 4, 2, GROUPS), (*TIME, "series"))
    return jax.shard_map(
        functools.partial(shards, filter_matrix()),
        mesh=split,
        in_specs=(P("series", TIME), P(), P()),
        out_specs=(P("series", TIME), P("series", TIME), P("series", None)),
        check_vma=False,
    )
```

```python
import functools

import jax
import jax.numpy as jnp
import numpy as np
from jax import lax
from jax.experimental import pallas as pl
from jax.experimental.pallas import tpu as pltpu
from jax.sharding import Mesh
from jax.sharding import PartitionSpec as P


HALF = 16
TAPS = 2 * HALF + 1
ROWS = 16
GROUPS = 4
LANES = 128
TIME = ("y", "z", "core")
MIB = 1 << 20

SECOND = float(sum(j * j for j in range(-HALF, HALF + 1)))
CENTRE_SQ = SECOND / TAPS
FOURTH = float(sum((j * j - CENTRE_SQ) ** 2 for j in range(-HALF, HALF + 1)))
SMOOTH_SCALE = 2048.0 / 2387.0
SLOPE_SCALE = HALF * 16.0 / SECOND


def filter_matrix():
    place = np.concatenate([np.arange(128), np.arange(128, 192), np.arange(-64, 0)])
    j = place[:, None] - np.arange(LANES)[None, :]
    near = np.abs(j) <= HALF
    smooth = np.where(near, (163 - j * j) / 2048.0, 0.0)
    slope = np.where(near, j / 16.0, 0.0)
    return np.concatenate([smooth, slope], axis=1).astype(np.float32)


def thirds(x):
    a = x.astype(jnp.bfloat16)
    rest = x - a.astype(jnp.float32)
    b = rest.astype(jnp.bfloat16)
    c = (rest - b.astype(jnp.float32)).astype(jnp.bfloat16)
    return a, b, c


def aligned(start, size):
    return pl.ds(pl.multiple_of(start, LANES), size)


def ends_of(group, first_ref, last_ref):
    row = lax.broadcasted_iota(jnp.int32, (ROWS, LANES), 0)
    first = jnp.zeros((ROWS, LANES), jnp.int32)
    last = jnp.zeros((ROWS, LANES), jnp.int32)
    for r in range(ROWS):
        first = jnp.where(row == r, first_ref[group * ROWS + r], first)
        last = jnp.where(row == r, last_ref[group * ROWS + r], last)
    return first, last


def fit_span(span, mark, group, samples, tables, to_fit, to_resid):
    blocks = span // LANES
    height = ROWS * blocks
    x_ref, at = samples
    taps_ref, first_ref, last_ref, first, last = tables
    if to_fit:
        fit_ref, out_at = to_fit
    if to_resid:
        resid_ref, k, piece_at = to_resid
    lane = lax.broadcasted_iota(jnp.int32, (ROWS, LANES), 1)
    row = lax.broadcasted_iota(jnp.int32, (ROWS, LANES), 0)
    low = lane < 64

    x = x_ref[:, aligned(at - LANES, span + 2 * LANES)]
    parts = thirds(x)

    def cut(m, b):
        return parts[m][:, b * LANES : (b + 1) * LANES]

    rows = [
        jnp.concatenate([cut(m, b + 1), jnp.where(low, cut(m, b + 2), cut(m, b))], axis=1)
        for m in range(3)
        for b in range(blocks)
    ]
    fit = jnp.dot(
        jnp.concatenate(rows, axis=0), taps_ref[...], preferred_element_type=jnp.float32
    )
    fit = fit[:height] + (fit[height : 2 * height] + fit[2 * height :])
    since = first - mark
    until = last - mark
    for b in range(blocks):
        part = fit[b * ROWS : (b + 1) * ROWS]
        moment = lane + b * LANES
        inside = (moment >= since) & (moment < until)
        smooth = part[:, :LANES] * SMOOTH_SCALE
        if to_fit:
            to = aligned(out_at + b * LANES, LANES)
            fit_ref[0, :, to] = jnp.where(inside, smooth, 0.0)
            fit_ref[1, :, to] = jnp.where(inside, part[:, LANES:] * SLOPE_SCALE, 0.0)
        if to_resid:
            resid = x[:, (b + 1) * LANES : (b + 2) * LANES] - smooth
            resid_ref[k, :, aligned(piece_at + b * LANES, LANES)] = jnp.where(inside, resid, 0.0)

    def starts_here(a):
        return (a > mark - HALF) & (a < mark + span)

    def stops_here(z):
        return (z > mark) & (z < mark + span + HALF)

    holds = False
    for r in range(ROWS):
        holds = holds | starts_here(first_ref[group * ROWS + r])
        holds = holds | stops_here(last_ref[group * ROWS + r])

    @pl.when(holds)
    def _():
        def mend(r, left, centre, side):
            b = (left + LANES) // LANES - 1
            v = x_ref[:, aligned(at + b * LANES, 2 * LANES)]
            j = lax.broadcasted_iota(jnp.int32, (ROWS, 2 * LANES), 1) + (b * LANES - centre)
            w = jnp.where((j >= -HALF) & (j <= HALF), v, 0.0)
            f = jnp.clip(j, -HALF, HALF).astype(jnp.float32)
            level = jnp.sum(w, axis=1, keepdims=True) * (1.0 / TAPS)
            tilt = jnp.sum(w * f, axis=1, keepdims=True) * (1.0 / SECOND)
            curve = f * f - CENTRE_SQ
            bend = jnp.sum(w * curve, axis=1, keepdims=True) * (1.0 / FOURTH)
            smooth = level + tilt * f + bend * curve
            slope = HALF * (tilt + 2.0 * f * bend)
            held = (j * side >= 1) & (j * side <= HALF)
            for h in range(2):

                @pl.when((b + h >= 0) & (b + h < blocks))
                def _():
                    part = slice(h * LANES, (h + 1) * LANES)
                    to = held[:, part] & (row == r)
                    if to_fit:
                        at_fit = aligned(out_at + (b + h) * LANES, LANES)
                        fit_ref[0, :, at_fit] = jnp.where(
                            to, smooth[:, part], fit_ref[0, :, at_fit]
                        )
                        fit_ref[1, :, at_fit] = jnp.where(to, slope[:, part], fit_ref[1, :, at_fit])
                    if to_resid:
                        at_piece = aligned(piece_at + (b + h) * LANES, LANES)
                        resid_ref[k, :, at_piece] = jnp.where(
                            to, v[:, part] - smooth[:, part], resid_ref[k, :, at_piece]
                        )

        def series(r, carry):
            a = first_ref[group * ROWS + r]
            z = last_ref[group * ROWS + r]

            @pl.when(starts_here(a))
            def _():
                mend(r, a - mark, a - mark + HALF, -1)

            @pl.when(stops_here(z))
            def _():
                mend(r, z - mark - TAPS, z - mark - HALF - 1, 1)

            return carry

        def bunch(q, carry):
            some = False
            for r in range(4):
                some = some | starts_here(first_ref[group * ROWS + 4 * q + r])
                some = some | stops_here(last_ref[group * ROWS + 4 * q + r])

            @pl.when(some)
            def _():
                lax.fori_loop(4 * q, 4 * q + 4, series, 0)

            return carry

        lax.fori_loop(0, ROWS // 4, bunch, 0)


def cut_kernel(plan, signal_ref, *refs):
    base, span, _ = plan
    pieces, edges, (side_ref, sems) = refs[:GROUPS], refs[GROUPS : GROUPS + 2], refs[-2:]
    width = signal_ref.shape[1]
    mine = lax.axis_index("series")
    core = lax.axis_index("core")
    copies = []

    def move(start, size, to):
        copy = pltpu.make_async_copy(
            signal_ref.at[:, aligned(start, size)], to, sems.at[len(copies)]
        )
        copy.start()
        copies.append(copy)

    for k in (2, 1, 3, 0):
        start = base + (mine + k) % GROUPS * span
        move(start - LANES, LANES, side_ref.at[2 * k])
        move(start + span, LANES, side_ref.at[2 * k + 1])
        move(start, span, pieces[k].at[:, pl.ds(0, span)])
    move((1 - core) * (width - LANES), LANES, edges[0])
    move(core * (width - LANES), LANES, edges[1])
    for copy in copies:
        copy.wait()
    low = lax.broadcasted_iota(jnp.int32, edges[0].shape, 1) < 64
    for k in range(GROUPS):
        pieces[k][:, span:] = jnp.where(low, side_ref[2 * k + 1], side_ref[2 * k])


def cut_chunk(plan, signal):
    rows, _ = signal.shape
    part = jax.ShapeDtypeStruct((rows, plan[1] + LANES), jnp.float32)
    edge = jax.ShapeDtypeStruct((rows, LANES), jnp.float32)
    return pl.pallas_call(
        functools.partial(cut_kernel, plan),
        in_specs=[pl.BlockSpec(memory_space=pltpu.HBM)],
        out_specs=[pl.BlockSpec(memory_space=pltpu.VMEM)] * (GROUPS + 2),
        out_shape=[part] * GROUPS + [edge] * 2,
        scratch_shapes=[
            pltpu.VMEM((2 * GROUPS, rows, LANES), jnp.float32),
            pltpu.SemaphoreType.DMA((3 * GROUPS + 2,)),
        ],
        compiler_params=pltpu.CompilerParams(vmem_limit_bytes=8 * MIB),
        cost_estimate=pl.CostEstimate(
            flops=0, bytes_accessed=rows * plan[1] * 32, transcendentals=0
        ),
        name="cut_early",
    )(pltpu.with_memory_space_constraint(signal, pltpu.HBM))


def fit_kernel(plan, fits, resids, ends, chain, *refs):
    base, span, count = plan
    refs = list(refs)
    first_hbm, last_hbm, signal_ref, taps_hbm = refs[:4]
    refs = refs[4:]
    if ends:
        halo_refs, refs = refs[:2], refs[2:]
    if chain:
        refs = refs[2:]
    if fits:
        fit_hbm, refs = refs[:2], refs[2:]
    if resids:
        outs, refs = refs[:GROUPS], refs[GROUPS:]
    x_ref, taps_ref, first_ref, last_ref, in_sems, side_sems = refs[:6]
    refs = refs[6:]
    if fits:
        fit_ref, out_sems = refs[:2]
        refs = refs[2:]
    if resids:
        resid_ref = refs[0]

    width = signal_ref.shape[1]
    per = max(count // GROUPS, 1)
    seam = (width - base) // span
    mine = lax.axis_index("series")
    begin = lax.axis_index(TIME) * width
    core = lax.axis_index("core")

    def place(n):
        at = LANES + n * span
        if not ends:
            return at
        if isinstance(n, int):
            return at + 2 * LANES * (n >= seam)
        return at + jnp.where(n >= seam, 2 * LANES, 0)

    def source(n):
        return lax.rem(base + n * span, width) if ends else base + n * span

    def fetch(n):
        return pltpu.make_async_copy(
            signal_ref.at[:, aligned(source(n), span)],
            x_ref.at[:, aligned(place(n), span)],
            in_sems.at[n],
        )

    middle = place(seam)
    tail = place(count - 1) + span
    after = (base + count * span) % width
    sides = [
        (first_hbm, first_ref),
        (last_hbm, last_ref),
        (taps_hbm, taps_ref),
        (signal_ref.at[:, pl.ds(base - LANES, LANES)], x_ref.at[:, pl.ds(0, LANES)]),
        (signal_ref.at[:, pl.ds(after, LANES)], x_ref.at[:, pl.ds(tail, LANES)]),
    ]
    if ends:
        at_left, at_right = middle - LANES, middle - 2 * LANES
        across = core * (at_left - at_right)
        sides += [
            (halo_refs[0], x_ref.at[:, aligned(at_right + across, LANES)]),
            (halo_refs[1], x_ref.at[:, aligned(at_left - across, LANES)]),
        ]
    sides = [pltpu.make_async_copy(a, b, side_sems.at[n]) for n, (a, b) in enumerate(sides)]
    for copy in sides:
        copy.start()
    for n in range(count):
        fetch(n).start()

    def give(n, kind):
        return pltpu.make_async_copy(
            fit_ref.at[kind, :, aligned(n * span, span)],
            fit_hbm[kind].at[:, aligned(source(n), span)],
            out_sems.at[kind, n],
        )

    for copy in sides:
        copy.wait()
    fetch(0).wait()

    first, last = ends_of(mine, first_ref, last_ref)

    def body(n, carry):
        k = (n // per + GROUPS - mine) % GROUPS

        @pl.when(n + 1 < count)
        def _():
            fetch(n + 1).wait()

        fit_span(
            span,
            begin + source(n),
            mine,
            (x_ref, place(n)),
            (taps_ref, first_ref, last_ref, first, last),
            (fit_ref, n * span) if fits else None,
            (resid_ref, k, n % per * span) if resids else None,
        )
        if fits:
            give(n, 0).start()
            give(n, 1).start()
        return carry

    lax.fori_loop(0, count, body, 0)
    if resids:
        for kk in range(GROUPS):
            outs[kk][...] = resid_ref[kk]
    if fits:
        for n in range(count):
            give(n, 0).wait()
            give(n, 1).wait()


def fit_steps(plan, first, last, signal, taps, fits, resids, halos, held):
    _, span, count = plan
    rows, width = signal.shape
    ends = halos is not None
    margins = 4 if ends else 2
    if not fits:
        taps = taps[:, :LANES]
    hbm = pl.BlockSpec(memory_space=pltpu.HBM)
    vmem = pl.BlockSpec(memory_space=pltpu.VMEM)
    loose = pl.BlockSpec(memory_space=pl.ANY)
    args = [pltpu.with_memory_space_constraint(a, pltpu.HBM) for a in (first, last, signal, taps)]
    args += list(halos or ()) + list(held or ())
    aliases = {len(args) - 2: 0, len(args) - 1: 1} if held else {}
    wide = jax.ShapeDtypeStruct((rows, width), jnp.float32)
    part = jax.ShapeDtypeStruct((rows, count // GROUPS * span), jnp.float32)
    scratch = [
        pltpu.VMEM((rows, count * span + margins * LANES), jnp.float32),
        pltpu.VMEM(taps.shape, taps.dtype),
        pltpu.SMEM(first.shape, jnp.int32),
        pltpu.SMEM(last.shape, jnp.int32),
        pltpu.SemaphoreType.DMA((count,)),
        pltpu.SemaphoreType.DMA((7,)),
    ]
    if fits:
        scratch += [
            pltpu.VMEM((2, rows, count * span), jnp.float32),
            pltpu.SemaphoreType.DMA((2, count)),
        ]
    if resids:
        scratch += [pltpu.VMEM((GROUPS, rows, count // GROUPS * span), jnp.float32)]
    return pl.pallas_call(
        functools.partial(fit_kernel, plan, fits, resids, ends, bool(held)),
        in_specs=[hbm] * 4 + [loose] * len(halos or ()) + [hbm] * len(held or ()),
        out_specs=[hbm] * (2 * fits) + [vmem] * (GROUPS * resids),
        out_shape=[wide] * (2 * fits) + [part] * (GROUPS * resids),
        scratch_shapes=scratch,
        input_output_aliases=aliases,
        compiler_params=pltpu.CompilerParams(vmem_limit_bytes=16 * MIB),
        cost_estimate=pl.CostEstimate(
            flops=count * 3 * rows * span * 256 * 4,
            bytes_accessed=count * rows * span * 4 * 4,
            transcendentals=0,
        ),
    )(*args)


def stacked(stack_ref, group, x):
    at = pl.multiple_of(group * ROWS, ROWS)
    a = x.astype(jnp.bfloat16)
    stack_ref[pl.ds(at, ROWS)] = a
    stack_ref[pl.ds(64 + at, ROWS)] = (x - a.astype(jnp.float32)).astype(jnp.bfloat16)


def product(stack_ref, so_far_ref, spread, out_ref):
    both = lax.dot_general(
        stack_ref[...],
        stack_ref[...],
        (((1,), (1,)), ((), ())),
        preferred_element_type=jnp.float32,
    )
    gram = both[:64] + both[64:]
    gram = gram + pltpu.roll(gram, 64, 1)
    low = lax.broadcasted_iota(jnp.int32, (8, LANES), 1) < 64
    for g in range(GROUPS):
        rows = jnp.where(low, gram[16 * g : 16 * g + 8], gram[16 * g + 8 : 16 * g + 16])
        if so_far_ref is not None:
            rows = rows + so_far_ref[g]
        if spread:
            for n in range(spread):
                out_ref[n, g] = rows
        else:
            out_ref[g] = rows


def raw_gram_kernel(plan, width, first_hbm, last_hbm, taps_hbm, *refs):
    base, span, _ = plan
    pieces, refs = refs[:GROUPS], refs[GROUPS:]
    out_ref, x_ref, resid_ref, stack_ref, taps_ref, first_ref, last_ref, sems = refs
    mine = lax.axis_index("series")
    mark = lax.axis_index(TIME) * width + base + mine * span
    copies = [
        pltpu.make_async_copy(a, b, sems.at[n])
        for n, (a, b) in enumerate(
            ((first_hbm, first_ref), (last_hbm, last_ref), (taps_hbm, taps_ref))
        )
    ]
    for copy in copies:
        copy.start()
    for k in range(GROUPS):
        x_ref[k, :, :LANES] = pieces[k][:, span:]
        x_ref[k, :, LANES:] = pieces[k][...]
    for copy in copies:
        copy.wait()

    def body(k, carry):
        group = (mine + GROUPS - k) % GROUPS
        first, last = ends_of(group, first_ref, last_ref)
        fit_span(
            span,
            mark,
            group,
            (x_ref.at[k], LANES),
            (taps_ref, first_ref, last_ref, first, last),
            None,
            (resid_ref, 0, 0),
        )
        stacked(stack_ref, group, resid_ref[0])
        return carry

    lax.fori_loop(0, GROUPS, body, 0)
    product(stack_ref, None, None, out_ref)


def raw_gram_of(plan, width, first, last, taps, pieces):
    _, span, _ = plan
    taps = taps[:, :LANES]
    hbm = pl.BlockSpec(memory_space=pltpu.HBM)
    vmem = pl.BlockSpec(memory_space=pltpu.VMEM)
    args = [pltpu.with_memory_space_constraint(a, pltpu.HBM) for a in (first, last, taps)]
    return pl.pallas_call(
        functools.partial(raw_gram_kernel, plan, width),
        in_specs=[hbm] * 3 + [vmem] * GROUPS,
        out_specs=vmem,
        out_shape=jax.ShapeDtypeStruct((GROUPS, 8, LANES), jnp.float32),
        scratch_shapes=[
            pltpu.VMEM((GROUPS, ROWS, span + 2 * LANES), jnp.float32),
            pltpu.VMEM((1, ROWS, span), jnp.float32),
            pltpu.VMEM((128, span), jnp.bfloat16),
            pltpu.VMEM(taps.shape, taps.dtype),
            pltpu.SMEM(first.shape, jnp.int32),
            pltpu.SMEM(last.shape, jnp.int32),
            pltpu.SemaphoreType.DMA((3,)),
        ],
        compiler_params=pltpu.CompilerParams(vmem_limit_bytes=16 * MIB),
        cost_estimate=pl.CostEstimate(
            flops=GROUPS * 3 * ROWS * span * 256 * 4,
            bytes_accessed=GROUPS * ROWS * span * 8,
            transcendentals=0,
        ),
    )(*args, *pieces)


def gram_kernel(add, spread, *refs):
    parts, refs = refs[:GROUPS], refs[GROUPS:]
    if add:
        so_far_ref, refs = refs[0], refs[1:]
    out_ref, stack_ref = refs
    mine = lax.axis_index("series")
    for k in range(GROUPS):
        stacked(stack_ref, (mine + GROUPS - k) % GROUPS, parts[k][...])
    product(stack_ref, so_far_ref if add else None, spread, out_ref)


def gram_of(parts, so_far, spread):
    width = parts[0].shape[1]
    vmem = pl.BlockSpec(memory_space=pltpu.VMEM)
    args = list(parts) + ([] if so_far is None else [so_far])
    lead = (spread,) if spread else ()
    return pl.pallas_call(
        functools.partial(gram_kernel, so_far is not None, spread),
        in_specs=[vmem] * len(args),
        out_specs=vmem,
        out_shape=jax.ShapeDtypeStruct((*lead, GROUPS, 8, LANES), jnp.float32),
        scratch_shapes=[pltpu.VMEM((128, width), jnp.bfloat16)],
        compiler_params=pltpu.CompilerParams(vmem_limit_bytes=12 * MIB),
        cost_estimate=pl.CostEstimate(
            flops=128 * 128 * width * 2, bytes_accessed=64 * width * 4, transcendentals=0
        ),
    )(*args)


def exchanged(pieces):
    parts = [pieces[0]]
    for k in (2, 1, 3):
        pairs = [(s, (s + k) % GROUPS) for s in range(GROUPS)]
        parts.append(lax.ppermute(pieces[k], "series", pairs))
    return [parts[0], parts[2], parts[1], parts[3]]


def shards(taps, signal, valid_start, valid_end):
    rows, width = signal.shape
    devices = lax.axis_size(TIME)
    taps = jnp.asarray(taps, jnp.bfloat16)
    mine = lax.axis_index("series")
    unit = width // 32
    early, mid = (2 * unit, 4 * unit, GROUPS), (18 * unit, 3 * unit, GROUPS)
    late = (30 * unit, unit, GROUPS)
    some, rest = (22 * unit, 4 * unit, 2), (30 * unit, 2 * unit, 12)

    def fit(plan, fits, resids, halos=None, held=None):
        return fit_steps(plan, valid_start, valid_end, signal, taps, fits, resids, halos, held)

    first = lax.dynamic_slice_in_dim(valid_start, mine * rows, rows)[:, None]
    last = lax.dynamic_slice_in_dim(valid_end, mine * rows, rows)[:, None]
    shared = jnp.minimum(last, valid_end[None, :])
    shared = shared - jnp.maximum(first, valid_start[None, :])
    shared = shared.astype(jnp.float32)

    *pieces, near, far = cut_chunk(early, signal)
    parts = exchanged(pieces)
    parts_mid = exchanged(fit(mid, False, True))
    near = lax.ppermute(near, TIME, [(t, t ^ 1) for t in range(devices)])
    pairs = [(t, t + 1) for t in range(1, devices - 1, 2)]
    far = lax.ppermute(far, TIME, pairs + [(b, a) for a, b in pairs])
    halos = (near, far)
    gram = raw_gram_of(early, width, valid_start, valid_end, taps, parts)
    parts = exchanged(fit(late, False, True, halos))
    held = fit(some, True, False)
    gram = gram_of(parts_mid, gram, None)
    copies = gram_of(parts, gram, devices // 2)
    copies = copies.reshape(devices * GROUPS, 4, LANES)
    copies = lax.all_to_all(copies, (*TIME[:2], "series", "core"), 0, 0, tiled=True)
    smooth, slope = fit(rest, True, False, halos, held)
    own = jnp.sum(copies, axis=0)
    other = lax.ppermute(own, "core", [(0, 1), (1, 0)])
    lead = lax.axis_index("core") == 0
    p, q = jnp.where(lead, own, other), jnp.where(lead, other, own)
    gram = jnp.concatenate([p[:, :64], q[:, :64], p[:, 64:], q[:, 64:]], axis=0)
    return smooth, slope, gram / shared


def solution(mesh):
    split = Mesh(mesh.devices.reshape(4, 4, 2, GROUPS), (*TIME, "series"))
    return jax.shard_map(
        functools.partial(shards, filter_matrix()),
        mesh=split,
        in_specs=(P("series", TIME), P(), P()),
        out_specs=(P("series", TIME), P("series", TIME), P("series", None)),
        check_vma=False,
    )
```

```python
import functools

import jax
import jax.numpy as jnp
import numpy as np
from jax import lax
from jax.experimental import pallas as pl
from jax.experimental.pallas import tpu as pltpu
from jax.sharding import Mesh
from jax.sharding import PartitionSpec as P


HALF = 16
TAPS = 2 * HALF + 1
ROWS = 16
GROUPS = 4
LANES = 128
TIME = ("y", "z", "core")
MIB = 1 << 20

SECOND = float(sum(j * j for j in range(-HALF, HALF + 1)))
CENTRE_SQ = SECOND / TAPS
FOURTH = float(sum((j * j - CENTRE_SQ) ** 2 for j in range(-HALF, HALF + 1)))
SMOOTH_SCALE = 2048.0 / 2387.0
SLOPE_SCALE = HALF * 16.0 / SECOND


def filter_matrix():
    place = np.concatenate([np.arange(128), np.arange(128, 192), np.arange(-64, 0)])
    j = place[:, None] - np.arange(LANES)[None, :]
    near = np.abs(j) <= HALF
    smooth = np.where(near, (163 - j * j) / 2048.0, 0.0)
    slope = np.where(near, j / 16.0, 0.0)
    return np.concatenate([smooth, slope], axis=1).astype(np.float32)


def thirds(x):
    a = x.astype(jnp.bfloat16)
    rest = x - a.astype(jnp.float32)
    b = rest.astype(jnp.bfloat16)
    c = (rest - b.astype(jnp.float32)).astype(jnp.bfloat16)
    return a, b, c


def aligned(start, size):
    return pl.ds(pl.multiple_of(start, LANES), size)


def ends_of(group, first_ref, last_ref):
    row = lax.broadcasted_iota(jnp.int32, (ROWS, LANES), 0)
    first = jnp.zeros((ROWS, LANES), jnp.int32)
    last = jnp.zeros((ROWS, LANES), jnp.int32)
    for r in range(ROWS):
        first = jnp.where(row == r, first_ref[group * ROWS + r], first)
        last = jnp.where(row == r, last_ref[group * ROWS + r], last)
    return first, last


def fit_span(span, mark, group, samples, tables, to_fit, to_resid):
    blocks = span // LANES
    height = ROWS * blocks
    x_ref, at = samples
    taps_ref, first_ref, last_ref, first, last = tables
    if to_fit:
        fit_ref, out_at = to_fit
    if to_resid:
        resid_ref, k, piece_at = to_resid
    lane = lax.broadcasted_iota(jnp.int32, (ROWS, LANES), 1)
    row = lax.broadcasted_iota(jnp.int32, (ROWS, LANES), 0)
    low = lane < 64

    x = x_ref[:, aligned(at - LANES, span + 2 * LANES)]
    parts = thirds(x)

    def cut(m, b):
        return parts[m][:, b * LANES : (b + 1) * LANES]

    rows = [
        jnp.concatenate([cut(m, b + 1), jnp.where(low, cut(m, b + 2), cut(m, b))], axis=1)
        for m in range(3)
        for b in range(blocks)
    ]
    fit = jnp.dot(
        jnp.concatenate(rows, axis=0), taps_ref[...], preferred_element_type=jnp.float32
    )
    fit = fit[:height] + (fit[height : 2 * height] + fit[2 * height :])
    since = first - mark
    until = last - mark
    for b in range(blocks):
        part = fit[b * ROWS : (b + 1) * ROWS]
        moment = lane + b * LANES
        inside = (moment >= since) & (moment < until)
        smooth = part[:, :LANES] * SMOOTH_SCALE
        if to_fit:
            to = aligned(out_at + b * LANES, LANES)
            fit_ref[0, :, to] = jnp.where(inside, smooth, 0.0)
            fit_ref[1, :, to] = jnp.where(inside, part[:, LANES:] * SLOPE_SCALE, 0.0)
        if to_resid:
            resid = x[:, (b + 1) * LANES : (b + 2) * LANES] - smooth
            resid_ref[k, :, aligned(piece_at + b * LANES, LANES)] = jnp.where(inside, resid, 0.0)

    def starts_here(a):
        return (a > mark - HALF) & (a < mark + span)

    def stops_here(z):
        return (z > mark) & (z < mark + span + HALF)

    holds = False
    for r in range(ROWS):
        holds = holds | starts_here(first_ref[group * ROWS + r])
        holds = holds | stops_here(last_ref[group * ROWS + r])

    @pl.when(holds)
    def _():
        def mend(r, left, centre, side):
            b = (left + LANES) // LANES - 1
            v = x_ref[:, aligned(at + b * LANES, 2 * LANES)]
            j = lax.broadcasted_iota(jnp.int32, (ROWS, 2 * LANES), 1) + (b * LANES - centre)
            w = jnp.where((j >= -HALF) & (j <= HALF), v, 0.0)
            f = jnp.clip(j, -HALF, HALF).astype(jnp.float32)
            level = jnp.sum(w, axis=1, keepdims=True) * (1.0 / TAPS)
            tilt = jnp.sum(w * f, axis=1, keepdims=True) * (1.0 / SECOND)
            curve = f * f - CENTRE_SQ
            bend = jnp.sum(w * curve, axis=1, keepdims=True) * (1.0 / FOURTH)
            smooth = level + tilt * f + bend * curve
            slope = HALF * (tilt + 2.0 * f * bend)
            held = (j * side >= 1) & (j * side <= HALF)
            for h in range(2):

                @pl.when((b + h >= 0) & (b + h < blocks))
                def _():
                    part = slice(h * LANES, (h + 1) * LANES)
                    to = held[:, part] & (row == r)
                    if to_fit:
                        at_fit = aligned(out_at + (b + h) * LANES, LANES)
                        fit_ref[0, :, at_fit] = jnp.where(
                            to, smooth[:, part], fit_ref[0, :, at_fit]
                        )
                        fit_ref[1, :, at_fit] = jnp.where(to, slope[:, part], fit_ref[1, :, at_fit])
                    if to_resid:
                        at_piece = aligned(piece_at + (b + h) * LANES, LANES)
                        resid_ref[k, :, at_piece] = jnp.where(
                            to, v[:, part] - smooth[:, part], resid_ref[k, :, at_piece]
                        )

        def series(r, carry):
            a = first_ref[group * ROWS + r]
            z = last_ref[group * ROWS + r]

            @pl.when(starts_here(a))
            def _():
                mend(r, a - mark, a - mark + HALF, -1)

            @pl.when(stops_here(z))
            def _():
                mend(r, z - mark - TAPS, z - mark - HALF - 1, 1)

            return carry

        def bunch(q, carry):
            some = False
            for r in range(4):
                some = some | starts_here(first_ref[group * ROWS + 4 * q + r])
                some = some | stops_here(last_ref[group * ROWS + 4 * q + r])

            @pl.when(some)
            def _():
                lax.fori_loop(4 * q, 4 * q + 4, series, 0)

            return carry

        lax.fori_loop(0, ROWS // 4, bunch, 0)


def cut_kernel(plan, signal_ref, *refs):
    base, span, _ = plan
    pieces, edges, (side_ref, sems) = refs[:GROUPS], refs[GROUPS : GROUPS + 2], refs[-2:]
    width = signal_ref.shape[1]
    mine = lax.axis_index("series")
    core = lax.axis_index("core")
    copies = []

    def move(start, size, to):
        copy = pltpu.make_async_copy(
            signal_ref.at[:, aligned(start, size)], to, sems.at[len(copies)]
        )
        copy.start()
        copies.append(copy)

    for k in (2, 1, 3, 0):
        start = base + (mine + k) % GROUPS * span
        move(start - LANES, LANES, side_ref.at[2 * k])
        move(start + span, LANES, side_ref.at[2 * k + 1])
        move(start, span, pieces[k].at[:, pl.ds(0, span)])
    move((1 - core) * (width - LANES), LANES, edges[0])
    move(core * (width - LANES), LANES, edges[1])
    for copy in copies:
        copy.wait()
    low = lax.broadcasted_iota(jnp.int32, edges[0].shape, 1) < 64
    for k in range(GROUPS):
        pieces[k][:, span:] = jnp.where(low, side_ref[2 * k + 1], side_ref[2 * k])


def cut_chunk(plan, signal):
    rows, _ = signal.shape
    part = jax.ShapeDtypeStruct((rows, plan[1] + LANES), jnp.float32)
    edge = jax.ShapeDtypeStruct((rows, LANES), jnp.float32)
    return pl.pallas_call(
        functools.partial(cut_kernel, plan),
        in_specs=[pl.BlockSpec(memory_space=pltpu.HBM)],
        out_specs=[pl.BlockSpec(memory_space=pltpu.VMEM)] * (GROUPS + 2),
        out_shape=[part] * GROUPS + [edge] * 2,
        scratch_shapes=[
            pltpu.VMEM((2 * GROUPS, rows, LANES), jnp.float32),
            pltpu.SemaphoreType.DMA((3 * GROUPS + 2,)),
        ],
        compiler_params=pltpu.CompilerParams(vmem_limit_bytes=8 * MIB),
        cost_estimate=pl.CostEstimate(
            flops=0, bytes_accessed=rows * plan[1] * 32, transcendentals=0
        ),
        name="cut_early",
    )(pltpu.with_memory_space_constraint(signal, pltpu.HBM))


def fit_kernel(plan, fits, resids, ends, *refs):
    base, span, count = plan
    refs = list(refs)
    whole = ends and base == 0
    first_hbm, last_hbm, signal_ref, taps_hbm = refs[:4]
    refs = refs[4:]
    if ends:
        halo_refs, refs = refs[:2], refs[2:]
    if fits:
        fit_hbm, refs = refs[:2], refs[2:]
    if resids:
        outs, refs = refs[:GROUPS], refs[GROUPS:]
    x_ref, taps_ref, first_ref, last_ref, in_sems, side_sems = refs[:6]
    refs = refs[6:]
    if fits:
        fit_ref, out_sems = refs[:2]
        refs = refs[2:]
    if resids:
        resid_ref = refs[0]

    width = signal_ref.shape[1]
    per = count // GROUPS
    half = count // 2
    mine = lax.axis_index("series")
    begin = lax.axis_index(TIME) * width
    core = lax.axis_index("core")

    def place(n):
        return LANES + n * span + (2 * LANES * (n // half) if ends and not whole else 0)

    def source(n):
        return lax.rem(base + n * span, width) if ends and not whole else base + n * span

    def fetch(n):
        return pltpu.make_async_copy(
            signal_ref.at[:, aligned(source(n), span)],
            x_ref.at[:, aligned(place(n), span)],
            in_sems.at[n],
        )

    middle = place(half)
    tail = place(count - 1) + span
    after = (base + count * span) % width
    sides = [(first_hbm, first_ref), (last_hbm, last_ref), (taps_hbm, taps_ref)]
    if not whole:
        sides += [
            (signal_ref.at[:, pl.ds(base - LANES, LANES)], x_ref.at[:, pl.ds(0, LANES)]),
            (signal_ref.at[:, pl.ds(after, LANES)], x_ref.at[:, pl.ds(tail, LANES)]),
        ]
    if ends:
        at_left, at_right = (0, tail) if whole else (middle - LANES, middle - 2 * LANES)
        across = core * (at_left - at_right)
        sides += [
            (halo_refs[0], x_ref.at[:, aligned(at_right + across, LANES)]),
            (halo_refs[1], x_ref.at[:, aligned(at_left - across, LANES)]),
        ]
    sides = [pltpu.make_async_copy(a, b, side_sems.at[n]) for n, (a, b) in enumerate(sides)]
    for copy in sides:
        copy.start()
    for n in range(count):
        fetch(n).start()

    def give(n, kind):
        return pltpu.make_async_copy(
            fit_ref.at[kind, :, aligned(n * span, span)],
            fit_hbm[kind].at[:, aligned(source(n), span)],
            out_sems.at[kind, n],
        )

    for copy in sides:
        copy.wait()
    fetch(0).wait()

    first, last = ends_of(mine, first_ref, last_ref)

    def body(n, carry):
        k = (n // per + GROUPS - mine) % GROUPS

        @pl.when(n + 1 < count)
        def _():
            fetch(n + 1).wait()

        fit_span(
            span,
            begin + source(n),
            mine,
            (x_ref, place(n)),
            (taps_ref, first_ref, last_ref, first, last),
            (fit_ref, n * span) if fits else None,
            (resid_ref, k, n % per * span) if resids else None,
        )
        if fits:
            give(n, 0).start()
            give(n, 1).start()
        return carry

    lax.fori_loop(0, count, body, 0)
    if resids:
        for kk in range(GROUPS):
            outs[kk][...] = resid_ref[kk]
    if fits:
        for n in range(count):
            give(n, 0).wait()
            give(n, 1).wait()


def fit_steps(plan, first, last, signal, taps, fits, resids, halos):
    base, span, count = plan
    rows, width = signal.shape
    ends = halos is not None
    margins = 4 if ends and base else 2
    if not fits:
        taps = taps[:, :LANES]
    hbm = pl.BlockSpec(memory_space=pltpu.HBM)
    vmem = pl.BlockSpec(memory_space=pltpu.VMEM)
    loose = pl.BlockSpec(memory_space=pl.ANY)
    args = [pltpu.with_memory_space_constraint(a, pltpu.HBM) for a in (first, last, signal, taps)]
    args += list(halos or ())
    wide = jax.ShapeDtypeStruct((rows, width), jnp.float32)
    part = jax.ShapeDtypeStruct((rows, count // GROUPS * span), jnp.float32)
    scratch = [
        pltpu.VMEM((rows, count * span + margins * LANES), jnp.float32),
        pltpu.VMEM(taps.shape, taps.dtype),
        pltpu.SMEM(first.shape, jnp.int32),
        pltpu.SMEM(last.shape, jnp.int32),
        pltpu.SemaphoreType.DMA((count,)),
        pltpu.SemaphoreType.DMA((7,)),
    ]
    if fits:
        scratch += [
            pltpu.VMEM((2, rows, count * span), jnp.float32),
            pltpu.SemaphoreType.DMA((2, count)),
        ]
    if resids:
        scratch += [pltpu.VMEM((GROUPS, rows, count // GROUPS * span), jnp.float32)]
    return pl.pallas_call(
        functools.partial(fit_kernel, plan, fits, resids, ends),
        in_specs=[hbm] * 4 + [loose] * len(halos or ()),
        out_specs=[hbm] * (2 * fits) + [vmem] * (GROUPS * resids),
        out_shape=[wide] * (2 * fits) + [part] * (GROUPS * resids),
        scratch_shapes=scratch,
        compiler_params=pltpu.CompilerParams(vmem_limit_bytes=16 * MIB),
        cost_estimate=pl.CostEstimate(
            flops=count * 3 * rows * span * 256 * 4,
            bytes_accessed=count * rows * span * 4 * 4,
            transcendentals=0,
        ),
    )(*args)


def stacked(stack_ref, group, x):
    at = pl.multiple_of(group * ROWS, ROWS)
    a = x.astype(jnp.bfloat16)
    stack_ref[pl.ds(at, ROWS)] = a
    stack_ref[pl.ds(64 + at, ROWS)] = (x - a.astype(jnp.float32)).astype(jnp.bfloat16)


def product(stack_ref, so_far_ref, spread, out_ref):
    both = lax.dot_general(
        stack_ref[...],
        stack_ref[...],
        (((1,), (1,)), ((), ())),
        preferred_element_type=jnp.float32,
    )
    gram = both[:64] + both[64:]
    gram = gram + pltpu.roll(gram, 64, 1)
    low = lax.broadcasted_iota(jnp.int32, (8, LANES), 1) < 64
    for g in range(GROUPS):
        rows = jnp.where(low, gram[16 * g : 16 * g + 8], gram[16 * g + 8 : 16 * g + 16])
        if so_far_ref is not None:
            rows = rows + so_far_ref[g]
        if spread:
            for n in range(spread):
                out_ref[n, g] = rows
        else:
            out_ref[g] = rows


def raw_gram_kernel(plan, width, first_hbm, last_hbm, taps_hbm, *refs):
    base, span, _ = plan
    pieces, refs = refs[:GROUPS], refs[GROUPS:]
    out_ref, x_ref, resid_ref, stack_ref, taps_ref, first_ref, last_ref, sems = refs
    mine = lax.axis_index("series")
    mark = lax.axis_index(TIME) * width + base + mine * span
    copies = [
        pltpu.make_async_copy(a, b, sems.at[n])
        for n, (a, b) in enumerate(
            ((first_hbm, first_ref), (last_hbm, last_ref), (taps_hbm, taps_ref))
        )
    ]
    for copy in copies:
        copy.start()
    for k in range(GROUPS):
        x_ref[k, :, :LANES] = pieces[k][:, span:]
        x_ref[k, :, LANES:] = pieces[k][...]
    for copy in copies:
        copy.wait()

    def body(k, carry):
        group = (mine + GROUPS - k) % GROUPS
        first, last = ends_of(group, first_ref, last_ref)
        fit_span(
            span,
            mark,
            group,
            (x_ref.at[k], LANES),
            (taps_ref, first_ref, last_ref, first, last),
            None,
            (resid_ref, 0, 0),
        )
        stacked(stack_ref, group, resid_ref[0])
        return carry

    lax.fori_loop(0, GROUPS, body, 0)
    product(stack_ref, None, None, out_ref)


def raw_gram_of(plan, width, first, last, taps, pieces):
    _, span, _ = plan
    taps = taps[:, :LANES]
    hbm = pl.BlockSpec(memory_space=pltpu.HBM)
    vmem = pl.BlockSpec(memory_space=pltpu.VMEM)
    args = [pltpu.with_memory_space_constraint(a, pltpu.HBM) for a in (first, last, taps)]
    return pl.pallas_call(
        functools.partial(raw_gram_kernel, plan, width),
        in_specs=[hbm] * 3 + [vmem] * GROUPS,
        out_specs=vmem,
        out_shape=jax.ShapeDtypeStruct((GROUPS, 8, LANES), jnp.float32),
        scratch_shapes=[
            pltpu.VMEM((GROUPS, ROWS, span + 2 * LANES), jnp.float32),
            pltpu.VMEM((1, ROWS, span), jnp.float32),
            pltpu.VMEM((128, span), jnp.bfloat16),
            pltpu.VMEM(taps.shape, taps.dtype),
            pltpu.SMEM(first.shape, jnp.int32),
            pltpu.SMEM(last.shape, jnp.int32),
            pltpu.SemaphoreType.DMA((3,)),
        ],
        compiler_params=pltpu.CompilerParams(vmem_limit_bytes=16 * MIB),
        cost_estimate=pl.CostEstimate(
            flops=GROUPS * 3 * ROWS * span * 256 * 4,
            bytes_accessed=GROUPS * ROWS * span * 8,
            transcendentals=0,
        ),
    )(*args, *pieces)


def gram_kernel(add, spread, *refs):
    parts, refs = refs[:GROUPS], refs[GROUPS:]
    if add:
        so_far_ref, refs = refs[0], refs[1:]
    out_ref, stack_ref = refs
    mine = lax.axis_index("series")
    for k in range(GROUPS):
        stacked(stack_ref, (mine + GROUPS - k) % GROUPS, parts[k][...])
    product(stack_ref, so_far_ref if add else None, spread, out_ref)


def gram_of(parts, so_far, spread):
    width = parts[0].shape[1]
    vmem = pl.BlockSpec(memory_space=pltpu.VMEM)
    args = list(parts) + ([] if so_far is None else [so_far])
    lead = (spread,) if spread else ()
    return pl.pallas_call(
        functools.partial(gram_kernel, so_far is not None, spread),
        in_specs=[vmem] * len(args),
        out_specs=vmem,
        out_shape=jax.ShapeDtypeStruct((*lead, GROUPS, 8, LANES), jnp.float32),
        scratch_shapes=[pltpu.VMEM((128, width), jnp.bfloat16)],
        compiler_params=pltpu.CompilerParams(vmem_limit_bytes=12 * MIB),
        cost_estimate=pl.CostEstimate(
            flops=128 * 128 * width * 2, bytes_accessed=64 * width * 4, transcendentals=0
        ),
    )(*args)


def exchanged(pieces):
    parts = [pieces[0]]
    for k in (2, 1, 3):
        pairs = [(s, (s + k) % GROUPS) for s in range(GROUPS)]
        parts.append(lax.ppermute(pieces[k], "series", pairs))
    return [parts[0], parts[2], parts[1], parts[3]]


def shards(taps, signal, valid_start, valid_end):
    rows, width = signal.shape
    devices = lax.axis_size(TIME)
    taps = jnp.asarray(taps, jnp.bfloat16)
    mine = lax.axis_index("series")
    unit = width // 32
    early, mid = (unit, 4 * unit, GROUPS), (17 * unit, unit * 7 // 2, GROUPS)
    late, whole = (31 * unit, unit // 2, GROUPS), (0, 8 * unit, 4)

    def fit(plan, fits, resids, halos=None):
        return fit_steps(plan, valid_start, valid_end, signal, taps, fits, resids, halos)

    first = lax.dynamic_slice_in_dim(valid_start, mine * rows, rows)[:, None]
    last = lax.dynamic_slice_in_dim(valid_end, mine * rows, rows)[:, None]
    shared = jnp.minimum(last, valid_end[None, :])
    shared = shared - jnp.maximum(first, valid_start[None, :])
    shared = shared.astype(jnp.float32)

    *pieces, near, far = cut_chunk(early, signal)
    parts = exchanged(pieces)
    parts_mid = exchanged(fit(mid, False, True))
    near = lax.ppermute(near, TIME, [(t, t ^ 1) for t in range(devices)])
    pairs = [(t, t + 1) for t in range(1, devices - 1, 2)]
    far = lax.ppermute(far, TIME, pairs + [(b, a) for a, b in pairs])
    halos = (near, far)
    gram = raw_gram_of(early, width, valid_start, valid_end, taps, parts)
    parts = exchanged(fit(late, False, True, halos))
    gram = gram_of(parts_mid, gram, None)
    copies = gram_of(parts, gram, devices // 2)
    copies = copies.reshape(devices * GROUPS, 4, LANES)
    copies = lax.all_to_all(copies, (*TIME[:2], "series", "core"), 0, 0, tiled=True)
    smooth, slope = fit(whole, True, False, halos)
    own = jnp.sum(copies, axis=0)
    other = lax.ppermute(own, "core", [(0, 1), (1, 0)])
    lead = lax.axis_index("core") == 0
    p, q = jnp.where(lead, own, other), jnp.where(lead, other, own)
    gram = jnp.concatenate([p[:, :64], q[:, :64], p[:, 64:], q[:, 64:]], axis=0)
    return smooth, slope, gram / shared


def solution(mesh):
    split = Mesh(mesh.devices.reshape(4, 4, 2, GROUPS), (*TIME, "series"))
    return jax.shard_map(
        functools.partial(shards, filter_matrix()),
        mesh=split,
        in_specs=(P("series", TIME), P(), P()),
        out_specs=(P("series", TIME), P("series", TIME), P("series", None)),
        check_vma=False,
    )
```

```python
import functools

import jax
import jax.numpy as jnp
import numpy as np
from jax import lax
from jax.experimental import pallas as pl
from jax.experimental.pallas import tpu as pltpu
from jax.sharding import Mesh
from jax.sharding import PartitionSpec as P


HALF = 16
TAPS = 2 * HALF + 1
ROWS = 16
GROUPS = 4
LANES = 128
TIME = ("y", "z", "core")
MIB = 1 << 20

SECOND = float(sum(j * j for j in range(-HALF, HALF + 1)))
CENTRE_SQ = SECOND / TAPS
FOURTH = float(sum((j * j - CENTRE_SQ) ** 2 for j in range(-HALF, HALF + 1)))
SMOOTH_SCALE = 2048.0 / 2387.0
SLOPE_SCALE = HALF * 16.0 / SECOND


def filter_matrix():
    place = np.concatenate([np.arange(128), np.arange(128, 192), np.arange(-64, 0)])
    j = place[:, None] - np.arange(LANES)[None, :]
    near = np.abs(j) <= HALF
    smooth = np.where(near, (163 - j * j) / 2048.0, 0.0)
    slope = np.where(near, j / 16.0, 0.0)
    return np.concatenate([smooth, slope], axis=1).astype(np.float32)


def thirds(x):
    a = x.astype(jnp.bfloat16)
    rest = x - a.astype(jnp.float32)
    b = rest.astype(jnp.bfloat16)
    c = (rest - b.astype(jnp.float32)).astype(jnp.bfloat16)
    return a, b, c


def aligned(start, size):
    return pl.ds(pl.multiple_of(start, LANES), size)


def ends_of(group, first_ref, last_ref):
    row = lax.broadcasted_iota(jnp.int32, (ROWS, LANES), 0)
    first = jnp.zeros((ROWS, LANES), jnp.int32)
    last = jnp.zeros((ROWS, LANES), jnp.int32)
    for r in range(ROWS):
        first = jnp.where(row == r, first_ref[group * ROWS + r], first)
        last = jnp.where(row == r, last_ref[group * ROWS + r], last)
    return first, last


def fit_span(span, mark, group, samples, tables, to_fit, to_resid):
    blocks = span // LANES
    height = ROWS * blocks
    x_ref, at = samples
    taps_ref, first_ref, last_ref, first, last = tables
    if to_fit:
        fit_ref, out_at = to_fit
    if to_resid:
        resid_ref, k, piece_at = to_resid
    lane = lax.broadcasted_iota(jnp.int32, (ROWS, LANES), 1)
    row = lax.broadcasted_iota(jnp.int32, (ROWS, LANES), 0)
    low = lane < 64

    x = x_ref[:, aligned(at - LANES, span + 2 * LANES)]
    parts = thirds(x)

    def cut(m, b):
        return parts[m][:, b * LANES : (b + 1) * LANES]

    rows = [
        jnp.concatenate([cut(m, b + 1), jnp.where(low, cut(m, b + 2), cut(m, b))], axis=1)
        for m in range(3)
        for b in range(blocks)
    ]
    fit = jnp.dot(
        jnp.concatenate(rows, axis=0), taps_ref[...], preferred_element_type=jnp.float32
    )
    fit = fit[:height] + (fit[height : 2 * height] + fit[2 * height :])
    since = first - mark
    until = last - mark
    for b in range(blocks):
        part = fit[b * ROWS : (b + 1) * ROWS]
        moment = lane + b * LANES
        inside = (moment >= since) & (moment < until)
        smooth = part[:, :LANES] * SMOOTH_SCALE
        if to_fit:
            to = aligned(out_at + b * LANES, LANES)
            fit_ref[0, :, to] = jnp.where(inside, smooth, 0.0)
            fit_ref[1, :, to] = jnp.where(inside, part[:, LANES:] * SLOPE_SCALE, 0.0)
        if to_resid:
            resid = x[:, (b + 1) * LANES : (b + 2) * LANES] - smooth
            resid_ref[k, :, aligned(piece_at + b * LANES, LANES)] = jnp.where(inside, resid, 0.0)

    def starts_here(a):
        return (a > mark - HALF) & (a < mark + span)

    def stops_here(z):
        return (z > mark) & (z < mark + span + HALF)

    holds = False
    for r in range(ROWS):
        holds = holds | starts_here(first_ref[group * ROWS + r])
        holds = holds | stops_here(last_ref[group * ROWS + r])

    @pl.when(holds)
    def _():
        def mend(r, left, centre, side):
            b = (left + LANES) // LANES - 1
            v = x_ref[:, aligned(at + b * LANES, 2 * LANES)]
            j = lax.broadcasted_iota(jnp.int32, (ROWS, 2 * LANES), 1) + (b * LANES - centre)
            w = jnp.where((j >= -HALF) & (j <= HALF), v, 0.0)
            f = jnp.clip(j, -HALF, HALF).astype(jnp.float32)
            level = jnp.sum(w, axis=1, keepdims=True) * (1.0 / TAPS)
            tilt = jnp.sum(w * f, axis=1, keepdims=True) * (1.0 / SECOND)
            curve = f * f - CENTRE_SQ
            bend = jnp.sum(w * curve, axis=1, keepdims=True) * (1.0 / FOURTH)
            smooth = level + tilt * f + bend * curve
            slope = HALF * (tilt + 2.0 * f * bend)
            held = (j * side >= 1) & (j * side <= HALF)
            for h in range(2):

                @pl.when((b + h >= 0) & (b + h < blocks))
                def _():
                    part = slice(h * LANES, (h + 1) * LANES)
                    to = held[:, part] & (row == r)
                    if to_fit:
                        at_fit = aligned(out_at + (b + h) * LANES, LANES)
                        fit_ref[0, :, at_fit] = jnp.where(
                            to, smooth[:, part], fit_ref[0, :, at_fit]
                        )
                        fit_ref[1, :, at_fit] = jnp.where(to, slope[:, part], fit_ref[1, :, at_fit])
                    if to_resid:
                        at_piece = aligned(piece_at + (b + h) * LANES, LANES)
                        resid_ref[k, :, at_piece] = jnp.where(
                            to, v[:, part] - smooth[:, part], resid_ref[k, :, at_piece]
                        )

        def series(r, carry):
            a = first_ref[group * ROWS + r]
            z = last_ref[group * ROWS + r]

            @pl.when(starts_here(a))
            def _():
                mend(r, a - mark, a - mark + HALF, -1)

            @pl.when(stops_here(z))
            def _():
                mend(r, z - mark - TAPS, z - mark - HALF - 1, 1)

            return carry

        def bunch(q, carry):
            some = False
            for r in range(4):
                some = some | starts_here(first_ref[group * ROWS + 4 * q + r])
                some = some | stops_here(last_ref[group * ROWS + 4 * q + r])

            @pl.when(some)
            def _():
                lax.fori_loop(4 * q, 4 * q + 4, series, 0)

            return carry

        lax.fori_loop(0, ROWS // 4, bunch, 0)


def cut_kernel(plan, signal_ref, *refs):
    base, span, _ = plan
    pieces, edges, (side_ref, sems) = refs[:GROUPS], refs[GROUPS : GROUPS + 2], refs[-2:]
    width = signal_ref.shape[1]
    mine = lax.axis_index("series")
    core = lax.axis_index("core")
    copies = []

    def move(start, size, to):
        copy = pltpu.make_async_copy(
            signal_ref.at[:, aligned(start, size)], to, sems.at[len(copies)]
        )
        copy.start()
        copies.append(copy)

    for k in (2, 1, 3, 0):
        start = base + (mine ^ k) * span
        move(start - LANES, LANES, side_ref.at[2 * k])
        move(start + span, LANES, side_ref.at[2 * k + 1])
        move(start, span, pieces[k].at[:, pl.ds(0, span)])
    move((1 - core) * (width - LANES), LANES, edges[0])
    move(core * (width - LANES), LANES, edges[1])
    for copy in copies:
        copy.wait()
    low = lax.broadcasted_iota(jnp.int32, edges[0].shape, 1) < 64
    for k in range(GROUPS):
        pieces[k][:, span:] = jnp.where(low, side_ref[2 * k + 1], side_ref[2 * k])


def cut_chunk(plan, signal):
    rows, _ = signal.shape
    part = jax.ShapeDtypeStruct((rows, plan[1] + LANES), jnp.float32)
    edge = jax.ShapeDtypeStruct((rows, LANES), jnp.float32)
    return pl.pallas_call(
        functools.partial(cut_kernel, plan),
        in_specs=[pl.BlockSpec(memory_space=pltpu.HBM)],
        out_specs=[pl.BlockSpec(memory_space=pltpu.VMEM)] * (GROUPS + 2),
        out_shape=[part] * GROUPS + [edge] * 2,
        scratch_shapes=[
            pltpu.VMEM((2 * GROUPS, rows, LANES), jnp.float32),
            pltpu.SemaphoreType.DMA((3 * GROUPS + 2,)),
        ],
        compiler_params=pltpu.CompilerParams(vmem_limit_bytes=8 * MIB),
        cost_estimate=pl.CostEstimate(
            flops=0, bytes_accessed=rows * plan[1] * 32, transcendentals=0
        ),
        name="cut_early",
    )(pltpu.with_memory_space_constraint(signal, pltpu.HBM))


def fit_kernel(plan, fits, resids, ends, *refs):
    base, span, count = plan
    refs = list(refs)
    whole = ends and base == 0
    first_hbm, last_hbm, signal_ref, taps_hbm = refs[:4]
    refs = refs[4:]
    if ends:
        halo_refs, refs = refs[:2], refs[2:]
    if fits:
        fit_hbm, refs = refs[:2], refs[2:]
    if resids:
        outs, refs = refs[:GROUPS], refs[GROUPS:]
    x_ref, taps_ref, first_ref, last_ref, in_sems, side_sems = refs[:6]
    refs = refs[6:]
    if fits:
        fit_ref, out_sems = refs[:2]
        refs = refs[2:]
    if resids:
        resid_ref = refs[0]

    width = signal_ref.shape[1]
    per = count // GROUPS
    half = count // 2
    mine = lax.axis_index("series")
    begin = lax.axis_index(TIME) * width
    core = lax.axis_index("core")

    def place(n):
        return LANES + n * span + (2 * LANES * (n // half) if ends and not whole else 0)

    def source(n):
        return lax.rem(base + n * span, width) if ends and not whole else base + n * span

    def fetch(n):
        return pltpu.make_async_copy(
            signal_ref.at[:, aligned(source(n), span)],
            x_ref.at[:, aligned(place(n), span)],
            in_sems.at[n],
        )

    middle = place(half)
    tail = place(count - 1) + span
    after = (base + count * span) % width
    sides = [(first_hbm, first_ref), (last_hbm, last_ref), (taps_hbm, taps_ref)]
    if not whole:
        sides += [
            (signal_ref.at[:, pl.ds(base - LANES, LANES)], x_ref.at[:, pl.ds(0, LANES)]),
            (signal_ref.at[:, pl.ds(after, LANES)], x_ref.at[:, pl.ds(tail, LANES)]),
        ]
    if ends:
        at_left, at_right = (0, tail) if whole else (middle - LANES, middle - 2 * LANES)
        across = core * (at_left - at_right)
        sides += [
            (halo_refs[0], x_ref.at[:, aligned(at_right + across, LANES)]),
            (halo_refs[1], x_ref.at[:, aligned(at_left - across, LANES)]),
        ]
    sides = [pltpu.make_async_copy(a, b, side_sems.at[n]) for n, (a, b) in enumerate(sides)]
    for copy in sides:
        copy.start()
    for n in range(count):
        fetch(n).start()

    def give(n, kind):
        return pltpu.make_async_copy(
            fit_ref.at[kind, :, aligned(n * span, span)],
            fit_hbm[kind].at[:, aligned(source(n), span)],
            out_sems.at[kind, n],
        )

    for copy in sides:
        copy.wait()
    fetch(0).wait()

    first, last = ends_of(mine, first_ref, last_ref)

    def body(n, carry):
        k = (n // per) ^ mine

        @pl.when(n + 1 < count)
        def _():
            fetch(n + 1).wait()

        fit_span(
            span,
            begin + source(n),
            mine,
            (x_ref, place(n)),
            (taps_ref, first_ref, last_ref, first, last),
            (fit_ref, n * span) if fits else None,
            (resid_ref, k, n % per * span) if resids else None,
        )
        if fits:
            give(n, 0).start()
            give(n, 1).start()
        return carry

    lax.fori_loop(0, count, body, 0)
    if resids:
        for kk in range(GROUPS):
            outs[kk][...] = resid_ref[kk]
    if fits:
        for n in range(count):
            give(n, 0).wait()
            give(n, 1).wait()


def fit_steps(plan, first, last, signal, taps, fits, resids, halos):
    base, span, count = plan
    rows, width = signal.shape
    ends = halos is not None
    margins = 4 if ends and base else 2
    if not fits:
        taps = taps[:, :LANES]
    hbm = pl.BlockSpec(memory_space=pltpu.HBM)
    vmem = pl.BlockSpec(memory_space=pltpu.VMEM)
    loose = pl.BlockSpec(memory_space=pl.ANY)
    args = [pltpu.with_memory_space_constraint(a, pltpu.HBM) for a in (first, last, signal, taps)]
    args += list(halos or ())
    wide = jax.ShapeDtypeStruct((rows, width), jnp.float32)
    part = jax.ShapeDtypeStruct((rows, count // GROUPS * span), jnp.float32)
    scratch = [
        pltpu.VMEM((rows, count * span + margins * LANES), jnp.float32),
        pltpu.VMEM(taps.shape, taps.dtype),
        pltpu.SMEM(first.shape, jnp.int32),
        pltpu.SMEM(last.shape, jnp.int32),
        pltpu.SemaphoreType.DMA((count,)),
        pltpu.SemaphoreType.DMA((7,)),
    ]
    if fits:
        scratch += [
            pltpu.VMEM((2, rows, count * span), jnp.float32),
            pltpu.SemaphoreType.DMA((2, count)),
        ]
    if resids:
        scratch += [pltpu.VMEM((GROUPS, rows, count // GROUPS * span), jnp.float32)]
    return pl.pallas_call(
        functools.partial(fit_kernel, plan, fits, resids, ends),
        in_specs=[hbm] * 4 + [loose] * len(halos or ()),
        out_specs=[hbm] * (2 * fits) + [vmem] * (GROUPS * resids),
        out_shape=[wide] * (2 * fits) + [part] * (GROUPS * resids),
        scratch_shapes=scratch,
        compiler_params=pltpu.CompilerParams(vmem_limit_bytes=16 * MIB),
        cost_estimate=pl.CostEstimate(
            flops=count * 3 * rows * span * 256 * 4,
            bytes_accessed=count * rows * span * 4 * 4,
            transcendentals=0,
        ),
    )(*args)


def stacked(stack_ref, group, x):
    at = pl.multiple_of(group * ROWS, ROWS)
    a = x.astype(jnp.bfloat16)
    stack_ref[pl.ds(at, ROWS)] = a
    stack_ref[pl.ds(64 + at, ROWS)] = (x - a.astype(jnp.float32)).astype(jnp.bfloat16)


def product(stack_ref, so_far_ref, spread, out_ref):
    both = lax.dot_general(
        stack_ref[...],
        stack_ref[...],
        (((1,), (1,)), ((), ())),
        preferred_element_type=jnp.float32,
    )
    gram = both[:64] + both[64:]
    gram = gram + pltpu.roll(gram, 64, 1)
    low = lax.broadcasted_iota(jnp.int32, (8, LANES), 1) < 64
    for g in range(GROUPS):
        rows = jnp.where(low, gram[16 * g : 16 * g + 8], gram[16 * g + 8 : 16 * g + 16])
        if so_far_ref is not None:
            rows = rows + so_far_ref[g]
        if spread:
            for n in range(spread):
                out_ref[n, g] = rows
        else:
            out_ref[g] = rows


def raw_gram_kernel(plan, width, first_hbm, last_hbm, taps_hbm, *refs):
    base, span, _ = plan
    pieces, refs = refs[:GROUPS], refs[GROUPS:]
    out_ref, x_ref, resid_ref, stack_ref, taps_ref, first_ref, last_ref, sems = refs
    mine = lax.axis_index("series")
    mark = lax.axis_index(TIME) * width + base + mine * span
    copies = [
        pltpu.make_async_copy(a, b, sems.at[n])
        for n, (a, b) in enumerate(
            ((first_hbm, first_ref), (last_hbm, last_ref), (taps_hbm, taps_ref))
        )
    ]
    for copy in copies:
        copy.start()
    for k in range(GROUPS):
        x_ref[k, :, :LANES] = pieces[k][:, span:]
        x_ref[k, :, LANES:] = pieces[k][...]
    for copy in copies:
        copy.wait()

    def body(k, carry):
        group = mine ^ k
        first, last = ends_of(group, first_ref, last_ref)
        fit_span(
            span,
            mark,
            group,
            (x_ref.at[k], LANES),
            (taps_ref, first_ref, last_ref, first, last),
            None,
            (resid_ref, 0, 0),
        )
        stacked(stack_ref, group, resid_ref[0])
        return carry

    lax.fori_loop(0, GROUPS, body, 0)
    product(stack_ref, None, None, out_ref)


def raw_gram_of(plan, width, first, last, taps, pieces):
    _, span, _ = plan
    taps = taps[:, :LANES]
    hbm = pl.BlockSpec(memory_space=pltpu.HBM)
    vmem = pl.BlockSpec(memory_space=pltpu.VMEM)
    args = [pltpu.with_memory_space_constraint(a, pltpu.HBM) for a in (first, last, taps)]
    return pl.pallas_call(
        functools.partial(raw_gram_kernel, plan, width),
        in_specs=[hbm] * 3 + [vmem] * GROUPS,
        out_specs=vmem,
        out_shape=jax.ShapeDtypeStruct((GROUPS, 8, LANES), jnp.float32),
        scratch_shapes=[
            pltpu.VMEM((GROUPS, ROWS, span + 2 * LANES), jnp.float32),
            pltpu.VMEM((1, ROWS, span), jnp.float32),
            pltpu.VMEM((128, span), jnp.bfloat16),
            pltpu.VMEM(taps.shape, taps.dtype),
            pltpu.SMEM(first.shape, jnp.int32),
            pltpu.SMEM(last.shape, jnp.int32),
            pltpu.SemaphoreType.DMA((3,)),
        ],
        compiler_params=pltpu.CompilerParams(vmem_limit_bytes=16 * MIB),
        cost_estimate=pl.CostEstimate(
            flops=GROUPS * 3 * ROWS * span * 256 * 4,
            bytes_accessed=GROUPS * ROWS * span * 8,
            transcendentals=0,
        ),
    )(*args, *pieces)


def gram_kernel(add, spread, *refs):
    parts, refs = refs[:GROUPS], refs[GROUPS:]
    if add:
        so_far_ref, refs = refs[0], refs[1:]
    out_ref, stack_ref = refs
    mine = lax.axis_index("series")
    for k in range(GROUPS):
        stacked(stack_ref, mine ^ k, parts[k][...])
    product(stack_ref, so_far_ref if add else None, spread, out_ref)


def gram_of(parts, so_far, spread):
    width = parts[0].shape[1]
    vmem = pl.BlockSpec(memory_space=pltpu.VMEM)
    args = list(parts) + ([] if so_far is None else [so_far])
    lead = (spread,) if spread else ()
    return pl.pallas_call(
        functools.partial(gram_kernel, so_far is not None, spread),
        in_specs=[vmem] * len(args),
        out_specs=vmem,
        out_shape=jax.ShapeDtypeStruct((*lead, GROUPS, 8, LANES), jnp.float32),
        scratch_shapes=[pltpu.VMEM((128, width), jnp.bfloat16)],
        compiler_params=pltpu.CompilerParams(vmem_limit_bytes=12 * MIB),
        cost_estimate=pl.CostEstimate(
            flops=128 * 128 * width * 2, bytes_accessed=64 * width * 4, transcendentals=0
        ),
    )(*args)


def exchanged(pieces):
    parts = [pieces[0]]
    for k in (2, 1, 3):
        pairs = [(s, s ^ k) for s in range(GROUPS)]
        parts.append(lax.ppermute(pieces[k], "series", pairs))
    return [parts[0], parts[2], parts[1], parts[3]]


def shards(taps, signal, valid_start, valid_end):
    rows, width = signal.shape
    devices = lax.axis_size(TIME)
    taps = jnp.asarray(taps, jnp.bfloat16)
    mine = lax.axis_index("series")
    unit = width // 32
    early, mid = (2 * unit, 4 * unit, GROUPS), (18 * unit, 3 * unit, GROUPS)
    late, whole = (30 * unit, unit, GROUPS), (0, 8 * unit, 4)

    def fit(plan, fits, resids, halos=None):
        return fit_steps(plan, valid_start, valid_end, signal, taps, fits, resids, halos)

    first = lax.dynamic_slice_in_dim(valid_start, mine * rows, rows)[:, None]
    last = lax.dynamic_slice_in_dim(valid_end, mine * rows, rows)[:, None]
    shared = jnp.minimum(last, valid_end[None, :])
    shared = shared - jnp.maximum(first, valid_start[None, :])
    shared = shared.astype(jnp.float32)

    *pieces, near, far = cut_chunk(early, signal)
    parts = exchanged(pieces)
    parts_mid = exchanged(fit(mid, False, True))
    near = lax.ppermute(near, TIME, [(t, t ^ 1) for t in range(devices)])
    pairs = [(t, t + 1) for t in range(1, devices - 1, 2)]
    far = lax.ppermute(far, TIME, pairs + [(b, a) for a, b in pairs])
    halos = (near, far)
    gram = raw_gram_of(early, width, valid_start, valid_end, taps, parts)
    parts = exchanged(fit(late, False, True, halos))
    gram = gram_of(parts_mid, gram, None)
    copies = gram_of(parts, gram, devices // 2)
    copies = copies.reshape(devices * GROUPS, 4, LANES)
    copies = lax.all_to_all(copies, (*TIME[:2], "series", "core"), 0, 0, tiled=True)
    smooth, slope = fit(whole, True, False, halos)
    own = jnp.sum(copies, axis=0)
    other = lax.ppermute(own, "core", [(0, 1), (1, 0)])
    lead = lax.axis_index("core") == 0
    p, q = jnp.where(lead, own, other), jnp.where(lead, other, own)
    gram = jnp.concatenate([p[:, :64], q[:, :64], p[:, 64:], q[:, 64:]], axis=0)
    return smooth, slope, gram / shared


def solution(mesh):
    split = Mesh(mesh.devices.reshape(4, 4, 2, GROUPS), (*TIME, "series"))
    return jax.shard_map(
        functools.partial(shards, filter_matrix()),
        mesh=split,
        in_specs=(P("series", TIME), P(), P()),
        out_specs=(P("series", TIME), P("series", TIME), P("series", None)),
        check_vma=False,
    )
```
